32 devices in a mesh: grid: 8 (over z, x), chan: 4 (over y, core).
Axes of the slice: x: 2, y: 2, z: 4, core: 2. Of those that a mesh axis runs over, the one named last changes fastest.
Arguments:
- input_field: bfloat16 [256, 1024, 1024], P('chan', 'grid'), may hold values from -6 to 6
- out_cotangent: bfloat16 [256, 1024, 1024], P('chan', 'grid'), may hold values from -6 to 6
- core_first: float32 [256, 16], replicated, may hold values from -1.5 to 1.5
- core_second: float32 [16, 256, 16], replicated, may hold values from -1.5 to 1.5
- core_third: float32 [16, 128, 16], replicated, may hold values from -1.5 to 1.5
- column_mode_core: float32 [2, 16, 128], replicated, may hold values from -2 to 2
Outputs:
- output_field: bfloat16 [256, 1024, 1024], P('chan', 'grid')
- input_grad: bfloat16 [256, 1024, 1024], P('chan', 'grid')
- grad_first: float32 [256, 16], replicated
- grad_second: float32 [16, 256, 16], replicated
- grad_third: float32 [16, 128, 16], replicated
- grad_fourth: float32 [2, 16, 128], replicated
The draws below stay inside these ranges and needn't reach their ends.
All inputs are finite; a program needn't handle non-finite values.
Results may differ from the reference program's by a relative error of at most 0.0079.
Values may be sent and summed in bfloat16 or wider, within the bound.
A program may use at most 128 MiB of HBM per device.

```python
import math
import jax
import jax.numpy as jnp
from jax import lax

CHANNELS = 256
GRID_SIDE = 1024
MODES_X = 128
MODES_Y = 128
RANK_ONE = 16
RANK_TWO = 16
RANK_THREE = 16


def block_scale(key, shape, split, smallest, top_value):
    factor_of, own = 1.0, jax.random.fold_in(key, 6)
    for position, shards_of in split:
        draws = jnp.exp(jax.random.uniform(jax.random.fold_in(own, position), (shards_of,), jnp.float32, smallest / len(split), top_value / len(split)))
        factor_of = factor_of * jnp.repeat(draws, shape[position] // shards_of).reshape([-1 if axis == position else 1 for axis in range(len(shape))])
    return factor_of


def centred(stream_key, shape, spread, most, split=(), kind=jnp.bfloat16):
    values = spread * jax.random.normal(stream_key, shape, jnp.float32)
    if split:
        values = values * block_scale(stream_key, shape, split, -0.22, 0.18)
    return jnp.clip(values, -most, most).astype(kind)


def setup_inputs(seed: int = 0) -> dict:
    keys = jax.random.split(jax.random.key(seed), 7)
    return {
        "input_field": centred(keys[0], (CHANNELS, GRID_SIDE, GRID_SIDE), 1.0, 6.0, ((0, 4), (1, 8))),
        "out_cotangent": centred(keys[1], (CHANNELS, GRID_SIDE, GRID_SIDE), 1.0, 6.0, ((0, 4), (1, 8))),
        "core_first": centred(keys[2], (CHANNELS, RANK_ONE), 0.25, 1.5, (), jnp.float32),
        "core_second": centred(keys[3], (RANK_ONE, CHANNELS, RANK_TWO), 0.25, 1.5, (), jnp.float32),
        "core_third": centred(keys[4], (RANK_TWO, MODES_X, RANK_THREE), 0.25, 1.5, (), jnp.float32),
        "column_mode_core": centred(keys[5], (2, RANK_THREE, MODES_Y), 0.35, 2.0, (), jnp.float32),
    }


full_turn = 2.0 * math.pi

def turn_tables(mode_index, row_index):
    freq = jnp.where(mode_index < MODES_X // 2, mode_index, GRID_SIDE - MODES_X + mode_index).astype(jnp.int32)
    phase = freq[:, None] * row_index[None, :] % GRID_SIDE
    angle = phase.astype(jnp.float32) * (full_turn / GRID_SIDE)
    cosine = jnp.cos(angle).astype(jnp.bfloat16)
    sine = jnp.sin(angle).astype(jnp.bfloat16)
    real_rows = jnp.stack([cosine, sine], axis=-1)
    imag_rows = jnp.stack([-sine, cosine], axis=-1)
    return jnp.stack([real_rows, imag_rows], axis=1)

def width_table():
    column = jnp.arange(GRID_SIDE, dtype=jnp.int32)
    wave = jnp.arange(MODES_Y, dtype=jnp.int32)
    phase = column[:, None] * wave[None, :] % GRID_SIDE
    angle = phase.astype(jnp.float32) * (full_turn / GRID_SIDE)
    cosine = jnp.cos(angle).astype(jnp.bfloat16)
    sine = jnp.sin(angle).astype(jnp.bfloat16)
    return jnp.stack([cosine, -sine], axis=1)

def mix_block(spec_block, third_core_block, core_first, core_second, column_mode_core):
    lead = jnp.einsum('ia,kiqy->kaqy', core_first, spec_block, precision=lax.Precision.HIGHEST)
    spectral_kernel = jnp.einsum('esz,pzm->sepm', third_core_block, column_mode_core, precision=lax.Precision.HIGHEST)
    inner = jnp.einsum('aob,kaqy->kobqy', core_second, lead, precision=lax.Precision.HIGHEST)
    kernel_re = spectral_kernel[:, None, :, 0, :]
    kernel_im = spectral_kernel[:, None, :, 1, :]
    inner_re = inner[:, :, :, 0, :]
    inner_im = inner[:, :, :, 1, :]
    out_re = lax.optimization_barrier(jnp.sum(inner_re * kernel_re - inner_im * kernel_im, axis=2))
    out_im = lax.optimization_barrier(jnp.sum(inner_re * kernel_im + inner_im * kernel_re, axis=2))
    return jnp.stack([out_re, out_im], axis=2)

def mix(spec_in, core_first, core_second, core_third, column_mode_core):
    blocks = spec_in.reshape(MODES_X // 8, 8, CHANNELS, 2, MODES_Y)
    third_blocks = core_third.reshape(RANK_TWO, MODES_X // 8, 8, RANK_THREE).transpose(1, 0, 2, 3)

    def one_block(pair):
        return mix_block(pair[0], pair[1], core_first, core_second, column_mode_core)
    result = lax.map(one_block, (blocks, third_blocks))
    return result.reshape(MODES_X, CHANNELS, 2, MODES_Y)

def rows_forward(field, table):
    blocks = field.reshape(16, CHANNELS // 16, GRID_SIDE, GRID_SIDE)

    def one_block(block):
        product = jnp.dot(block.reshape(-1, GRID_SIDE).astype(jnp.float32), table, precision=lax.Precision.HIGHEST)
        return product.astype(jnp.bfloat16).reshape(CHANNELS // 16, GRID_SIDE, 2, MODES_Y)
    return lax.map(one_block, blocks).reshape(CHANNELS, GRID_SIDE, 2, MODES_Y)

def rows_inverse(rows, table):
    blocks = rows.reshape(16, CHANNELS // 16 * GRID_SIDE, 2 * MODES_Y)

    def one_block(block):
        product = jnp.dot(block.astype(jnp.float32), table, precision=lax.Precision.HIGHEST)
        return (product * (1.0 / GRID_SIDE)).astype(jnp.bfloat16)
    return lax.map(one_block, blocks).reshape(CHANNELS, GRID_SIDE, GRID_SIDE)

def reference(input_field, out_cotangent, core_first, core_second, core_third, column_mode_core):
    base = width_table()
    forward_table = base.reshape(GRID_SIDE, 2 * MODES_Y).astype(jnp.float32)
    weight_c = jnp.where(jnp.arange(MODES_Y, dtype=jnp.int32) == 0, 1.0, 2.0).astype(jnp.float32)
    tables = turn_tables(jnp.arange(MODES_X, dtype=jnp.int32), jnp.arange(GRID_SIDE, dtype=jnp.int32)).astype(jnp.float32)

    def modes_of(rows):
        return jnp.einsum('kphq,chqy->kcpy', tables, rows.astype(jnp.float32), precision=lax.Precision.HIGHEST)
    spec_in = modes_of(rows_forward(input_field, forward_table)) * (1.0 / GRID_SIDE)
    spec_grad = modes_of(rows_forward(out_cotangent, forward_table)) * (weight_c / GRID_SIDE)
    spec_out, pullback = jax.vjp(mix, spec_in, core_first, core_second, core_third, column_mode_core)
    back_in, grad_one, grad_two, grad_three, grad_four = pullback(spec_grad)
    out_half = spec_out.astype(jnp.bfloat16)
    back_half = back_in.astype(jnp.bfloat16)
    inverse = tables.transpose(2, 3, 0, 1)

    def rows_of(modes):
        rows = jnp.einsum('hpkq,koqy->ohpy', inverse, modes.astype(jnp.float32), precision=lax.Precision.HIGHEST)
        return rows.astype(jnp.bfloat16)
    plain = base.transpose(1, 2, 0)
    weighted = plain * weight_c.astype(jnp.bfloat16)[None, :, None]
    output_field = rows_inverse(rows_of(out_half), weighted.reshape(2 * MODES_Y, GRID_SIDE).astype(jnp.float32))
    input_grad = rows_inverse(rows_of(back_half), plain.reshape(2 * MODES_Y, GRID_SIDE).astype(jnp.float32))
    scale = 1.0 / MODES_X
    return (output_field, input_grad, grad_one * scale, grad_two * scale, grad_three * scale, grad_four * scale)
```

```python
import math

import jax
import jax.numpy as jnp
import numpy as np
from jax import lax
from jax.experimental import pallas as pl
from jax.experimental.pallas import tpu as pltpu
from jax.sharding import PartitionSpec as P

F32 = jnp.float32
BF16 = jnp.bfloat16
HI = lax.Precision.HIGHEST
STEP = 16
LANES = 128
MESH = pl.DeviceIdType.MESH


def params(mib=48):
    return pltpu.CompilerParams(vmem_limit_bytes=mib * 2**20)


def dot(a, b, precision=None):
    return jnp.dot(a, b, preferred_element_type=F32, precision=precision)


def dot_nt(a, b, precision=None):
    return lax.dot_general(
        a, b, (((1,), (1,)), ((), ())), preferred_element_type=F32, precision=precision
    )


def dot_tn(a, b, precision=None):
    return lax.dot_general(
        a, b, (((0,), (0,)), ((), ())), preferred_element_type=F32, precision=precision
    )


def width_table(side, modes_y):
    phase = np.arange(side)[:, None] * np.arange(modes_y)[None, :] % side
    angle = phase.astype(np.float32) * np.float32(2.0 * math.pi / side)
    return np.concatenate([np.cos(angle), -np.sin(angle)], axis=1).astype(BF16)


def turn_table(side, modes_x):
    kx = np.arange(modes_x)
    freq = np.where(kx < modes_x // 2, kx, side - modes_x + kx)
    phase = freq[:, None] * np.arange(side)[None, :] % side
    angle = phase.astype(np.float32) * np.float32(2.0 * math.pi / side)
    return np.stack([np.cos(angle), np.sin(angle)]).astype(BF16)


def spread(values, rows):
    n = values.shape[1]
    lane = lax.broadcasted_iota(jnp.int32, (n, n * STEP), 1)
    row = lax.broadcasted_iota(jnp.int32, (n, n * STEP), 0)
    wide = dot(values, (lane // STEP == row).astype(BF16))
    at = lax.broadcasted_iota(jnp.int32, (STEP, n * STEP), 1) % STEP
    unit = (at == lax.broadcasted_iota(jnp.int32, (STEP, n * STEP), 0)).astype(F32)
    return (wide[:, None, :] * unit[None]).reshape(rows * STEP, n * STEP).astype(BF16)


def lead_kernel(first_t, table, cs, field, modes, lead, csf, csb, kron, pairs, held):
    step = pl.program_id(0)
    chan, _, side = field.shape
    rank = first_t.shape[0]
    wide = table.shape[1]
    my = wide // 2
    mx, n = cs.shape[1:]

    @pl.when(step == 0)
    def _():
        kron[...] = spread(first_t[...], rank)
        c, s = cs[0], cs[1]
        csf[:mx, :n], csf[:mx, n:], csf[mx:, :n], csf[mx:, n:] = c, s, -s, c
        ct = jnp.swapaxes(c.astype(F32), 0, 1).astype(BF16)
        st = jnp.swapaxes(s.astype(F32), 0, 1).astype(BF16)
        csb[:n, :mx], csb[:n, mx:], csb[n:, :mx], csb[n:, mx:] = ct, -st, st, ct

    product = dot(field[...].reshape(chan * STEP, side), table[...]).astype(BF16)
    modes[...] = product.reshape(chan, STEP, wide)
    mixed = dot(kron[...], product).astype(BF16)
    for a in range(rank):
        for q in range(2):
            at = pl.ds(pl.multiple_of(q * n + step * STEP, STEP), STEP)
            pairs[a // 2, at, a % 2 * my : (a % 2 + 1) * my] = mixed[
                a * STEP : (a + 1) * STEP, q * my : (q + 1) * my
            ]

    @pl.when(step == pl.num_programs(0) - 1)
    def _():
        for p in range(rank // 2):
            z = dot(csf[...], pairs[p]) * (1.0 / side)
            held[2 * p] = z[:, :my]
            held[2 * p + 1] = z[:, my:]
        turned = jnp.swapaxes(held[...], 0, 1).astype(BF16)
        lead[:, 0] = turned[:mx]
        lead[:, 1] = turned[mx:]


def flip(index, bits):
    bit = 1
    while bit <= bits:
        if bits & bit:
            index = index + bit * (1 - 2 * (index // bit % 2))
        bit *= 2
    return index


class Place:
    def __init__(self):
        self.grid, self.chan = lax.axis_index("grid"), lax.axis_index("chan")
        self.core = self.chan % 2
        self.planes = lax.axis_size("chan")
        self.stacks = lax.axis_size("grid") // 2
        self.plane = self.chan // 2 * 2 + self.grid % 2
        self.stack = self.grid // 2

    def across_core(self):
        return {"grid": self.grid, "chan": flip(self.chan, 1)}

    def across_plane(self, s):
        return {"grid": flip(self.grid, s % 2), "chan": flip(self.chan, s // 2 * 2)}

    def across_stack(self, s):
        return {"grid": flip(self.grid, s * 2), "chan": self.chan}

    def peers(self):
        return (
            [self.across_core()]
            + [self.across_plane(s) for s in range(1, self.planes)]
            + [self.across_stack(s) for s in range(1, self.stacks)]
        )


def remote(src, dst, send, recv, peer):
    return pltpu.make_async_remote_copy(
        src_ref=src, dst_ref=dst, send_sem=send, recv_sem=recv,
        device_id=peer, device_id_type=MESH,
    )


class Reduce:
    def __init__(self, place, source, result, land_plane, land_stack, mid, send, recv):
        self.at, self.source, self.result = place, source, result
        self.land_plane, self.land_stack, self.mid = land_plane, land_stack, mid
        self.send, self.recv = send, recv
        self.chunk = source.shape[0] // place.planes
        self.piece = self.chunk // place.stacks

    def plane_copy(self, s):
        there = flip(self.at.plane, s)
        return remote(
            self.source.at[pl.ds(there * self.chunk, self.chunk)],
            self.land_plane.at[s - 1],
            self.send.at[0, s - 1], self.recv.at[0, s - 1], self.at.across_plane(s),
        )

    def plane_send(self):
        for s in range(1, self.at.planes):
            self.plane_copy(s).start()

    def plane_wait(self):
        for s in range(1, self.at.planes):
            self.plane_copy(s).wait()
        total = self.source[pl.ds(self.at.plane * self.chunk, self.chunk)].astype(F32)
        for s in range(1, self.at.planes):
            total = total + self.land_plane[s - 1].astype(F32)
        self.mid[...] = total.astype(self.mid.dtype)

    def stack_copy(self, s):
        there = flip(self.at.stack, s)
        return remote(
            self.mid.at[pl.ds(there * self.piece, self.piece)],
            self.land_stack.at[s - 1],
            self.send.at[1, s - 1], self.recv.at[1, s - 1], self.at.across_stack(s),
        )

    def stack_send(self):
        for s in range(1, self.at.stacks):
            self.stack_copy(s).start()

    def own(self):
        return pl.ds(self.at.plane * self.chunk + self.at.stack * self.piece, self.piece)

    def stack_wait(self):
        for s in range(1, self.at.stacks):
            self.stack_copy(s).wait()
        total = self.mid[pl.ds(self.at.stack * self.piece, self.piece)].astype(F32)
        for s in range(1, self.at.stacks):
            total = total + self.land_stack[s - 1].astype(F32)
        self.result[self.own()] = total.astype(self.result.dtype)

    def stack_back_copy(self, s):
        return remote(
            self.result.at[self.own()], self.result.at[self.own()],
            self.send.at[2, s - 1], self.recv.at[2, s - 1], self.at.across_stack(s),
        )

    def stack_back_send(self):
        for s in range(1, self.at.stacks):
            self.stack_back_copy(s).start()

    def stack_back_wait(self):
        for s in range(1, self.at.stacks):
            self.stack_back_copy(s).wait()

    def plane_back_copy(self, s):
        here = pl.ds(self.at.plane * self.chunk, self.chunk)
        return remote(
            self.result.at[here], self.result.at[here],
            self.send.at[3, s - 1], self.recv.at[3, s - 1], self.at.across_plane(s),
        )

    def plane_back_send(self):
        for s in range(1, self.at.planes):
            self.plane_back_copy(s).start()

    def plane_back_wait(self):
        for s in range(1, self.at.planes):
            self.plane_back_copy(s).wait()


def spectral_kernel(
    cot, modes_in, lead, csf, csb, table, second, third, column,
    rows_out, back_rows, g_first, g_second, g_third, g_fourth,
    cot_v, modes_v, rows_v, y, held, spec_stage, spec, s_stage, spec_out,
    by_ab, by_ba, by_t, kern, lead_f, kgrad, outer, held_o, part_second, back_in, total,
    lead_core, lead_x, lead_res, lead_lp, lead_ls, lead_mid,
    lg_x, lg_all, lg_lp, lg_ls, lg_mid,
    gp_core, gp_x, gp_all, gp_lp, gp_ls, gp_mid,
    f_core, f_plane, f_stack,
    lead_send, lead_recv, lg_send, lg_recv, gp_send, gp_recv,
    core_send, core_recv, spec_send, spec_recv, out_send, out_recv, f_send, f_recv,
    cot_sem, modes_sem, rows_sem,
):
    at = Place()
    core = at.core
    other = 1 - core
    chan, n, side = cot.shape
    wide = table.shape[1]
    my = wide // 2
    mx = lead.shape[0]
    half = mx // 2
    ra, rb, rd = lead.shape[2], third.shape[0], third.shape[1]
    pairs = ra * rb
    both = second.shape[1]
    channels = g_first.shape[1]
    sub = cot_v.shape[1]
    slots = cot_v.shape[0]
    subs = chan // sub
    lane = lax.broadcasted_iota(jnp.int32, (1, wide), 1)
    weight = jnp.where(lane % my == 0, 1.0, 2.0) * (1.0 / side)
    partner = at.across_core()

    def cot_copy(j):
        return pltpu.make_async_copy(
            cot.at[pl.ds(j * sub, sub)], cot_v.at[lax.rem(j, slots)], cot_sem.at[lax.rem(j, slots)]
        )

    modes_copy = pltpu.make_async_copy(modes_in, modes_v, modes_sem)

    barrier = pltpu.get_barrier_semaphore()
    peers = at.peers()
    for peer in peers:
        pl.semaphore_signal(barrier, inc=1, device_id=peer, device_id_type=MESH)
    for j in range(slots):
        cot_copy(j).start()
    modes_copy.start()

    sec = second[...]
    by_ab[...] = sec.astype(BF16)
    by_ba[...] = jnp.swapaxes(sec.reshape(ra, rb, both), 0, 1).reshape(pairs, both).astype(BF16)
    by_t[...] = jnp.swapaxes(sec, 0, 1).astype(BF16)
    col = jnp.concatenate([column[0], column[1]], axis=1)
    for b in range(rb):
        kgrad[b * half : (b + 1) * half, :] = dot_tn(third[b], col, HI)
    kern[...] = jnp.swapaxes(kgrad[...].reshape(rb, half, wide), 0, 1)

    lead_sum = Reduce(at, lead_x, lead_res, lead_lp, lead_ls, lead_mid, lead_send, lead_recv)
    lg_sum = Reduce(at, lg_x, lg_all.at[core], lg_lp, lg_ls, lg_mid, lg_send, lg_recv)
    gp_sum = Reduce(at, gp_x, gp_all.at[core], gp_lp, gp_ls, gp_mid, gp_send, gp_recv)

    def lead_core_copy():
        return remote(
            lead.at[pl.ds(other * half, half)], lead_core, core_send.at[0], core_recv.at[0], partner
        )

    pl.semaphore_wait(barrier, len(peers))
    lead_core_copy().start()

    def lead_start():
        lead_core_copy().wait()
        mine = lead[pl.ds(core * half, half)].astype(F32) + lead_core[...].astype(F32)
        lead_x[...] = mine.reshape(lead_x.shape).astype(BF16)
        lead_sum.plane_send()

    def spec_copy(i):
        return remote(
            spec_stage.at[i, pl.ds(other * half, half)],
            spec.at[:, pl.ds(core * chan + i * STEP, STEP), :],
            spec_send.at[i], spec_recv.at[i], partner,
        )

    def cot_body(i, carry):
        for s in range(STEP // sub):
            j = i * (STEP // sub) + s
            cot_copy(j).wait()
            block = cot_v[lax.rem(j, slots)].reshape(sub * n, side)
            product = dot(block, table[...]).astype(BF16)

            @pl.when(j + slots < subs)
            def _():
                cot_copy(j + slots).start()

            for c in range(sub):
                for q in range(2):
                    y[c // 2, q * n : (q + 1) * n, c % 2 * my : (c % 2 + 1) * my] = product[
                        c * n : (c + 1) * n, q * my : (q + 1) * my
                    ]
            for p in range(sub // 2):
                z = dot(csf[...], y[p]) * weight
                held[s * sub + 2 * p] = z[:, :my]
                held[s * sub + 2 * p + 1] = z[:, my:]
        turned = jnp.swapaxes(held[...], 0, 1).astype(BF16)
        spec_stage[i, :, :, :my] = turned[:mx]
        spec_stage[i, :, :, my:] = turned[mx:]
        spec_copy(i).start()
        spec[:, pl.ds(pl.multiple_of(core * chan + i * STEP, STEP), STEP), :] = spec_stage[
            i, pl.ds(core * half, half)
        ]

        @pl.when(i == 0)
        def _():
            lead_start()

        return carry

    lax.fori_loop(0, chan // STEP, cot_body, 0)
    lead_sum.plane_wait()
    lead_sum.stack_send()
    for i in range(chan // STEP):
        spec_copy(i).wait()

    unroll = 4

    def back_body(j, carry):
        for u in range(unroll):
            k = j * unroll + u
            g = dot(by_ba[...], spec[k])
            re = jnp.zeros((ra, my), F32)
            im = jnp.zeros((ra, my), F32)
            for b in range(rb):
                gre = g[b * ra : (b + 1) * ra, :my]
                gim = g[b * ra : (b + 1) * ra, my:]
                kre, kim = kern[k, b : b + 1, :my], kern[k, b : b + 1, my:]
                re += gre * kre + gim * kim
                im += gim * kre - gre * kim
            lg_x[2 * k] = re.astype(BF16)
            lg_x[2 * k + 1] = im.astype(BF16)
        return carry

    lax.fori_loop(0, half // unroll, back_body, 0)
    lg_sum.plane_send()
    lead_sum.stack_wait()
    lead_sum.stack_back_send()
    lead_sum.stack_back_wait()
    lead_sum.plane_back_send()
    lg_sum.plane_wait()
    lg_sum.stack_send()
    lead_sum.plane_back_wait()
    whole_lead = lead_res[...].reshape(half, 2, ra, my).astype(F32)
    lead_f[:, :, :my] = whole_lead[:, 0]
    lead_f[:, :, my:] = whole_lead[:, 1]
    part_second[...] = jnp.zeros_like(part_second)

    def out_copy(g):
        return remote(
            s_stage.at[g, pl.ds(other * (chan // 2), chan // 2)],
            spec_out.at[:, :, pl.ds(core * half + g * STEP, STEP), :],
            out_send.at[g], out_recv.at[g], partner,
        )

    per = 2

    def mix_body(j, carry):
        for u in range(per):
            k = j * per + u
            g = dot(by_ab[...], spec[k])
            kr = kern[k]
            kre, kim = kr[:, :my], kr[:, my:]
            re = jnp.zeros((rb, my), F32)
            im = jnp.zeros((rb, my), F32)
            for a in range(ra):
                rows = slice(a * rb, (a + 1) * rb)
                lre, lim = lead_f[k, a : a + 1, :my], lead_f[k, a : a + 1, my:]
                outer[rows, u * wide : u * wide + my] = (kre * lre - kim * lim).astype(BF16)
                outer[rows, u * wide + my : (u + 1) * wide] = (kre * lim + kim * lre).astype(BF16)
                gre, gim = g[rows, :my], g[rows, my:]
                re += gre * lre + gim * lim
                im += gim * lre - gre * lim
            at_k = pl.ds(pl.multiple_of(k * rb, rb), rb)
            kgrad[at_k, :my] = re
            kgrad[at_k, my:] = im
        for u in range(per):
            k = j * per + u
            held_o[lax.rem(k, STEP)] = dot(by_t[...], outer[:, u * wide : (u + 1) * wide])
        rhs = jnp.concatenate([spec[j * per + u] for u in range(per)], axis=1)
        part_second[...] += dot_nt(outer[...], rhs)
        return carry

    def mix_group(g, carry):
        lax.fori_loop(g * (STEP // per), (g + 1) * (STEP // per), mix_body, 0)
        turned = jnp.swapaxes(held_o[...], 0, 1).astype(BF16)
        turned = turned.reshape(both // 2, 2, STEP, wide)
        for c in range(2):
            for q in range(2):
                s_stage[g, :, q, :, c * my : (c + 1) * my] = turned[
                    :, c, :, q * my : (q + 1) * my
                ]
        out_copy(g).start()
        row = pl.ds(pl.multiple_of(core * half + g * STEP, STEP), STEP)
        spec_out[:, :, row, :] = s_stage[g, pl.ds(core * (chan // 2), chan // 2)]

        @pl.when(g == 1)
        def _():
            lg_sum.stack_wait()
            lg_sum.stack_back_send()

        @pl.when(g == 2)
        def _():
            lg_sum.stack_back_wait()
            lg_sum.plane_back_send()

        return carry

    groups = half // STEP
    lax.fori_loop(0, groups, mix_group, 0)

    def second_copy():
        return remote(
            part_second.at[pl.ds(other * (pairs // 2), pairs // 2)], gp_core,
            core_send.at[1], core_recv.at[1], partner,
        )

    def back_copy():
        return remote(lg_all.at[core], lg_all.at[core], core_send.at[2], core_recv.at[2], partner)

    second_copy().start()
    lg_sum.plane_back_wait()
    back_copy().start()
    by_mode = jnp.swapaxes(kgrad[...].reshape(half, rb, wide), 0, 1).reshape(rb * half, wide)
    part_third = dot_nt(col, by_mode, HI)
    third_flat = jnp.concatenate([third[b] for b in range(rb)], axis=1)
    part_fourth = dot(third_flat, by_mode, HI)
    second_copy().wait()
    mine = part_second[pl.ds(core * (pairs // 2), pairs // 2)] + gp_core[...]
    lane_c = lax.broadcasted_iota(jnp.int32, (both, channels), 1)
    row_c = lax.broadcasted_iota(jnp.int32, (both, channels), 0)
    mine = dot(mine, (lane_c == row_c + at.chan // 2 * both).astype(F32), HI)

    pieces = []
    for value in (mine, part_third, part_fourth):
        for c in range(value.shape[1] // LANES):
            pieces.append((value, c))
    spots, count = [], 0
    for value, c in pieces:
        tiles = value.shape[0] // 8
        gp_x[count : count + tiles] = value[:, c * LANES : (c + 1) * LANES].reshape(
            tiles, 8, LANES
        )
        spots.append((count, tiles))
        count += tiles
    if count < gp_x.shape[0]:
        gp_x[count:] = jnp.zeros((gp_x.shape[0] - count, 8, LANES), F32)
    gp_sum.plane_send()

    back_copy().wait()
    for q in range(2):
        for h in range(2):
            got = lg_all[h].reshape(half, 2, ra, my)[:, q].astype(F32)
            turned = jnp.swapaxes(got, 0, 1).astype(BF16)
            for a in range(ra):
                back_in[
                    a // 2, q * mx + h * half : q * mx + (h + 1) * half,
                    a % 2 * my : (a % 2 + 1) * my,
                ] = turned[a]
    for p in range(ra // 2):
        r = dot(csb[...], back_in[p]).astype(BF16)
        for c in range(2):
            for q in range(2):
                back_rows[2 * p + c, :, q * my : (q + 1) * my] = r[
                    q * n : (q + 1) * n, c * my : (c + 1) * my
                ]
    modes_copy.wait()
    total[...] = jnp.zeros_like(total)

    def first_body(i, carry):
        row = pl.ds(pl.multiple_of(i * STEP, STEP), STEP)
        block = back_rows[:, row, :].reshape(ra * STEP, wide)
        total[...] += dot_nt(modes_v[:, row, :].reshape(chan * STEP, wide), block)
        return carry

    lax.fori_loop(0, n // STEP, first_body, 0)
    gp_sum.plane_wait()
    gp_sum.stack_send()
    shape = (STEP, ra * STEP)
    unit = lax.broadcasted_iota(jnp.int32, shape, 1) % STEP == lax.broadcasted_iota(
        jnp.int32, shape, 0
    )
    kept = total[...].reshape(chan, STEP, ra * STEP) * unit.astype(F32)[None]
    lane_f = lax.broadcasted_iota(jnp.int32, (ra, ra * STEP), 1)
    row_f = lax.broadcasted_iota(jnp.int32, (ra, ra * STEP), 0)
    pick = (lane_f // STEP == row_f).astype(F32)
    part_first = dot_nt(pick, jnp.sum(kept, axis=1), HI)
    lane_f = lax.broadcasted_iota(jnp.int32, (chan, channels), 1)
    row_f = lax.broadcasted_iota(jnp.int32, (chan, channels), 0)
    place_f = (lane_f == row_f + at.chan * chan).astype(F32)
    f_core[core] = dot(part_first, place_f, HI)

    def first_core_copy():
        return remote(f_core.at[core], f_core.at[core], core_send.at[3], core_recv.at[3], partner)

    def first_plane_copy(s):
        return remote(
            f_plane.at[at.plane], f_plane.at[at.plane],
            f_send.at[0, s - 1], f_recv.at[0, s - 1], at.across_plane(s),
        )

    def first_stack_copy(s):
        return remote(
            f_stack.at[at.stack], f_stack.at[at.stack],
            f_send.at[1, s - 1], f_recv.at[1, s - 1], at.across_stack(s),
        )

    def first_plane():
        first_core_copy().wait()
        f_plane[at.plane] = f_core[0] + f_core[1]
        for s in range(1, at.planes):
            first_plane_copy(s).start()

    def first_stack():
        for s in range(1, at.planes):
            first_plane_copy(s).wait()
        value = f_plane[0]
        for s in range(1, at.planes):
            value = value + f_plane[s]
        f_stack[at.stack] = value
        for s in range(1, at.stacks):
            first_stack_copy(s).start()

    first_core_copy().start()
    for g in range(groups):
        out_copy(g).wait()

    turns = 4

    def rows_copy(i):
        where = pl.ds(i * 2 * turns, 2 * turns)
        return pltpu.make_async_copy(rows_v.at[where], rows_out.at[where], rows_sem.at[i])

    def rows_body(i, carry):
        for t in range(turns):
            p = i * turns + t
            r = (dot(csb[...], spec_out[p].reshape(2 * mx, wide)) * weight).astype(BF16)
            for c in range(2):
                for q in range(2):
                    rows_v[2 * p + c, :, q * my : (q + 1) * my] = r[
                        q * n : (q + 1) * n, c * my : (c + 1) * my
                    ]
        rows_copy(i).start()

        @pl.when(i == 0)
        def _():
            first_plane()

        return carry

    steps = chan // 2 // turns
    lax.fori_loop(0, steps, rows_body, 0)
    first_stack()
    gp_sum.stack_wait()
    gp_sum.stack_back_send()
    gp_sum.stack_back_wait()
    gp_sum.plane_back_send()
    for s in range(1, at.stacks):
        first_stack_copy(s).wait()
    value = f_stack[0]
    for s in range(1, at.stacks):
        value = value + f_stack[s]
    g_first[...] = value * (1.0 / (side * mx))
    gp_sum.plane_back_wait()

    def grads_copy():
        return remote(gp_all.at[core], gp_all.at[core], core_send.at[4], core_recv.at[4], partner)

    grads_copy().start()
    grads_copy().wait()

    def tile(h, index):
        start, size = spots[index]
        return gp_all[h, start : start + size].reshape(size * 8, LANES) * (1.0 / mx)

    cols = channels // LANES
    for h in range(2):
        for c in range(cols):
            g_second[
                h * (pairs // 2) : (h + 1) * (pairs // 2), c * LANES : (c + 1) * LANES
            ] = tile(h, c)
    low = lax.broadcasted_iota(jnp.int32, (rd, LANES), 1) < half
    for j in range(rb // 2):
        t0, t1 = tile(0, cols + j), tile(1, cols + j)
        g_third[2 * j] = jnp.where(low, t0, pltpu.roll(t1, half, 1))
        g_third[2 * j + 1] = jnp.where(low, pltpu.roll(t0, half, 1), t1)
    for q in range(2):
        g_fourth[q] = tile(0, cols + rb // 2 + q) + tile(1, cols + rb // 2 + q)
    for i in range(steps):
        rows_copy(i).wait()


def output_kernel(table, rows, out):
    chan, n, side = out.shape
    out[...] = dot(rows[...].reshape(chan * n, rows.shape[2]), table[...]).astype(BF16).reshape(
        out.shape
    )


def input_kernel(first, table, rows, out, kron):
    rank, _, wide = rows.shape
    chan, _, side = out.shape

    @pl.when(pl.program_id(0) == 0)
    def _():
        kron[...] = spread(first[...], chan)

    block = dot(kron[...], rows[...].reshape(rank * STEP, wide)) * (1.0 / side)
    out[...] = dot(block.astype(BF16), table[...]).astype(BF16).reshape(out.shape)


def whole(shape):
    return pl.BlockSpec(shape, lambda i: (0,) * len(shape))


def local(input_field, out_cotangent, core_first, core_second, core_third, column_mode_core):
    grid_count, chan_count = lax.axis_size("grid"), lax.axis_size("chan")
    grid_index = lax.axis_index("grid")
    chan_index = lax.axis_index("chan")
    chan, rows, side = input_field.shape
    channels, rank_a = core_first.shape
    rank_b, modes_x, rank_d = core_third.shape
    modes_y = column_mode_core.shape[2]
    wide = 2 * modes_y
    half = modes_x // 2
    both = 2 * chan
    pairs = rank_a * rank_b

    table_np = width_table(side, modes_y)
    table = jnp.asarray(table_np)
    table_t = jnp.asarray(np.ascontiguousarray(table_np.T))
    turns = turn_table(side, modes_x).reshape(2, modes_x, grid_count, rows)
    turns = jnp.asarray(np.ascontiguousarray(turns.transpose(2, 0, 1, 3)))
    cs = lax.dynamic_index_in_dim(turns, grid_index, 0, keepdims=False)

    first_local = lax.dynamic_slice_in_dim(core_first, chan_index * chan, chan, 0).astype(BF16)
    second = core_second.transpose(0, 2, 1).reshape(pairs, channels)
    second = lax.dynamic_slice_in_dim(second, chan_index // 2 * both, both, 1)
    third = lax.dynamic_slice_in_dim(
        core_third.transpose(0, 2, 1), chan_index % 2 * half, half, 2
    )

    row_steps = rows // STEP
    row_modes, lead, csf, csb = pl.pallas_call(
        lead_kernel,
        grid=(row_steps,),
        in_specs=[
            whole((rank_a, chan)),
            whole((side, wide)),
            whole((2, modes_x, rows)),
            pl.BlockSpec((chan, STEP, side), lambda i: (0, i, 0)),
        ],
        out_specs=[
            pl.BlockSpec((chan, STEP, wide), lambda i: (0, i, 0)),
            whole((modes_x, 2, rank_a, modes_y)),
            whole((2 * modes_x, 2 * rows)),
            whole((2 * rows, 2 * modes_x)),
        ],
        out_shape=[
            jax.ShapeDtypeStruct((chan, rows, wide), BF16),
            jax.ShapeDtypeStruct((modes_x, 2, rank_a, modes_y), BF16),
            jax.ShapeDtypeStruct((2 * modes_x, 2 * rows), BF16),
            jax.ShapeDtypeStruct((2 * rows, 2 * modes_x), BF16),
        ],
        scratch_shapes=[
            pltpu.VMEM((rank_a * STEP, chan * STEP), BF16),
            pltpu.VMEM((rank_a // 2, 2 * rows, wide), BF16),
            pltpu.VMEM((rank_a, 2 * modes_x, modes_y), F32),
        ],
        compiler_params=params(),
        name="lead",
    )(first_local.T, table, cs, input_field)

    planes, stacks = chan_count, grid_count // 2
    tiles = 2 * half
    owners = planes * stacks
    grad_tiles = (pairs // 2 * channels + rank_d * rank_b * half + rank_d * wide) // (8 * LANES)
    grad_tiles += -grad_tiles % owners
    sub = min(8, STEP)
    subs = chan // sub
    slots = min(4, subs)
    blocks = chan // STEP
    groups = half // STEP
    peers = max(planes, stacks) - 1
    steps = chan // 8

    def reduce_buffers(count, shape, dtype):
        chunk = count // planes
        return [
            pltpu.VMEM((planes - 1, chunk, *shape), dtype),
            pltpu.VMEM((stacks - 1, chunk // stacks, *shape), dtype),
            pltpu.VMEM((chunk, *shape), dtype),
        ]

    tile = (rank_a, modes_y)
    scratch = [
        pltpu.VMEM((slots, sub, rows, side), BF16),
        pltpu.VMEM((chan, rows, wide), BF16),
        pltpu.VMEM((chan, rows, wide), BF16),
        pltpu.VMEM((sub // 2, 2 * rows, wide), BF16),
        pltpu.VMEM((STEP, 2 * modes_x, modes_y), F32),
        pltpu.VMEM((blocks, modes_x, STEP, wide), BF16),
        pltpu.VMEM((half, both, wide), BF16),
        pltpu.VMEM((groups, chan, 2, STEP, wide), BF16),
        pltpu.VMEM((chan // 2, 2, modes_x, wide), BF16),
        pltpu.VMEM((pairs, both), BF16),
        pltpu.VMEM((pairs, both), BF16),
        pltpu.VMEM((both, pairs), BF16),
        pltpu.VMEM((half, rank_b, wide), F32),
        pltpu.VMEM((half, rank_a, wide), F32),
        pltpu.VMEM((half * rank_b, wide), F32),
        pltpu.VMEM((pairs, 2 * wide), BF16),
        pltpu.VMEM((STEP, both, wide), F32),
        pltpu.VMEM((pairs, both), F32),
        pltpu.VMEM((rank_a // 2, 2 * modes_x, wide), BF16),
        pltpu.VMEM((chan * STEP, rank_a * STEP), F32),
        pltpu.VMEM((half, 2, *tile), BF16),
        pltpu.VMEM((tiles, *tile), BF16),
        pltpu.VMEM((tiles, *tile), BF16),
        *reduce_buffers(tiles, tile, BF16),
        pltpu.VMEM((tiles, *tile), BF16),
        pltpu.VMEM((2, tiles, *tile), BF16),
        *reduce_buffers(tiles, tile, BF16),
        pltpu.VMEM((pairs // 2, both), F32),
        pltpu.VMEM((grad_tiles, 8, LANES), F32),
        pltpu.VMEM((2, grad_tiles, 8, LANES), F32),
        *reduce_buffers(grad_tiles, (8, LANES), F32),
        pltpu.VMEM((2, rank_a, channels), F32),
        pltpu.VMEM((planes, rank_a, channels), F32),
        pltpu.VMEM((stacks, rank_a, channels), F32),
        *[pltpu.SemaphoreType.DMA((4, peers))] * 6,
        *[pltpu.SemaphoreType.DMA((5,))] * 2,
        *[pltpu.SemaphoreType.DMA((blocks,))] * 2,
        *[pltpu.SemaphoreType.DMA((groups,))] * 2,
        *[pltpu.SemaphoreType.DMA((2, peers))] * 2,
        pltpu.SemaphoreType.DMA((slots,)),
        pltpu.SemaphoreType.DMA,
        pltpu.SemaphoreType.DMA((steps,)),
    ]
    vmem = pl.BlockSpec(memory_space=pltpu.VMEM)
    anywhere = pl.BlockSpec(memory_space=pl.ANY)
    out_rows, back_rows, g_first, g_second, g_third, g_fourth = pl.pallas_call(
        spectral_kernel,
        in_specs=[anywhere, anywhere] + [vmem] * 7,
        out_specs=[anywhere] + [vmem] * 5,
        out_shape=[
            jax.ShapeDtypeStruct((chan, rows, wide), BF16),
            jax.ShapeDtypeStruct((rank_a, rows, wide), BF16),
            jax.ShapeDtypeStruct((rank_a, channels), F32),
            jax.ShapeDtypeStruct((pairs, channels), F32),
            jax.ShapeDtypeStruct((rank_b, rank_d, modes_x), F32),
            jax.ShapeDtypeStruct((2, rank_d, modes_y), F32),
        ],
        scratch_shapes=scratch,
        compiler_params=pltpu.CompilerParams(
            collective_id=0, has_side_effects=True, vmem_limit_bytes=62 * 2**20
        ),
        name="spectral",
    )(out_cotangent, row_modes, lead, csf, csb, table, second, third, column_mode_core)

    out_step = min(chan, 8)
    output_field = pl.pallas_call(
        output_kernel,
        grid=(chan // out_step,),
        in_specs=[
            whole((wide, side)),
            pl.BlockSpec((out_step, rows, wide), lambda i: (i, 0, 0)),
        ],
        out_specs=pl.BlockSpec((out_step, rows, side), lambda i: (i, 0, 0)),
        out_shape=jax.ShapeDtypeStruct((chan, rows, side), BF16),
        compiler_params=params(),
        name="output",
    )(table_t, out_rows)

    input_grad = pl.pallas_call(
        input_kernel,
        grid=(row_steps,),
        in_specs=[
            whole((chan, rank_a)),
            whole((wide, side)),
            pl.BlockSpec((rank_a, STEP, wide), lambda i: (0, i, 0)),
        ],
        out_specs=pl.BlockSpec((chan, STEP, side), lambda i: (0, i, 0)),
        out_shape=jax.ShapeDtypeStruct((chan, rows, side), BF16),
        scratch_shapes=[pltpu.VMEM((chan * STEP, rank_a * STEP), BF16)],
        compiler_params=params(),
        name="input_grad",
    )(first_local, table_t, back_rows)

    return (
        output_field,
        input_grad,
        g_first.T,
        g_second.reshape(rank_a, rank_b, channels).transpose(0, 2, 1),
        g_third.transpose(0, 2, 1),
        g_fourth,
    )


def solution(mesh):
    placed = (P("chan", "grid", None), P("chan", "grid", None), P(), P(), P(), P())
    return jax.shard_map(
        local,
        mesh=mesh,
        in_specs=placed,
        out_specs=(P("chan", "grid", None), P("chan", "grid", None), P(), P(), P(), P()),
        check_vma=False,
    )
```

```python
import math

import jax
import jax.numpy as jnp
import numpy as np
from jax import lax
from jax.experimental import pallas as pl
from jax.experimental.pallas import tpu as pltpu
from jax.sharding import PartitionSpec as P

F32 = jnp.float32
BF16 = jnp.bfloat16
HI = lax.Precision.HIGHEST
STEP = 16
LANES = 128
SLOTS = 3
MESH = pl.DeviceIdType.MESH


def params(mib=48):
    return pltpu.CompilerParams(vmem_limit_bytes=mib * 2**20)


def dot(a, b, precision=None):
    return jnp.dot(a, b, preferred_element_type=F32, precision=precision)


def dot_nt(a, b, precision=None):
    return lax.dot_general(
        a, b, (((1,), (1,)), ((), ())), preferred_element_type=F32, precision=precision
    )


def dot_tn(a, b, precision=None):
    return lax.dot_general(
        a, b, (((0,), (0,)), ((), ())), preferred_element_type=F32, precision=precision
    )


def width_table(side, modes_y):
    phase = np.arange(side)[:, None] * np.arange(modes_y)[None, :] % side
    angle = phase.astype(np.float32) * np.float32(2.0 * math.pi / side)
    return np.concatenate([np.cos(angle), -np.sin(angle)], axis=1).astype(BF16)


def turn_table(side, modes_x):
    kx = np.arange(modes_x)
    freq = np.where(kx < modes_x // 2, kx, side - modes_x + kx)
    phase = freq[:, None] * np.arange(side)[None, :] % side
    angle = phase.astype(np.float32) * np.float32(2.0 * math.pi / side)
    return np.stack([np.cos(angle), np.sin(angle)]).astype(BF16)


def one_hot(rows, cols, offset):
    row = lax.broadcasted_iota(jnp.int32, (rows, cols), 0)
    col = lax.broadcasted_iota(jnp.int32, (rows, cols), 1)
    return col == row + offset


def spread(values, rows, n, offset=0):
    lane = lax.broadcasted_iota(jnp.int32, (values.shape[1], n * STEP), 1)
    row = lax.broadcasted_iota(jnp.int32, (values.shape[1], n * STEP), 0)
    wide = dot(values, (lane // STEP + offset == row).astype(BF16))
    at = lax.broadcasted_iota(jnp.int32, (STEP, n * STEP), 1) % STEP
    unit = (at == lax.broadcasted_iota(jnp.int32, (STEP, n * STEP), 0)).astype(F32)
    return (wide[:, None, :] * unit[None]).reshape(rows * STEP, n * STEP).astype(BF16)


def flip(index, bits):
    bit = 1
    while bit <= bits:
        if bits & bit:
            index = index + bit * (1 - 2 * (index // bit % 2))
        bit *= 2
    return index


class Place:
    def __init__(self):
        self.grid, self.chan = lax.axis_index("grid"), lax.axis_index("chan")
        self.core = self.chan % 2
        self.planes = lax.axis_size("chan")
        self.stacks = lax.axis_size("grid") // 2
        self.plane = self.chan // 2 * 2 + self.grid % 2
        self.stack = self.grid // 2

    def across_core(self):
        return {"grid": self.grid, "chan": flip(self.chan, 1)}

    def across_plane(self, s):
        return {"grid": flip(self.grid, s % 2), "chan": flip(self.chan, s // 2 * 2)}

    def across_stack(self, s):
        return {"grid": flip(self.grid, s * 2), "chan": self.chan}

    def peers(self):
        return (
            [self.across_core()]
            + [self.across_plane(s) for s in range(1, self.planes)]
            + [self.across_stack(s) for s in range(1, self.stacks)]
        )


def remote(src, dst, send, recv, peer):
    return pltpu.make_async_remote_copy(
        src_ref=src, dst_ref=dst, send_sem=send, recv_sem=recv,
        device_id=peer, device_id_type=MESH,
    )


class Reduce:
    def __init__(self, place, source, result, land_plane, land_stack, mid, send, recv):
        self.at, self.source, self.result = place, source, result
        self.land_plane, self.land_stack, self.mid = land_plane, land_stack, mid
        self.send, self.recv = send, recv
        self.chunk = source.shape[0] // place.planes
        self.piece = self.chunk // place.stacks

    def plane_copy(self, s):
        there = flip(self.at.plane, s)
        return remote(
            self.source.at[pl.ds(there * self.chunk, self.chunk)],
            self.land_plane.at[s - 1],
            self.send.at[0, s - 1], self.recv.at[0, s - 1], self.at.across_plane(s),
        )

    def plane_send(self):
        for s in range(1, self.at.planes):
            self.plane_copy(s).start()

    def plane_wait(self):
        for s in range(1, self.at.planes):
            self.plane_copy(s).wait()
        total = self.source[pl.ds(self.at.plane * self.chunk, self.chunk)].astype(F32)
        for s in range(1, self.at.planes):
            total = total + self.land_plane[s - 1].astype(F32)
        self.mid[...] = total.astype(self.mid.dtype)

    def stack_copy(self, s):
        there = flip(self.at.stack, s)
        return remote(
            self.mid.at[pl.ds(there * self.piece, self.piece)],
            self.land_stack.at[s - 1],
            self.send.at[1, s - 1], self.recv.at[1, s - 1], self.at.across_stack(s),
        )

    def stack_send(self):
        for s in range(1, self.at.stacks):
            self.stack_copy(s).start()

    def own(self):
        return pl.ds(self.at.plane * self.chunk + self.at.stack * self.piece, self.piece)

    def stack_wait(self):
        for s in range(1, self.at.stacks):
            self.stack_copy(s).wait()
        total = self.mid[pl.ds(self.at.stack * self.piece, self.piece)].astype(F32)
        for s in range(1, self.at.stacks):
            total = total + self.land_stack[s - 1].astype(F32)
        self.result[self.own()] = total.astype(self.result.dtype)

    def stack_back_copy(self, s):
        return remote(
            self.result.at[self.own()], self.result.at[self.own()],
            self.send.at[2, s - 1], self.recv.at[2, s - 1], self.at.across_stack(s),
        )

    def stack_back_send(self):
        for s in range(1, self.at.stacks):
            self.stack_back_copy(s).start()

    def stack_back_wait(self):
        for s in range(1, self.at.stacks):
            self.stack_back_copy(s).wait()

    def plane_back_copy(self, s):
        here = pl.ds(self.at.plane * self.chunk, self.chunk)
        return remote(
            self.result.at[here], self.result.at[here],
            self.send.at[3, s - 1], self.recv.at[3, s - 1], self.at.across_plane(s),
        )

    def plane_back_send(self):
        for s in range(1, self.at.planes):
            self.plane_back_copy(s).start()

    def plane_back_wait(self):
        for s in range(1, self.at.planes):
            self.plane_back_copy(s).wait()


def spectral_kernel(
    field, cot, turns_in, table, first_t, second, third, column,
    rows_out, back_rows, g_first, g_second, g_third, g_fourth,
    block_v, modes_v, y, held, spec_stage, spec, s_stage, spec_out, cs, csf, csb, kron, mixed,
    by_ab, by_ba, by_t, kern, lead_f, kgrad, outer, held_o, part_second, back_in, total,
    lead_v, lead_core, lead_x, lead_res, lead_lp, lead_ls, lead_mid,
    lg_x, lg_all, lg_lp, lg_ls, lg_mid,
    gp_core, gp_x, gp_all, gp_lp, gp_ls, gp_mid,
    f_core, f_plane, f_stack,
    lead_send, lead_recv, lg_send, lg_recv, gp_send, gp_recv,
    core_send, core_recv, spec_send, spec_recv, out_send, out_recv, f_send, f_recv,
    block_sem, turns_sem, rows_sem,
):
    if outer.shape[0] * outer.shape[1] * 2 < kern.shape[0]:
        outer = block_v
    at = Place()
    core = at.core
    other = 1 - core
    chan, n, side = cot.shape
    wide = table.shape[1]
    my = wide // 2
    mx = cs.shape[1]
    half = mx // 2
    ra, rb, rd = first_t.shape[0], third.shape[0], third.shape[1]
    pairs = ra * rb
    both = 2 * chan
    channels = g_first.shape[1]
    slots, sub = block_v.shape[:2]
    subs = chan // sub
    parts = lead_lp.shape[0]
    row_groups = n // STEP
    lane = lax.broadcasted_iota(jnp.int32, (1, wide), 1)
    weight = jnp.where(lane % my == 0, 1.0, 2.0) * (1.0 / side)
    partner = at.across_core()

    def block_copy(source, j, k):
        slot = lax.rem(k, slots)
        return pltpu.make_async_copy(
            source.at[pl.ds(j * sub, sub)], block_v.at[slot], block_sem.at[slot]
        )

    def fetch(k):
        @pl.when(k < subs)
        def _():
            block_copy(field, k, k).start()

        @pl.when(jnp.logical_and(k >= subs, k < 2 * subs))
        def _():
            block_copy(cot, k - subs, k).start()

    def rows_of_block(source, j, k):
        block_copy(source, j, k).wait()
        block = block_v[lax.rem(k, slots)].reshape(sub * n, side)
        product = dot(block, table[...]).astype(BF16)
        fetch(k + slots)
        return product

    barrier = pltpu.get_barrier_semaphore()
    peers = at.peers()
    for peer in peers:
        pl.semaphore_signal(barrier, inc=1, device_id=peer, device_id_type=MESH)
    for k in range(min(slots, 2 * subs)):
        fetch(jnp.int32(k))
    turns_copy = pltpu.make_async_copy(turns_in.at[at.grid], cs, turns_sem)
    turns_copy.start()
    kron[...] = spread(first_t[...].astype(BF16), ra, chan, at.chan * chan)
    turns_copy.wait()
    c, s = cs[0], cs[1]
    csf[:mx, :n], csf[:mx, n:], csf[mx:, :n], csf[mx:, n:] = c, s, -s, c
    ct = jnp.swapaxes(c.astype(F32), 0, 1).astype(BF16)
    st = jnp.swapaxes(s.astype(F32), 0, 1).astype(BF16)
    csb[:n, :mx], csb[:n, mx:], csb[n:, :mx], csb[n:, mx:] = ct, -st, st, ct

    mixed[...] = jnp.zeros_like(mixed)

    def field_body(i, carry):
        product = rows_of_block(field, i, i)
        shaped = product.reshape(sub, n, wide)
        modes_v[pl.ds(i * sub, sub)] = shaped
        for g in range(row_groups):
            y[: sub * STEP, g * wide : (g + 1) * wide] = shaped[
                :, g * STEP : (g + 1) * STEP
            ].reshape(sub * STEP, wide)
        part = pl.ds(pl.multiple_of(i * sub * STEP, sub * STEP), sub * STEP)
        mixed[...] += dot(kron[:, part], y[: sub * STEP, : row_groups * wide])
        return carry

    lax.fori_loop(0, subs, field_body, 0)
    for g in range(row_groups):
        for q in range(2):
            for a in range(ra):
                back_in[q * n + g * STEP : q * n + (g + 1) * STEP, a * my : (a + 1) * my] = mixed[
                    a * STEP : (a + 1) * STEP, g * wide + q * my : g * wide + (q + 1) * my
                ].astype(BF16)
    z = dot(csf[...], back_in[: 2 * n]) * (1.0 / side)
    for a in range(ra):
        held[a] = z[:, a * my : (a + 1) * my]
    turned = jnp.swapaxes(held[...], 0, 1).astype(BF16)
    lead_v[:, 0] = turned[:mx]
    lead_v[:, 1] = turned[mx:]

    def lead_core_copy():
        return remote(
            lead_v.at[pl.ds(other * half, half)], lead_core,
            core_send.at[0], core_recv.at[0], partner,
        )

    pl.semaphore_wait(barrier, len(peers))
    lead_core_copy().start()

    if second.shape[1] > both and both % LANES == 0:
        sec = second[:, pl.ds(pl.multiple_of(at.chan // 2 * both, both), both)]
    else:
        sec = second[...]
    by_ab[...] = sec.astype(BF16)
    by_ba[...] = jnp.swapaxes(sec.reshape(ra, rb, both), 0, 1).reshape(pairs, both).astype(BF16)
    by_t[...] = jnp.swapaxes(sec, 0, 1).astype(BF16)
    col = jnp.concatenate([column[0], column[1]], axis=1)
    for b in range(rb):
        held_o[b, :mx] = dot_tn(third[b], col, HI)
    own_half = pl.ds(pl.multiple_of(core * half, half), half)
    kern[...] = jnp.swapaxes(held_o[:, own_half, :], 0, 1)

    def sums(source, result, land_plane, land_stack, mid, send, recv):
        share = source.shape[0] // parts
        made = []
        for p in range(parts):
            where = pl.ds(p * share, share)
            made.append(Reduce(
                at, source.at[where], result(where), land_plane.at[p], land_stack.at[p],
                mid.at[p], send.at[p], recv.at[p],
            ))
        return made

    lead_sums = sums(
        lead_x, lambda w: lead_res.at[w], lead_lp, lead_ls, lead_mid, lead_send, lead_recv
    )
    lg_sums = sums(
        lg_x, lambda w: lg_all.at[core, w], lg_lp, lg_ls, lg_mid, lg_send, lg_recv
    )
    gp_sum = Reduce(at, gp_x, gp_all.at[core], gp_lp, gp_ls, gp_mid, gp_send, gp_recv)

    lead_core_copy().wait()
    mine = lead_v[pl.ds(core * half, half)].astype(F32) + lead_core[...].astype(F32)
    lead_x[...] = mine.reshape(lead_x.shape).astype(BF16)
    for r in lead_sums:
        r.plane_send()

    def plan(hooks, index):
        for when, todo in hooks:
            @pl.when(index == when)
            def _():
                for step in todo:
                    step()

    def spec_copy(i):
        return remote(
            spec_stage.at[i, pl.ds(other * half, half)],
            spec.at[:, pl.ds(core * chan + i * STEP, STEP), :],
            spec_send.at[i], spec_recv.at[i], partner,
        )

    first_lead, last_lead = lead_sums[0], lead_sums[-1]
    first_lg, last_lg = lg_sums[0], lg_sums[-1]
    split = parts > 1

    def both_of(one, two):
        return [one] + ([two] if split else [])

    cot_hooks = [
        (min(1, subs - 1), [first_lead.plane_wait, first_lead.stack_send]),
        (min(2, subs - 1), [last_lead.plane_wait, last_lead.stack_send] if split else []),
        (min(3, subs - 1), [first_lead.stack_wait, first_lead.stack_back_send]),
    ]

    def cot_body(i, carry):
        product = rows_of_block(cot, i, i + subs)
        for c in range(sub):
            for q in range(2):
                y[q * n : (q + 1) * n, c * my : (c + 1) * my] = product[
                    c * n : (c + 1) * n, q * my : (q + 1) * my
                ]
        z = dot(csf[...], y[: 2 * n, : sub * my])
        for c in range(sub):
            held[c] = z[:, c * my : (c + 1) * my] * weight[:, :my]
        turned = jnp.swapaxes(held[...], 0, 1).astype(BF16)
        spec_stage[i, :, :, :my] = turned[:mx]
        spec_stage[i, :, :, my:] = turned[mx:]
        spec_copy(i).start()
        spec[:, pl.ds(pl.multiple_of(core * chan + i * STEP, STEP), STEP), :] = spec_stage[
            i, pl.ds(core * half, half)
        ]

        plan(cot_hooks, i)
        return carry

    lax.fori_loop(0, subs, cot_body, 0)
    for i in range(subs):
        spec_copy(i).wait()

    unroll = 4

    def back_body(j, carry):
        for u in range(unroll):
            k = j * unroll + u
            g = dot(by_ba[...], spec[k])
            re = jnp.zeros((ra, my), F32)
            im = jnp.zeros((ra, my), F32)
            for b in range(rb):
                gre = g[b * ra : (b + 1) * ra, :my]
                gim = g[b * ra : (b + 1) * ra, my:]
                kre, kim = kern[k, b : b + 1, :my], kern[k, b : b + 1, my:]
                re += gre * kre + gim * kim
                im += gim * kre - gre * kim
            lg_x[2 * k] = re.astype(BF16)
            lg_x[2 * k + 1] = im.astype(BF16)

        plan(back_hooks, j)
        return carry

    rounds = half // unroll
    back_hooks = []
    if split:
        back_hooks = [
            (rounds // 4, [last_lead.stack_wait, last_lead.stack_back_send]),
            (rounds // 2, [first_lg.plane_send]),
            (rounds * 3 // 4, [first_lead.stack_back_wait, first_lead.plane_back_send]),
        ]
    lax.fori_loop(0, rounds, back_body, 0)
    last_lg.plane_send()
    last_lead.stack_back_wait()
    last_lead.plane_back_send()
    part_second[...] = jnp.zeros_like(part_second)

    per = 2
    folded = outer.shape[1] != half // per

    def outer_put(j, a, lanes, value):
        row = a * rb
        if folded:
            lanes += row // (pairs // 2) * per * wide
            row %= pairs // 2
        outer[j // outer.shape[1], j % outer.shape[1], row : row + rb, lanes : lanes + my] = (
            value.astype(BF16)
        )

    def outer_get(j, lanes, size):
        slab = outer.at[j // outer.shape[1], j % outer.shape[1]]
        if not folded:
            return slab[:, lanes : lanes + size]
        low = slab[:, lanes : lanes + size]
        high = slab[:, per * wide + lanes : per * wide + lanes + size]
        return jnp.concatenate([low, high], axis=0)

    def mix_body(j, carry):
        for u in range(per):
            k = j * per + u
            g = dot(by_ab[...], spec[k])
            kr = kern[k]
            kre, kim = kr[:, :my], kr[:, my:]
            re = jnp.zeros((rb, my), F32)
            im = jnp.zeros((rb, my), F32)
            for a in range(ra):
                rows = slice(a * rb, (a + 1) * rb)
                lre, lim = lead_f[k, a : a + 1, :my], lead_f[k, a : a + 1, my:]
                outer_put(j, a, u * wide, kre * lre - kim * lim)
                outer_put(j, a, u * wide + my, kre * lim + kim * lre)
                gre, gim = g[rows, :my], g[rows, my:]
                re += gre * lre + gim * lim
                im += gim * lre - gre * lim
            at_k = pl.ds(pl.multiple_of(k * rb, rb), rb)
            kgrad[at_k, :my] = re
            kgrad[at_k, my:] = im
        rhs = jnp.concatenate([spec[j * per + u] for u in range(per)], axis=1)
        part_second[...] += dot_nt(outer_get(j, 0, per * wide), rhs)

        plan(mix_hooks, j)
        return carry

    turns_of_part = half // per // parts
    if split:
        mix_hooks = [
            (turns_of_part // 4, [first_lg.plane_wait, first_lg.stack_send]),
            (turns_of_part // 2, [last_lg.plane_wait, last_lg.stack_send]),
            (turns_of_part * 3 // 4, [first_lg.stack_wait, first_lg.stack_back_send]),
            (turns_of_part * 9 // 8, [last_lg.stack_wait, last_lg.stack_back_send]),
            (turns_of_part * 5 // 4, [first_lg.stack_back_wait, first_lg.plane_back_send]),
            (turns_of_part * 13 // 8, [last_lg.stack_back_wait, last_lg.plane_back_send]),
        ]
    else:
        mix_hooks = [
            (turns_of_part // 8, [last_lg.plane_wait, last_lg.stack_send]),
            (turns_of_part * 3 // 8, [last_lg.stack_wait, last_lg.stack_back_send]),
            (turns_of_part * 7 // 8, [last_lg.stack_back_wait, last_lg.plane_back_send]),
        ]
    for p in range(parts):
        share = half // parts
        lead_sums[p].plane_back_wait()
        where = pl.ds(p * 2 * share, 2 * share)
        got = lead_res[where].reshape(share, 2, ra, my).astype(F32)
        lead_f[p * share : (p + 1) * share, :, :my] = got[:, 0]
        lead_f[p * share : (p + 1) * share, :, my:] = got[:, 1]
        lax.fori_loop(p * turns_of_part, (p + 1) * turns_of_part, mix_body, 0)

    def second_copy():
        return remote(
            part_second.at[pl.ds(other * (pairs // 2), pairs // 2)], gp_core,
            core_send.at[1], core_recv.at[1], partner,
        )

    def back_copy():
        return remote(lg_all.at[core], lg_all.at[core], core_send.at[2], core_recv.at[2], partner)

    second_copy().start()
    by_mode = jnp.swapaxes(kgrad[...].reshape(half, rb, wide), 0, 1).reshape(rb * half, wide)
    part_third = dot_nt(col, by_mode, HI)
    third_flat = jnp.concatenate(
        [jnp.where(core == 0, third[b][:, :half], third[b][:, half:]) for b in range(rb)], axis=1
    )
    part_fourth = dot(third_flat, by_mode, HI)
    second_copy().wait()
    mine = part_second[pl.ds(core * (pairs // 2), pairs // 2)] + gp_core[...]
    mine = dot(mine, one_hot(both, channels, at.chan // 2 * both).astype(F32), HI)

    pieces = []
    for value in (mine, part_third, part_fourth):
        for c in range(value.shape[1] // LANES):
            pieces.append((value, c))
    spots, count = [], 0
    for value, c in pieces:
        tiles = value.shape[0] // 8
        gp_x[count : count + tiles] = value[:, c * LANES : (c + 1) * LANES].reshape(
            tiles, 8, LANES
        )
        spots.append((count, tiles))
        count += tiles
    if count < gp_x.shape[0]:
        gp_x[count:] = jnp.zeros((gp_x.shape[0] - count, 8, LANES), F32)
    gp_sum.plane_send()
    for r in lg_sums:
        r.plane_back_wait()
    back_copy().start()

    back_copy().wait()
    for q in range(2):
        for h in range(2):
            got = lg_all[h].reshape(half, 2, ra, my)[:, q].astype(F32)
            turned = jnp.swapaxes(got, 0, 1).astype(BF16)
            for a in range(ra):
                back_in[
                    q * mx + h * half : q * mx + (h + 1) * half, a * my : (a + 1) * my
                ] = turned[a]
    r = dot(csb[...], back_in[...]).astype(BF16)
    for a in range(ra):
        for q in range(2):
            back_rows[a, :, q * my : (q + 1) * my] = r[
                q * n : (q + 1) * n, a * my : (a + 1) * my
            ]
    total[...] = jnp.zeros_like(total)

    def first_body(i, carry):
        row = pl.ds(pl.multiple_of(i * STEP, STEP), STEP)
        block = back_rows[:, row, :].reshape(ra * STEP, wide)
        total[...] += dot_nt(modes_v[:, row, :].reshape(chan * STEP, wide), block)
        return carry

    lax.fori_loop(0, n // STEP, first_body, 0)
    shape = (STEP, ra * STEP)
    unit = lax.broadcasted_iota(jnp.int32, shape, 1) % STEP == lax.broadcasted_iota(
        jnp.int32, shape, 0
    )
    kept = total[...].reshape(chan, STEP, ra * STEP) * unit.astype(F32)[None]
    lane_f = lax.broadcasted_iota(jnp.int32, (ra, ra * STEP), 1)
    row_f = lax.broadcasted_iota(jnp.int32, (ra, ra * STEP), 0)
    pick = (lane_f // STEP == row_f).astype(F32)
    part_first = dot_nt(pick, jnp.sum(kept, axis=1), HI)
    f_core[core] = dot(part_first, one_hot(chan, channels, at.chan * chan).astype(F32), HI)

    def first_core_copy():
        return remote(f_core.at[core], f_core.at[core], core_send.at[3], core_recv.at[3], partner)

    def first_plane_copy(s):
        return remote(
            f_plane.at[at.plane], f_plane.at[at.plane],
            f_send.at[0, s - 1], f_recv.at[0, s - 1], at.across_plane(s),
        )

    def first_stack_copy(s):
        return remote(
            f_stack.at[at.stack], f_stack.at[at.stack],
            f_send.at[1, s - 1], f_recv.at[1, s - 1], at.across_stack(s),
        )

    def first_plane():
        first_core_copy().wait()
        f_plane[at.plane] = f_core[0] + f_core[1]
        for s in range(1, at.planes):
            first_plane_copy(s).start()

    def first_stack():
        for s in range(1, at.planes):
            first_plane_copy(s).wait()
        value = f_plane[0]
        for s in range(1, at.planes):
            value = value + f_plane[s]
        f_stack[at.stack] = value
        for s in range(1, at.stacks):
            first_stack_copy(s).start()

    first_core_copy().start()
    gp_sum.plane_wait()
    gp_sum.stack_send()

    def out_copy(g):
        return remote(
            s_stage.at[g, :, :, pl.ds(other * chan * my, chan * my)],
            spec_out.at[:, pl.ds(core * half + g * STEP, STEP), :],
            out_send.at[g], out_recv.at[g], partner,
        )

    def out_body(g, carry):
        for j in range(STEP // per):
            for u in range(per):
                held_o[j * per + u, :both] = dot(
                    by_t[...], outer_get(g * (STEP // per) + j, u * wide, wide)
                )
        turned = jnp.swapaxes(held_o[:, :both], 0, 1).astype(BF16)
        for o in range(both):
            for q in range(2):
                s_stage[g, q, :, o * my : (o + 1) * my] = turned[o, :, q * my : (q + 1) * my]
        out_copy(g).start()
        row = pl.ds(pl.multiple_of(core * half + g * STEP, STEP), STEP)
        lanes = pl.ds(pl.multiple_of(core * chan * my, chan * my), chan * my)
        spec_out[:, row, :] = s_stage[g, :, :, lanes]

        @pl.when(g == 0)
        def _():
            first_plane()

        @pl.when(g == 2)
        def _():
            gp_sum.stack_wait()
            gp_sum.stack_back_send()
            first_stack()

        return carry

    groups = half // STEP
    lax.fori_loop(0, groups, out_body, 0)
    for g in range(groups):
        out_copy(g).wait()

    turns = 8

    def rows_copy(i):
        where = pl.ds(i * turns, turns)
        return pltpu.make_async_copy(modes_v.at[where], rows_out.at[where], rows_sem.at[i])

    def rows_body(i, carry):
        lanes = pl.ds(pl.multiple_of(i * turns * my, turns * my), turns * my)
        r = dot(csb[...], spec_out[:, :, lanes].reshape(2 * mx, turns * my))
        for c in range(turns):
            for q in range(2):
                part = r[q * n : (q + 1) * n, c * my : (c + 1) * my] * weight[:, :my]
                modes_v[i * turns + c, :, q * my : (q + 1) * my] = part.astype(BF16)
        rows_copy(i).start()

        @pl.when(i == 0)
        def _():
            gp_sum.stack_back_wait()
            gp_sum.plane_back_send()

        return carry

    steps = chan // turns
    lax.fori_loop(0, steps, rows_body, 0)
    for s in range(1, at.stacks):
        first_stack_copy(s).wait()
    value = f_stack[0]
    for s in range(1, at.stacks):
        value = value + f_stack[s]
    g_first[...] = value * (1.0 / (side * mx))
    gp_sum.plane_back_wait()

    def grads_copy():
        return remote(gp_all.at[core], gp_all.at[core], core_send.at[4], core_recv.at[4], partner)

    grads_copy().start()
    grads_copy().wait()

    def tile(h, index):
        start, size = spots[index]
        return gp_all[h, start : start + size].reshape(size * 8, LANES) * (1.0 / mx)

    cols = channels // LANES
    for h in range(2):
        for c in range(cols):
            g_second[
                h * (pairs // 2) : (h + 1) * (pairs // 2), c * LANES : (c + 1) * LANES
            ] = tile(h, c)
    low = lax.broadcasted_iota(jnp.int32, (rd, LANES), 1) < half
    for j in range(rb // 2):
        t0, t1 = tile(0, cols + j), tile(1, cols + j)
        g_third[2 * j] = jnp.where(low, t0, pltpu.roll(t1, half, 1))
        g_third[2 * j + 1] = jnp.where(low, pltpu.roll(t0, half, 1), t1)
    for q in range(2):
        g_fourth[q] = tile(0, cols + rb // 2 + q) + tile(1, cols + rb // 2 + q)
    for i in range(steps):
        rows_copy(i).wait()


def output_kernel(
    first_t, table_in, rows_in, back_in, *refs
):
    grads_in, (out, out_back), grads_out = refs[:4], refs[4:6], refs[6:10]
    table, rows, back, out_v, back_v, kron = refs[10:16]
    grads, (in_sem, rows_sem, grad_sem, out_sem, back_sem) = refs[16:20], refs[20:]
    chan, n, side = out.shape
    rank, _, wide = back.shape
    slots, block = out_v.shape[:2]
    steps, row_steps = chan // block, n // STEP
    back_slots = back_v.shape[0]

    def rows_copy(i):
        where = pl.ds(i * block, block)
        return pltpu.make_async_copy(rows_in.at[where], rows.at[where], rows_sem.at[i])

    table_copy = pltpu.make_async_copy(table_in, table, in_sem.at[0])
    back_copy = pltpu.make_async_copy(back_in, back, in_sem.at[1])
    table_copy.start()
    for i in range(steps):
        rows_copy(i).start()
    back_copy.start()
    for i in range(4):
        pltpu.make_async_copy(grads_in[i], grads[i], grad_sem.at[0, i]).start()
    pick = one_hot(chan, first_t.shape[1], lax.axis_index("chan") * chan).astype(BF16)
    first = dot_nt(pick, first_t[...].astype(BF16)).astype(BF16)
    kron[...] = spread(first, chan, rank)

    def out_copy(i):
        slot = lax.rem(i, slots)
        return pltpu.make_async_copy(
            out_v.at[slot], out.at[pl.ds(i * block, block)], out_sem.at[slot]
        )

    def out_body(i, carry):
        rows_copy(i).wait()

        @pl.when(i >= slots)
        def _():
            out_copy(i - slots).wait()

        product = dot(rows[pl.ds(i * block, block)].reshape(block * n, wide), table[...])
        out_v[lax.rem(i, slots)] = product.astype(BF16).reshape(block, n, side)
        out_copy(i).start()
        return carry

    def in_copy(i):
        slot = lax.rem(i, back_slots)
        return pltpu.make_async_copy(
            back_v.at[slot],
            out_back.at[:, pl.ds(pl.multiple_of(i * STEP, STEP), STEP), :],
            back_sem.at[slot],
        )

    def in_body(i, carry):
        @pl.when(i >= back_slots)
        def _():
            in_copy(i - back_slots).wait()

        part = back[:, pl.ds(pl.multiple_of(i * STEP, STEP), STEP), :].reshape(rank * STEP, wide)
        mid = (dot(kron[...], part) * (1.0 / side)).astype(BF16)
        product = dot(mid, table[...])
        back_v[lax.rem(i, back_slots)] = product.astype(BF16).reshape(chan, STEP, side)
        in_copy(i).start()
        return carry

    table_copy.wait()
    lax.fori_loop(0, steps, out_body, 0)
    back_copy.wait()
    for i in range(4):
        pltpu.make_async_copy(grads_in[i], grads[i], grad_sem.at[0, i]).wait()
        pltpu.make_async_copy(grads[i], grads_out[i], grad_sem.at[1, i]).start()
    lax.fori_loop(0, row_steps, in_body, 0)
    for i in range(max(steps - slots, 0), steps):
        out_copy(jnp.int32(i)).wait()
    for i in range(max(row_steps - back_slots, 0), row_steps):
        in_copy(jnp.int32(i)).wait()
    for i in range(4):
        pltpu.make_async_copy(grads[i], grads_out[i], grad_sem.at[1, i]).wait()


def local(input_field, out_cotangent, core_first, core_second, core_third, column_mode_core):
    grid_count, chan_count = lax.axis_size("grid"), lax.axis_size("chan")
    chan_index = lax.axis_index("chan")
    chan, rows, side = input_field.shape
    channels, rank_a = core_first.shape
    rank_b, modes_x, rank_d = core_third.shape
    modes_y = column_mode_core.shape[2]
    wide = 2 * modes_y
    half = modes_x // 2
    both = 2 * chan
    pairs = rank_a * rank_b

    table_np = width_table(side, modes_y)
    table = jnp.asarray(table_np)
    table_t = jnp.asarray(np.ascontiguousarray(table_np.T))
    turns = turn_table(side, modes_x).reshape(2, modes_x, grid_count, rows)
    turns = jnp.asarray(np.ascontiguousarray(turns.transpose(2, 0, 1, 3)))

    first_t = core_first.T
    second = core_second.transpose(0, 2, 1).reshape(pairs, channels)
    if both % LANES:
        second = lax.dynamic_slice_in_dim(second, chan_index // 2 * both, both, 1)
    third = core_third.transpose(0, 2, 1)
    anywhere = pl.BlockSpec(memory_space=pl.ANY)

    row_steps = rows // STEP
    planes, stacks = chan_count, grid_count // 2
    tiles = 2 * half
    owners = planes * stacks
    grad_tiles = (pairs // 2 * channels + rank_d * rank_b * half + rank_d * wide) // (8 * LANES)
    grad_tiles += -grad_tiles % owners
    sub = STEP
    subs = chan // sub
    slots = min(SLOTS, 2 * subs)
    blocks = subs
    fold = rows == pairs // 2 and side == 4 * wide and slots * sub >= half // 2
    outer_shape = (1, 1, 16, LANES) if fold else (1, half // 2, pairs, 2 * wide)
    parts = 2 if tiles % (2 * owners) == 0 else 1
    row_groups = rows // STEP
    wide_y = max(sub * modes_y, row_groups * wide)
    groups = half // STEP
    peers = max(planes, stacks) - 1
    steps = chan // 8

    def reduce_buffers(count, shape, dtype, lead=()):
        chunk = count // planes
        return [
            pltpu.VMEM((*lead, planes - 1, chunk, *shape), dtype),
            pltpu.VMEM((*lead, stacks - 1, chunk // stacks, *shape), dtype),
            pltpu.VMEM((*lead, chunk, *shape), dtype),
        ]

    tile = (rank_a, modes_y)
    scratch = [
        pltpu.VMEM((slots, sub, rows, side), BF16),
        pltpu.VMEM((chan, rows, wide), BF16),
        pltpu.VMEM((max(2 * rows, sub * STEP), wide_y), BF16),
        pltpu.VMEM((STEP, 2 * modes_x, modes_y), F32),
        pltpu.VMEM((blocks, modes_x, STEP, wide), BF16),
        pltpu.VMEM((half, both, wide), BF16),
        pltpu.VMEM((groups, 2, STEP, both * modes_y), BF16),
        pltpu.VMEM((2, modes_x, chan * modes_y), BF16),
        pltpu.VMEM((2, modes_x, rows), BF16),
        pltpu.VMEM((2 * modes_x, 2 * rows), BF16),
        pltpu.VMEM((2 * rows, 2 * modes_x), BF16),
        pltpu.VMEM((rank_a * STEP, chan * STEP), BF16),
        pltpu.VMEM((rank_a * STEP, row_groups * wide), F32),
        pltpu.VMEM((pairs, both), BF16),
        pltpu.VMEM((pairs, both), BF16),
        pltpu.VMEM((both, pairs), BF16),
        pltpu.VMEM((half, rank_b, wide), F32),
        pltpu.VMEM((half, rank_a, wide), F32),
        pltpu.VMEM((half * rank_b, wide), F32),
        pltpu.VMEM(outer_shape, BF16),
        pltpu.VMEM((STEP, max(both, modes_x), wide), F32),
        pltpu.VMEM((pairs, both), F32),
        pltpu.VMEM((2 * modes_x, rank_a * modes_y), BF16),
        pltpu.VMEM((chan * STEP, rank_a * STEP), F32),
        pltpu.VMEM((modes_x, 2, *tile), BF16),
        pltpu.VMEM((half, 2, *tile), BF16),
        pltpu.VMEM((tiles, *tile), BF16),
        pltpu.VMEM((tiles, *tile), BF16),
        *reduce_buffers(tiles // parts, tile, BF16, (parts,)),
        pltpu.VMEM((tiles, *tile), BF16),
        pltpu.VMEM((2, tiles, *tile), BF16),
        *reduce_buffers(tiles // parts, tile, BF16, (parts,)),
        pltpu.VMEM((pairs // 2, both), F32),
        pltpu.VMEM((grad_tiles, 8, LANES), F32),
        pltpu.VMEM((2, grad_tiles, 8, LANES), F32),
        *reduce_buffers(grad_tiles, (8, LANES), F32),
        pltpu.VMEM((2, rank_a, channels), F32),
        pltpu.VMEM((planes, rank_a, channels), F32),
        pltpu.VMEM((stacks, rank_a, channels), F32),
        *[pltpu.SemaphoreType.DMA((parts, 4, peers))] * 4,
        *[pltpu.SemaphoreType.DMA((4, peers))] * 2,
        *[pltpu.SemaphoreType.DMA((5,))] * 2,
        *[pltpu.SemaphoreType.DMA((blocks,))] * 2,
        *[pltpu.SemaphoreType.DMA((groups,))] * 2,
        *[pltpu.SemaphoreType.DMA((2, peers))] * 2,
        pltpu.SemaphoreType.DMA((slots,)),
        pltpu.SemaphoreType.DMA,
        pltpu.SemaphoreType.DMA((steps,)),
    ]
    vmem = pl.BlockSpec(memory_space=pltpu.VMEM)
    out_rows, back_rows, g_first, g_second, g_third, g_fourth = pl.pallas_call(
        spectral_kernel,
        in_specs=[anywhere] * 3 + [vmem] * 5,
        out_specs=[anywhere] + [vmem] * 5,
        out_shape=[
            jax.ShapeDtypeStruct((chan, rows, wide), BF16),
            jax.ShapeDtypeStruct((rank_a, rows, wide), BF16),
            jax.ShapeDtypeStruct((rank_a, channels), F32),
            jax.ShapeDtypeStruct((pairs, channels), F32),
            jax.ShapeDtypeStruct((rank_b, rank_d, modes_x), F32),
            jax.ShapeDtypeStruct((2, rank_d, modes_y), F32),
        ],
        scratch_shapes=scratch,
        compiler_params=pltpu.CompilerParams(
            collective_id=0, has_side_effects=True, vmem_limit_bytes=63 * 2**20
        ),
        name="spectral",
    )(input_field, out_cotangent, turns, table, first_t, second, third, column_mode_core)

    out_step = min(chan, 8)
    out_steps = chan // out_step
    out_slots, back_slots = min(4, out_steps), min(4, row_steps)
    grads = [
        (rank_a, channels), (pairs, channels), (rank_b, rank_d, modes_x), (2, rank_d, modes_y)
    ]
    output_field, input_grad, g_first, g_second, g_third, g_fourth = pl.pallas_call(
        output_kernel,
        in_specs=[vmem] + [anywhere] * 7,
        out_specs=[anywhere] * 6,
        out_shape=[
            jax.ShapeDtypeStruct((chan, rows, side), BF16),
            jax.ShapeDtypeStruct((chan, rows, side), BF16),
            *[jax.ShapeDtypeStruct(shape, F32) for shape in grads],
        ],
        scratch_shapes=[
            pltpu.VMEM((wide, side), BF16),
            pltpu.VMEM((chan, rows, wide), BF16),
            pltpu.VMEM((rank_a, rows, wide), BF16),
            pltpu.VMEM((out_slots, out_step, rows, side), BF16),
            pltpu.VMEM((back_slots, chan, STEP, side), BF16),
            pltpu.VMEM((chan * STEP, rank_a * STEP), BF16),
            *[pltpu.VMEM(shape, F32) for shape in grads],
            pltpu.SemaphoreType.DMA((2,)),
            pltpu.SemaphoreType.DMA((out_steps,)),
            pltpu.SemaphoreType.DMA((2, 4)),
            pltpu.SemaphoreType.DMA((out_slots,)),
            pltpu.SemaphoreType.DMA((back_slots,)),
        ],
        compiler_params=params(60),
        name="output",
    )(first_t, table_t, out_rows, back_rows, g_first, g_second, g_third, g_fourth)

    return (
        output_field,
        input_grad,
        g_first.T,
        g_second.reshape(rank_a, rank_b, channels).transpose(0, 2, 1),
        g_third.transpose(0, 2, 1),
        g_fourth,
    )


def solution(mesh):
    placed = (P("chan", "grid", None), P("chan", "grid", None), P(), P(), P(), P())
    return jax.shard_map(
        local,
        mesh=mesh,
        in_specs=placed,
        out_specs=(P("chan", "grid", None), P("chan", "grid", None), P(), P(), P(), P()),
        check_vma=False,
    )
```

```python
import math

import jax
import jax.numpy as jnp
import numpy as np
from jax import lax
from jax.experimental import pallas as pl
from jax.experimental.pallas import tpu as pltpu
from jax.sharding import PartitionSpec as P

F32 = jnp.float32
BF16 = jnp.bfloat16
HI = lax.Precision.HIGHEST
STEP = 16
LANES = 128
SLOTS = 3
MESH = pl.DeviceIdType.MESH


def params(mib=48):
    return pltpu.CompilerParams(vmem_limit_bytes=mib * 2**20)


def dot(a, b, precision=None):
    return jnp.dot(a, b, preferred_element_type=F32, precision=precision)


def dot_nt(a, b, precision=None):
    return lax.dot_general(
        a, b, (((1,), (1,)), ((), ())), preferred_element_type=F32, precision=precision
    )


def dot_tn(a, b, precision=None):
    return lax.dot_general(
        a, b, (((0,), (0,)), ((), ())), preferred_element_type=F32, precision=precision
    )


def width_table(side, modes_y):
    phase = np.arange(side)[:, None] * np.arange(modes_y)[None, :] % side
    angle = phase.astype(np.float32) * np.float32(2.0 * math.pi / side)
    return np.concatenate([np.cos(angle), -np.sin(angle)], axis=1).astype(BF16)


def turn_table(side, modes_x):
    kx = np.arange(modes_x)
    freq = np.where(kx < modes_x // 2, kx, side - modes_x + kx)
    phase = freq[:, None] * np.arange(side)[None, :] % side
    angle = phase.astype(np.float32) * np.float32(2.0 * math.pi / side)
    return np.stack([np.cos(angle), np.sin(angle)]).astype(BF16)


def one_hot(rows, cols, offset):
    row = lax.broadcasted_iota(jnp.int32, (rows, cols), 0)
    col = lax.broadcasted_iota(jnp.int32, (rows, cols), 1)
    return col == row + offset


def spread(values, rows, n, offset=0):
    lane = lax.broadcasted_iota(jnp.int32, (values.shape[1], n * STEP), 1)
    row = lax.broadcasted_iota(jnp.int32, (values.shape[1], n * STEP), 0)
    wide = dot(values, (lane // STEP + offset == row).astype(BF16))
    at = lax.broadcasted_iota(jnp.int32, (STEP, n * STEP), 1) % STEP
    unit = (at == lax.broadcasted_iota(jnp.int32, (STEP, n * STEP), 0)).astype(F32)
    return (wide[:, None, :] * unit[None]).reshape(rows * STEP, n * STEP).astype(BF16)


def flip(index, bits):
    bit = 1
    while bit <= bits:
        if bits & bit:
            index = index + bit * (1 - 2 * (index // bit % 2))
        bit *= 2
    return index


class Place:
    def __init__(self):
        self.grid, self.chan = lax.axis_index("grid"), lax.axis_index("chan")
        self.core = self.chan % 2
        self.planes = lax.axis_size("chan")
        self.stacks = lax.axis_size("grid") // 2
        self.plane = self.chan // 2 * 2 + self.grid % 2
        self.stack = self.grid // 2

    def across_core(self):
        return {"grid": self.grid, "chan": flip(self.chan, 1)}

    def across_plane(self, s):
        return {"grid": flip(self.grid, s % 2), "chan": flip(self.chan, s // 2 * 2)}

    def across_stack(self, s):
        return {"grid": flip(self.grid, s * 2), "chan": self.chan}

    def peers(self):
        return (
            [self.across_core()]
            + [self.across_plane(s) for s in range(1, self.planes)]
            + [self.across_stack(s) for s in range(1, self.stacks)]
        )


def remote(src, dst, send, recv, peer):
    return pltpu.make_async_remote_copy(
        src_ref=src, dst_ref=dst, send_sem=send, recv_sem=recv,
        device_id=peer, device_id_type=MESH,
    )


class Reduce:
    def __init__(self, place, source, result, land_plane, land_stack, mid, send, recv):
        self.at, self.source, self.result = place, source, result
        self.land_plane, self.land_stack, self.mid = land_plane, land_stack, mid
        self.send, self.recv = send, recv
        self.chunk = source.shape[0] // place.planes
        self.piece = self.chunk // place.stacks

    def plane_copy(self, s):
        there = flip(self.at.plane, s)
        return remote(
            self.source.at[pl.ds(there * self.chunk, self.chunk)],
            self.land_plane.at[s - 1],
            self.send.at[0, s - 1], self.recv.at[0, s - 1], self.at.across_plane(s),
        )

    def plane_send(self):
        for s in range(1, self.at.planes):
            self.plane_copy(s).start()

    def plane_wait(self):
        for s in range(1, self.at.planes):
            self.plane_copy(s).wait()
        total = self.source[pl.ds(self.at.plane * self.chunk, self.chunk)].astype(F32)
        for s in range(1, self.at.planes):
            total = total + self.land_plane[s - 1].astype(F32)
        self.mid[...] = total.astype(self.mid.dtype)

    def stack_copy(self, s):
        there = flip(self.at.stack, s)
        return remote(
            self.mid.at[pl.ds(there * self.piece, self.piece)],
            self.land_stack.at[s - 1],
            self.send.at[1, s - 1], self.recv.at[1, s - 1], self.at.across_stack(s),
        )

    def stack_send(self):
        for s in range(1, self.at.stacks):
            self.stack_copy(s).start()

    def own(self):
        return pl.ds(self.at.plane * self.chunk + self.at.stack * self.piece, self.piece)

    def stack_wait(self):
        for s in range(1, self.at.stacks):
            self.stack_copy(s).wait()
        total = self.mid[pl.ds(self.at.stack * self.piece, self.piece)].astype(F32)
        for s in range(1, self.at.stacks):
            total = total + self.land_stack[s - 1].astype(F32)
        self.result[self.own()] = total.astype(self.result.dtype)

    def stack_back_copy(self, s):
        return remote(
            self.result.at[self.own()], self.result.at[self.own()],
            self.send.at[2, s - 1], self.recv.at[2, s - 1], self.at.across_stack(s),
        )

    def stack_back_send(self):
        for s in range(1, self.at.stacks):
            self.stack_back_copy(s).start()

    def stack_back_wait(self):
        for s in range(1, self.at.stacks):
            self.stack_back_copy(s).wait()

    def plane_back_copy(self, s):
        here = pl.ds(self.at.plane * self.chunk, self.chunk)
        return remote(
            self.result.at[here], self.result.at[here],
            self.send.at[3, s - 1], self.recv.at[3, s - 1], self.at.across_plane(s),
        )

    def plane_back_send(self):
        for s in range(1, self.at.planes):
            self.plane_back_copy(s).start()

    def plane_back_wait(self):
        for s in range(1, self.at.planes):
            self.plane_back_copy(s).wait()


def spectral_kernel(
    field, cot, turns_in, table_in, first_t, second, third, column,
    rows_out, back_out, kron_out, g_first, g_second, g_third, g_fourth,
    block_v, kron_back, table, back_rows, outer_a, outer_b, modes_v, y, held, spec_stage, spec, s_stage, spec_out, cs, csf, csb, kron, mixed,
    by_ab, by_ba, by_t, kern, lead_f, kgrad, outer, held_o, part_second, back_in, total,
    lead_v, lead_core, lead_x, lead_res, lead_lp, lead_ls, lead_mid,
    lg_x, lg_all, lg_lp, lg_ls, lg_mid,
    gp_core, gp_x, gp_all, gp_lp, gp_ls, gp_mid,
    f_core, f_plane, f_stack,
    lead_send, lead_recv, lg_send, lg_recv, gp_send, gp_recv,
    core_send, core_recv, spec_send, spec_recv, out_send, out_recv, f_send, f_recv,
    block_sem, turns_sem, rows_sem, wide_sem,
):
    if outer.shape[0] * outer.shape[1] * 2 < kern.shape[0]:
        outer = block_v
    at = Place()
    core = at.core
    other = 1 - core
    chan, n, side = cot.shape
    wide = table.shape[1]
    my = wide // 2
    mx = cs.shape[1]
    half = mx // 2
    ra, rb, rd = first_t.shape[0], third.shape[0], third.shape[1]
    pairs = ra * rb
    both = 2 * chan
    channels = g_first.shape[1]
    slots, sub = block_v.shape[:2]
    subs = chan // sub
    parts = lead_lp.shape[0]
    row_groups = n // STEP
    lane = lax.broadcasted_iota(jnp.int32, (1, wide), 1)
    weight = jnp.where(lane % my == 0, 1.0, 2.0) * (1.0 / side)
    partner = at.across_core()

    def block_copy(source, j, k):
        slot = lax.rem(k, slots)
        return pltpu.make_async_copy(
            source.at[pl.ds(j * sub, sub)], block_v.at[slot], block_sem.at[slot]
        )

    def fetch(k):
        @pl.when(k < subs)
        def _():
            block_copy(field, k, k).start()

        @pl.when(jnp.logical_and(k >= subs, k < 2 * subs))
        def _():
            block_copy(cot, k - subs, k).start()

    def rows_of_block(source, j, k):
        block_copy(source, j, k).wait()
        block = block_v[lax.rem(k, slots)].reshape(sub * n, side)
        product = dot(block, table[...]).astype(BF16)
        fetch(k + slots)
        return product

    barrier = pltpu.get_barrier_semaphore()
    peers = at.peers()
    for peer in peers:
        pl.semaphore_signal(barrier, inc=1, device_id=peer, device_id_type=MESH)
    table_copy = pltpu.make_async_copy(table_in, table, turns_sem.at[1])
    table_copy.start()
    for k in range(min(slots, 2 * subs)):
        if k < subs:
            block_copy(field, k, k).start()
        else:
            block_copy(cot, k - subs, k).start()
    turns_copy = pltpu.make_async_copy(turns_in.at[at.grid], cs, turns_sem.at[0])
    turns_copy.start()
    kron[...] = spread(first_t[...].astype(BF16), ra, chan, at.chan * chan)
    table_copy.wait()

    mixed[...] = jnp.zeros_like(mixed)

    def field_body(i, carry):
        product = rows_of_block(field, i, i)
        shaped = product.reshape(sub, n, wide)
        modes_v[pl.ds(i * sub, sub)] = shaped
        for g in range(row_groups):
            y[: sub * STEP, g * wide : (g + 1) * wide] = shaped[
                :, g * STEP : (g + 1) * STEP
            ].reshape(sub * STEP, wide)
        part = pl.ds(pl.multiple_of(i * sub * STEP, sub * STEP), sub * STEP)
        mixed[...] += dot(kron[:, part], y[: sub * STEP, : row_groups * wide])
        return carry

    lax.fori_loop(0, subs, field_body, 0)
    turns_copy.wait()
    c, s = cs[0], cs[1]
    csf[:mx, :n], csf[:mx, n:], csf[mx:, :n], csf[mx:, n:] = c, s, -s, c
    ct = jnp.swapaxes(c.astype(F32), 0, 1).astype(BF16)
    st = jnp.swapaxes(s.astype(F32), 0, 1).astype(BF16)
    csb[:n, :mx], csb[:n, mx:], csb[n:, :mx], csb[n:, mx:] = ct, -st, st, ct
    for g in range(row_groups):
        for q in range(2):
            for a in range(ra):
                back_in[q * n + g * STEP : q * n + (g + 1) * STEP, a * my : (a + 1) * my] = mixed[
                    a * STEP : (a + 1) * STEP, g * wide + q * my : g * wide + (q + 1) * my
                ].astype(BF16)
    z = dot(csf[...], back_in[: 2 * n]) * (1.0 / side)
    for a in range(ra):
        held[a] = z[:, a * my : (a + 1) * my]
    turned = jnp.swapaxes(held[...], 0, 1).astype(BF16)
    lead_v[:, 0] = turned[:mx]
    lead_v[:, 1] = turned[mx:]

    def lead_core_copy():
        return remote(
            lead_v.at[pl.ds(other * half, half)], lead_core,
            core_send.at[0], core_recv.at[0], partner,
        )

    pl.semaphore_wait(barrier, len(peers))
    lead_core_copy().start()

    if second.shape[1] > both and both % LANES == 0:
        sec = second[:, pl.ds(pl.multiple_of(at.chan // 2 * both, both), both)]
    else:
        sec = second[...]
    by_ab[...] = sec.astype(BF16)
    by_ba[...] = jnp.swapaxes(sec.reshape(ra, rb, both), 0, 1).reshape(pairs, both).astype(BF16)
    by_t[...] = jnp.swapaxes(sec, 0, 1).astype(BF16)
    col = jnp.concatenate([column[0], column[1]], axis=1)
    for b in range(rb):
        held_o[b, :mx] = dot_tn(third[b], col, HI)
    own_half = pl.ds(pl.multiple_of(core * half, half), half)
    kern[...] = jnp.swapaxes(held_o[:, own_half, :], 0, 1)

    def sums(source, result, land_plane, land_stack, mid, send, recv):
        share = source.shape[0] // parts
        made = []
        for p in range(parts):
            where = pl.ds(p * share, share)
            made.append(Reduce(
                at, source.at[where], result(where), land_plane.at[p], land_stack.at[p],
                mid.at[p], send.at[p], recv.at[p],
            ))
        return made

    lead_sums = sums(
        lead_x, lambda w: lead_res.at[w], lead_lp, lead_ls, lead_mid, lead_send, lead_recv
    )
    lg_sums = sums(
        lg_x, lambda w: lg_all.at[core, w], lg_lp, lg_ls, lg_mid, lg_send, lg_recv
    )
    gp_sum = Reduce(at, gp_x, gp_all.at[core], gp_lp, gp_ls, gp_mid, gp_send, gp_recv)

    lead_core_copy().wait()
    mine = lead_v[pl.ds(core * half, half)].astype(F32) + lead_core[...].astype(F32)
    lead_x[...] = mine.reshape(lead_x.shape).astype(BF16)
    lead_sums[0].plane_send()

    def plan(hooks, index):
        for when, todo in hooks:
            @pl.when(index == when)
            def _():
                for step in todo:
                    step()

    def spec_copy(i):
        return remote(
            spec_stage.at[i, pl.ds(other * half, half)],
            spec.at[:, pl.ds(core * chan + i * STEP, STEP), :],
            spec_send.at[i], spec_recv.at[i], partner,
        )

    first_lead, last_lead = lead_sums[0], lead_sums[-1]
    first_lg, last_lg = lg_sums[0], lg_sums[-1]
    split = parts > 1

    def both_of(one, two):
        return [one] + ([two] if split else [])

    cot_hooks = [
        (
            min(1, subs - 1),
            [first_lead.plane_wait, first_lead.stack_send]
            + ([last_lead.plane_send] if split else []),
        ),
        (
            min(3, subs - 1),
            [first_lead.stack_wait, first_lead.stack_back_send]
            + ([last_lead.plane_wait, last_lead.stack_send] if split else []),
        ),
    ]

    def cot_body(i, carry):
        product = rows_of_block(cot, i, i + subs)
        for c in range(sub):
            for q in range(2):
                y[q * n : (q + 1) * n, c * my : (c + 1) * my] = product[
                    c * n : (c + 1) * n, q * my : (q + 1) * my
                ]
        z = dot(csf[...], y[: 2 * n, : sub * my])
        for c in range(sub):
            held[c] = z[:, c * my : (c + 1) * my] * weight[:, :my]
        turned = jnp.swapaxes(held[...], 0, 1).astype(BF16)
        spec_stage[i, :, :, :my] = turned[:mx]
        spec_stage[i, :, :, my:] = turned[mx:]
        spec_copy(i).start()
        spec[:, pl.ds(pl.multiple_of(core * chan + i * STEP, STEP), STEP), :] = spec_stage[
            i, pl.ds(core * half, half)
        ]

        plan(cot_hooks, i)
        return carry

    lax.fori_loop(0, subs, cot_body, 0)
    for i in range(subs):
        spec_copy(i).wait()

    unroll = 4

    def back_body(j, carry):
        for u in range(unroll):
            k = j * unroll + u
            g = dot(by_ba[...], spec[k])
            re = jnp.zeros((ra, my), F32)
            im = jnp.zeros((ra, my), F32)
            for b in range(rb):
                gre = g[b * ra : (b + 1) * ra, :my]
                gim = g[b * ra : (b + 1) * ra, my:]
                kre, kim = kern[k, b : b + 1, :my], kern[k, b : b + 1, my:]
                re += gre * kre + gim * kim
                im += gim * kre - gre * kim
            lg_x[2 * k] = re.astype(BF16)
            lg_x[2 * k + 1] = im.astype(BF16)

        plan(back_hooks, j)
        return carry

    rounds = half // unroll
    back_hooks = []
    if split:
        back_hooks = [
            (
                rounds * 11 // 16,
                [
                    first_lead.stack_back_wait, first_lead.plane_back_send,
                    last_lead.stack_wait, last_lead.stack_back_send, first_lg.plane_send,
                ],
            ),
        ]
    lax.fori_loop(0, rounds, back_body, 0)
    last_lg.plane_send()
    last_lead.stack_back_wait()
    last_lead.plane_back_send()
    part_second[...] = jnp.zeros_like(part_second)

    per = 2
    folded = outer.shape[1] != half // per

    def outer_put(j, a, lanes, value):
        row = a * rb
        if folded:
            lanes += row // (pairs // 2) * per * wide
            row %= pairs // 2
        outer[j // outer.shape[1], j % outer.shape[1], row : row + rb, lanes : lanes + my] = value

    def outer_get(j, lanes, size):
        slab = outer.at[j // outer.shape[1], j % outer.shape[1]]
        if not folded:
            return slab[:, lanes : lanes + size]
        low = slab[:, lanes : lanes + size]
        high = slab[:, per * wide + lanes : per * wide + lanes + size]
        return jnp.concatenate([low, high], axis=0)

    outer_b[...] = jnp.zeros_like(outer_b)

    def add_second(kept, j):
        rhs = jnp.concatenate([spec[j * per + u] for u in range(per)], axis=1)
        part_second[...] += dot_nt(kept[...], rhs)

    def products(j, kept):
        for u in range(per):
            k = j * per + u
            g = dot(by_ab[...], spec[k])
            kr = kern[k]
            kre, kim = kr[:, :my], kr[:, my:]
            re = jnp.zeros((rb, my), F32)
            im = jnp.zeros((rb, my), F32)
            for a in range(ra):
                rows = slice(a * rb, (a + 1) * rb)
                lre, lim = lead_f[k, a : a + 1, :my], lead_f[k, a : a + 1, my:]
                ore = (kre * lre - kim * lim).astype(BF16)
                oim = (kre * lim + kim * lre).astype(BF16)
                kept[rows, u * wide : u * wide + my] = ore
                kept[rows, u * wide + my : (u + 1) * wide] = oim
                outer_put(j, a, u * wide, ore)
                outer_put(j, a, u * wide + my, oim)
                gre, gim = g[rows, :my], g[rows, my:]
                re += gre * lre + gim * lim
                im += gim * lre - gre * lim
            at_k = pl.ds(pl.multiple_of(k * rb, rb), rb)
            kgrad[at_k, :my] = re
            kgrad[at_k, my:] = im

    def mix_body(i, carry):
        add_second(outer_b, jnp.maximum(2 * i - 1, 0))
        products(2 * i, outer_a)
        add_second(outer_a, 2 * i)
        products(2 * i + 1, outer_b)
        plan(mix_hooks, i)
        return carry

    turns_of_part = half // per // parts // 2
    tp = turns_of_part
    if split:
        mix_hooks = [
            (tp // 4, [first_lg.plane_wait, first_lg.stack_send]),
            (tp * 5 // 8, [last_lg.plane_wait, last_lg.stack_send]),
            (tp * 7 // 8, [first_lg.stack_wait, first_lg.stack_back_send]),
            (tp + tp * 2 // 8, [last_lg.stack_wait, last_lg.stack_back_send]),
            (tp + tp * 4 // 8, [first_lg.stack_back_wait, first_lg.plane_back_send]),
            (tp + tp * 7 // 8, [last_lg.stack_back_wait, last_lg.plane_back_send]),
        ]
    else:
        mix_hooks = [
            (tp // 8, [last_lg.plane_wait, last_lg.stack_send]),
            (tp * 3 // 8, [last_lg.stack_wait, last_lg.stack_back_send]),
            (tp * 7 // 8, [last_lg.stack_back_wait, last_lg.plane_back_send]),
        ]
    for p in range(parts):
        share = half // parts
        lead_sums[p].plane_back_wait()
        where = pl.ds(p * 2 * share, 2 * share)
        got = lead_res[where].reshape(share, 2, ra, my).astype(F32)
        lead_f[p * share : (p + 1) * share, :, :my] = got[:, 0]
        lead_f[p * share : (p + 1) * share, :, my:] = got[:, 1]
        lax.fori_loop(p * turns_of_part, (p + 1) * turns_of_part, mix_body, 0)
    add_second(outer_b, half // per - 1)

    def second_copy():
        return remote(
            part_second.at[pl.ds(other * (pairs // 2), pairs // 2)], gp_core,
            core_send.at[1], core_recv.at[1], partner,
        )

    def back_copy(p):
        where = pl.ds(p * (lg_all.shape[1] // parts), lg_all.shape[1] // parts)
        return remote(
            lg_all.at[core, where], lg_all.at[core, where],
            core_send.at[5 + p], core_recv.at[5 + p], partner,
        )

    second_copy().start()
    by_mode = jnp.swapaxes(kgrad[...].reshape(half, rb, wide), 0, 1).reshape(rb * half, wide)
    by_mode = by_mode.astype(BF16)
    part_third = dot_nt(col.astype(BF16), by_mode)
    third_flat = jnp.concatenate(
        [jnp.where(core == 0, third[b][:, :half], third[b][:, half:]) for b in range(rb)], axis=1
    )
    part_fourth = dot(third_flat.astype(BF16), by_mode)
    second_copy().wait()
    mine = part_second[pl.ds(core * (pairs // 2), pairs // 2)] + gp_core[...]
    if both % LANES:
        mine = dot(mine, one_hot(both, channels, at.chan // 2 * both).astype(F32), HI)
    else:
        mine = jnp.concatenate(
            [jnp.where(at.chan // 2 == p, mine, 0.0) for p in range(channels // both)], axis=1
        )

    pieces = []
    for value in (mine, part_third, part_fourth):
        for c in range(value.shape[1] // LANES):
            pieces.append((value, c))
    spots, count = [], 0
    for value, c in pieces:
        tiles = value.shape[0] // 8
        gp_x[count : count + tiles] = value[:, c * LANES : (c + 1) * LANES].reshape(
            tiles, 8, LANES
        )
        spots.append((count, tiles))
        count += tiles
    if count < gp_x.shape[0]:
        gp_x[count:] = jnp.zeros((gp_x.shape[0] - count, 8, LANES), F32)
    gp_sum.plane_send()
    if split:
        first_lg.plane_back_wait()
        back_copy(0).start()
    pick = one_hot(chan, channels, at.chan * chan).astype(BF16)
    first_bf = dot_nt(pick, first_t[...].astype(BF16)).astype(BF16)
    kron_back[...] = spread(first_bf, chan, ra)
    kron_copy = pltpu.make_async_copy(kron_back, kron_out, turns_sem.at[3])
    kron_copy.start()

    groups = half // STEP

    def out_copy(g):
        return remote(
            s_stage.at[g, :, :, pl.ds(other * chan * my, chan * my)],
            spec_out.at[:, pl.ds(core * half + g * STEP, STEP), :],
            out_send.at[g], out_recv.at[g], partner,
        )

    def out_body(g, carry):
        for j in range(STEP // per):
            for u in range(per):
                held_o[j * per + u, :both] = dot(
                    by_t[...], outer_get(g * (STEP // per) + j, u * wide, wide)
                )
        turned = jnp.swapaxes(held_o[:, :both], 0, 1).astype(BF16)
        for o in range(both):
            for q in range(2):
                s_stage[g, q, :, o * my : (o + 1) * my] = turned[o, :, q * my : (q + 1) * my]
        out_copy(g).start()
        row = pl.ds(pl.multiple_of(core * half + g * STEP, STEP), STEP)
        lanes = pl.ds(pl.multiple_of(core * chan * my, chan * my), chan * my)
        spec_out[:, row, :] = s_stage[g, :, :, lanes]

        @pl.when(g == groups - 1)
        def _():
            gp_sum.plane_wait()
            gp_sum.stack_send()

        return carry

    lax.fori_loop(0, groups, out_body, 0)
    last_lg.plane_back_wait()
    back_copy(parts - 1).start()
    for p in range(parts):
        back_copy(p).wait()
    for q in range(2):
        for h in range(2):
            got = lg_all[h].reshape(half, 2, ra, my)[:, q].astype(F32)
            turned = jnp.swapaxes(got, 0, 1).astype(BF16)
            for a in range(ra):
                back_in[
                    q * mx + h * half : q * mx + (h + 1) * half, a * my : (a + 1) * my
                ] = turned[a]
    r = dot(csb[...], back_in[...]).astype(BF16)
    for a in range(ra):
        for q in range(2):
            back_rows[a, :, q * my : (q + 1) * my] = r[
                q * n : (q + 1) * n, a * my : (a + 1) * my
            ]
    total[...] = jnp.zeros_like(total)

    def first_body(i, carry):
        row = pl.ds(pl.multiple_of(i * STEP, STEP), STEP)
        block = back_rows[:, row, :].reshape(ra * STEP, wide)
        total[...] += dot_nt(modes_v[:, row, :].reshape(chan * STEP, wide), block)
        return carry

    lax.fori_loop(0, n // STEP, first_body, 0)
    shape = (STEP, ra * STEP)
    unit = lax.broadcasted_iota(jnp.int32, shape, 1) % STEP == lax.broadcasted_iota(
        jnp.int32, shape, 0
    )
    kept = total[...].reshape(chan, STEP, ra * STEP) * unit.astype(F32)[None]
    lane_f = lax.broadcasted_iota(jnp.int32, (ra, ra * STEP), 1)
    row_f = lax.broadcasted_iota(jnp.int32, (ra, ra * STEP), 0)
    pick = (lane_f // STEP == row_f).astype(F32)
    part_first = dot_nt(pick, jnp.sum(kept, axis=1), HI)
    f_core[core] = dot(part_first, one_hot(chan, channels, at.chan * chan).astype(F32), HI)

    def first_core_copy():
        return remote(f_core.at[core], f_core.at[core], core_send.at[3], core_recv.at[3], partner)

    def first_plane_copy(s):
        return remote(
            f_plane.at[at.plane], f_plane.at[at.plane],
            f_send.at[0, s - 1], f_recv.at[0, s - 1], at.across_plane(s),
        )

    def first_stack_copy(s):
        return remote(
            f_stack.at[at.stack], f_stack.at[at.stack],
            f_send.at[1, s - 1], f_recv.at[1, s - 1], at.across_stack(s),
        )

    def first_plane():
        first_core_copy().wait()
        f_plane[at.plane] = f_core[0] + f_core[1]
        for s in range(1, at.planes):
            first_plane_copy(s).start()

    def first_stack():
        for s in range(1, at.planes):
            first_plane_copy(s).wait()
        value = f_plane[0]
        for s in range(1, at.planes):
            value = value + f_plane[s]
        f_stack[at.stack] = value
        for s in range(1, at.stacks):
            first_stack_copy(s).start()

    first_core_copy().start()
    for g in range(groups):
        out_copy(g).wait()

    turns = 8

    def rows_copy(i):
        where = pl.ds(i * turns, turns)
        return pltpu.make_async_copy(modes_v.at[where], rows_out.at[where], rows_sem.at[i])

    def rows_body(i, carry):
        lanes = pl.ds(pl.multiple_of(i * turns * my, turns * my), turns * my)
        r = dot(csb[...], spec_out[:, :, lanes].reshape(2 * mx, turns * my))
        for c in range(turns):
            for q in range(2):
                part = r[q * n : (q + 1) * n, c * my : (c + 1) * my] * weight[:, :my]
                modes_v[i * turns + c, :, q * my : (q + 1) * my] = part.astype(BF16)
        rows_copy(i).start()

        @pl.when(i == steps // 4)
        def _():
            gp_sum.stack_wait()
            gp_sum.stack_back_send()
            first_plane()

        return carry

    steps = chan // turns
    lax.fori_loop(0, steps, rows_body, 0)
    first_stack()
    gp_sum.stack_back_wait()
    gp_sum.plane_back_send()

    def wide_copy(i):
        where = pl.ds(i * 4, 4)
        return pltpu.make_async_copy(block_v.at[0, where], back_out.at[where], wide_sem.at[i])

    def wide_body(i, carry):
        part = back_rows[pl.ds(i * 4, 4)].reshape(4 * n, wide)
        product = dot_nt(part, table[...]) * (1.0 / side)
        block_v[0, pl.ds(i * 4, 4)] = product.astype(BF16).reshape(4, n, side)
        wide_copy(i).start()
        return carry

    lax.fori_loop(0, ra // 4, wide_body, 0)
    for s in range(1, at.stacks):
        first_stack_copy(s).wait()
    value = f_stack[0]
    for s in range(1, at.stacks):
        value = value + f_stack[s]
    g_first[...] = value * (1.0 / (side * mx))
    gp_sum.plane_back_wait()

    def grads_copy():
        return remote(gp_all.at[core], gp_all.at[core], core_send.at[4], core_recv.at[4], partner)

    grads_copy().start()
    grads_copy().wait()

    def tile(h, index):
        start, size = spots[index]
        return gp_all[h, start : start + size].reshape(size * 8, LANES) * (1.0 / mx)

    cols = channels // LANES
    for h in range(2):
        for c in range(cols):
            g_second[
                h * (pairs // 2) : (h + 1) * (pairs // 2), c * LANES : (c + 1) * LANES
            ] = tile(h, c)
    low = lax.broadcasted_iota(jnp.int32, (rd, LANES), 1) < half
    for j in range(rb // 2):
        t0, t1 = tile(0, cols + j), tile(1, cols + j)
        g_third[2 * j] = jnp.where(low, t0, pltpu.roll(t1, half, 1))
        g_third[2 * j + 1] = jnp.where(low, pltpu.roll(t0, half, 1), t1)
    for q in range(2):
        g_fourth[q] = tile(0, cols + rb // 2 + q) + tile(1, cols + rb // 2 + q)
    for i in range(steps):
        rows_copy(i).wait()
    kron_copy.wait()
    for i in range(ra // 4):
        wide_copy(i).wait()


def output_kernel(
    table_in, rows_in, back_in, kron_in, *refs
):
    grads_in, (out, out_back), grads_out = refs[:4], refs[4:6], refs[6:10]
    table, rows, back, out_v, back_v, kron = refs[10:16]
    grads, (in_sem, rows_sem, grad_sem, out_sem, back_sem) = refs[16:20], refs[20:]
    chan, n, side = out.shape
    rank, wide = back.shape[0], rows.shape[2]
    slots, block = out_v.shape[:2]
    steps, row_steps = chan // block, n // STEP
    back_slots = back_v.shape[0]

    def rows_copy(i):
        where = pl.ds(i * block, block)
        return pltpu.make_async_copy(rows_in.at[where], rows.at[where], rows_sem.at[i])

    table_copy = pltpu.make_async_copy(table_in, table, in_sem.at[0])
    back_copy = pltpu.make_async_copy(back_in, back, in_sem.at[1])
    table_copy.start()
    for i in range(steps):
        rows_copy(i).start()
    kron_copy = pltpu.make_async_copy(kron_in, kron, in_sem.at[2])
    kron_copy.start()
    back_copy.start()
    for i in range(4):
        pltpu.make_async_copy(grads_in[i], grads[i], grad_sem.at[0, i]).start()

    def out_copy(i):
        slot = lax.rem(i, slots)
        return pltpu.make_async_copy(
            out_v.at[slot], out.at[pl.ds(i * block, block)], out_sem.at[slot]
        )

    def out_body(i, carry):
        rows_copy(i).wait()

        @pl.when(i >= slots)
        def _():
            out_copy(i - slots).wait()

        product = dot(rows[pl.ds(i * block, block)].reshape(block * n, wide), table[...])
        out_v[lax.rem(i, slots)] = product.astype(BF16).reshape(block, n, side)
        out_copy(i).start()
        return carry

    def in_copy(i):
        slot = lax.rem(i, back_slots)
        return pltpu.make_async_copy(
            back_v.at[slot],
            out_back.at[:, pl.ds(pl.multiple_of(i * STEP, STEP), STEP), :],
            back_sem.at[slot],
        )

    def in_body(i, carry):
        @pl.when(i >= back_slots)
        def _():
            in_copy(i - back_slots).wait()

        part = back[:, pl.ds(pl.multiple_of(i * STEP, STEP), STEP), :].reshape(rank * STEP, side)
        product = dot(kron[...], part)
        back_v[lax.rem(i, back_slots)] = product.astype(BF16).reshape(chan, STEP, side)
        in_copy(i).start()
        return carry

    table_copy.wait()
    lax.fori_loop(0, steps, out_body, 0)
    kron_copy.wait()
    back_copy.wait()
    for i in range(4):
        pltpu.make_async_copy(grads_in[i], grads[i], grad_sem.at[0, i]).wait()
        pltpu.make_async_copy(grads[i], grads_out[i], grad_sem.at[1, i]).start()
    lax.fori_loop(0, row_steps, in_body, 0)
    for i in range(max(steps - slots, 0), steps):
        out_copy(jnp.int32(i)).wait()
    for i in range(max(row_steps - back_slots, 0), row_steps):
        in_copy(jnp.int32(i)).wait()
    for i in range(4):
        pltpu.make_async_copy(grads[i], grads_out[i], grad_sem.at[1, i]).wait()


def local(input_field, out_cotangent, core_first, core_second, core_third, column_mode_core):
    grid_count, chan_count = lax.axis_size("grid"), lax.axis_size("chan")
    chan_index = lax.axis_index("chan")
    chan, rows, side = input_field.shape
    channels, rank_a = core_first.shape
    rank_b, modes_x, rank_d = core_third.shape
    modes_y = column_mode_core.shape[2]
    wide = 2 * modes_y
    half = modes_x // 2
    both = 2 * chan
    pairs = rank_a * rank_b

    table_np = width_table(side, modes_y)
    table = jnp.asarray(table_np)
    table_t = jnp.asarray(np.ascontiguousarray(table_np.T))
    turns = turn_table(side, modes_x).reshape(2, modes_x, grid_count, rows)
    turns = jnp.asarray(np.ascontiguousarray(turns.transpose(2, 0, 1, 3)))

    first_t = core_first.T
    second = core_second.transpose(0, 2, 1).reshape(pairs, channels)
    if both % LANES:
        second = lax.dynamic_slice_in_dim(second, chan_index // 2 * both, both, 1)
    third = core_third.transpose(0, 2, 1)
    anywhere = pl.BlockSpec(memory_space=pl.ANY)

    row_steps = rows // STEP
    planes, stacks = chan_count, grid_count // 2
    tiles = 2 * half
    owners = planes * stacks
    grad_tiles = (pairs // 2 * channels + rank_d * rank_b * half + rank_d * wide) // (8 * LANES)
    grad_tiles += -grad_tiles % owners
    sub = STEP
    subs = chan // sub
    slots = min(SLOTS, 2 * subs)
    blocks = subs
    fold = rows == pairs // 2 and side == 4 * wide and slots * sub >= half // 2
    outer_shape = (1, 1, 16, LANES) if fold else (1, half // 2, pairs, 2 * wide)
    parts = 2 if tiles % (2 * owners) == 0 else 1
    row_groups = rows // STEP
    wide_y = max(sub * modes_y, row_groups * wide)
    groups = half // STEP
    peers = max(planes, stacks) - 1
    steps = chan // 8

    def reduce_buffers(count, shape, dtype, lead=()):
        chunk = count // planes
        return [
            pltpu.VMEM((*lead, planes - 1, chunk, *shape), dtype),
            pltpu.VMEM((*lead, stacks - 1, chunk // stacks, *shape), dtype),
            pltpu.VMEM((*lead, chunk, *shape), dtype),
        ]

    tile = (rank_a, modes_y)
    scratch = [
        pltpu.VMEM((slots, sub, rows, side), BF16),
        pltpu.VMEM((chan * STEP, rank_a * STEP), BF16),
        pltpu.VMEM((side, wide), BF16),
        pltpu.VMEM((rank_a, rows, wide), BF16),
        pltpu.VMEM((pairs, 2 * wide), BF16),
        pltpu.VMEM((pairs, 2 * wide), BF16),
        pltpu.VMEM((chan, rows, wide), BF16),
        pltpu.VMEM((max(2 * rows, sub * STEP), wide_y), BF16),
        pltpu.VMEM((STEP, 2 * modes_x, modes_y), F32),
        pltpu.VMEM((blocks, modes_x, STEP, wide), BF16),
        pltpu.VMEM((half, both, wide), BF16),
        pltpu.VMEM((groups, 2, STEP, both * modes_y), BF16),
        pltpu.VMEM((2, modes_x, chan * modes_y), BF16),
        pltpu.VMEM((2, modes_x, rows), BF16),
        pltpu.VMEM((2 * modes_x, 2 * rows), BF16),
        pltpu.VMEM((2 * rows, 2 * modes_x), BF16),
        pltpu.VMEM((rank_a * STEP, chan * STEP), BF16),
        pltpu.VMEM((rank_a * STEP, row_groups * wide), F32),
        pltpu.VMEM((pairs, both), BF16),
        pltpu.VMEM((pairs, both), BF16),
        pltpu.VMEM((both, pairs), BF16),
        pltpu.VMEM((half, rank_b, wide), F32),
        pltpu.VMEM((half, rank_a, wide), F32),
        pltpu.VMEM((half * rank_b, wide), F32),
        pltpu.VMEM(outer_shape, BF16),
        pltpu.VMEM((STEP, max(both, modes_x), wide), F32),
        pltpu.VMEM((pairs, both), F32),
        pltpu.VMEM((2 * modes_x, rank_a * modes_y), BF16),
        pltpu.VMEM((chan * STEP, rank_a * STEP), F32),
        pltpu.VMEM((modes_x, 2, *tile), BF16),
        pltpu.VMEM((half, 2, *tile), BF16),
        pltpu.VMEM((tiles, *tile), BF16),
        pltpu.VMEM((tiles, *tile), BF16),
        *reduce_buffers(tiles // parts, tile, BF16, (parts,)),
        pltpu.VMEM((tiles, *tile), BF16),
        pltpu.VMEM((2, tiles, *tile), BF16),
        *reduce_buffers(tiles // parts, tile, BF16, (parts,)),
        pltpu.VMEM((pairs // 2, both), F32),
        pltpu.VMEM((grad_tiles, 8, LANES), F32),
        pltpu.VMEM((2, grad_tiles, 8, LANES), F32),
        *reduce_buffers(grad_tiles, (8, LANES), F32),
        pltpu.VMEM((2, rank_a, channels), F32),
        pltpu.VMEM((planes, rank_a, channels), F32),
        pltpu.VMEM((stacks, rank_a, channels), F32),
        *[pltpu.SemaphoreType.DMA((parts, 4, peers))] * 4,
        *[pltpu.SemaphoreType.DMA((4, peers))] * 2,
        *[pltpu.SemaphoreType.DMA((5 + parts,))] * 2,
        *[pltpu.SemaphoreType.DMA((blocks,))] * 2,
        *[pltpu.SemaphoreType.DMA((groups,))] * 2,
        *[pltpu.SemaphoreType.DMA((2, peers))] * 2,
        pltpu.SemaphoreType.DMA((slots,)),
        pltpu.SemaphoreType.DMA((4,)),
        pltpu.SemaphoreType.DMA((steps,)),
        pltpu.SemaphoreType.DMA((rank_a // 4,)),
    ]
    vmem = pl.BlockSpec(memory_space=pltpu.VMEM)
    out_rows, back_rows, kron, g_first, g_second, g_third, g_fourth = pl.pallas_call(
        spectral_kernel,
        in_specs=[anywhere] * 4 + [vmem] * 4,
        out_specs=[anywhere] * 3 + [vmem] * 4,
        out_shape=[
            jax.ShapeDtypeStruct((chan, rows, wide), BF16),
            jax.ShapeDtypeStruct((rank_a, rows, side), BF16),
            jax.ShapeDtypeStruct((chan * STEP, rank_a * STEP), BF16),
            jax.ShapeDtypeStruct((rank_a, channels), F32),
            jax.ShapeDtypeStruct((pairs, channels), F32),
            jax.ShapeDtypeStruct((rank_b, rank_d, modes_x), F32),
            jax.ShapeDtypeStruct((2, rank_d, modes_y), F32),
        ],
        scratch_shapes=scratch,
        compiler_params=pltpu.CompilerParams(
            collective_id=0, has_side_effects=True, vmem_limit_bytes=63 * 2**20
        ),
        name="spectral",
    )(input_field, out_cotangent, turns, table, first_t, second, third, column_mode_core)

    out_step = min(chan, 8)
    out_steps = chan // out_step
    out_slots, back_slots = min(4, out_steps), min(4, row_steps)
    grads = [
        (rank_a, channels), (pairs, channels), (rank_b, rank_d, modes_x), (2, rank_d, modes_y)
    ]
    output_field, input_grad, g_first, g_second, g_third, g_fourth = pl.pallas_call(
        output_kernel,
        in_specs=[anywhere] * 8,
        out_specs=[anywhere] * 6,
        out_shape=[
            jax.ShapeDtypeStruct((chan, rows, side), BF16),
            jax.ShapeDtypeStruct((chan, rows, side), BF16),
            *[jax.ShapeDtypeStruct(shape, F32) for shape in grads],
        ],
        scratch_shapes=[
            pltpu.VMEM((wide, side), BF16),
            pltpu.VMEM((chan, rows, wide), BF16),
            pltpu.VMEM((rank_a, rows, side), BF16),
            pltpu.VMEM((out_slots, out_step, rows, side), BF16),
            pltpu.VMEM((back_slots, chan, STEP, side), BF16),
            pltpu.VMEM((chan * STEP, rank_a * STEP), BF16),
            *[pltpu.VMEM(shape, F32) for shape in grads],
            pltpu.SemaphoreType.DMA((3,)),
            pltpu.SemaphoreType.DMA((out_steps,)),
            pltpu.SemaphoreType.DMA((2, 4)),
            pltpu.SemaphoreType.DMA((out_slots,)),
            pltpu.SemaphoreType.DMA((back_slots,)),
        ],
        compiler_params=params(60),
        name="output",
    )(table_t, out_rows, back_rows, kron, g_first, g_second, g_third, g_fourth)

    return (
        output_field,
        input_grad,
        g_first.T,
        g_second.reshape(rank_a, rank_b, channels).transpose(0, 2, 1),
        g_third.transpose(0, 2, 1),
        g_fourth,
    )


def solution(mesh):
    placed = (P("chan", "grid", None), P("chan", "grid", None), P(), P(), P(), P())
    return jax.shard_map(
        local,
        mesh=mesh,
        in_specs=placed,
        out_specs=(P("chan", "grid", None), P("chan", "grid", None), P(), P(), P(), P()),
        check_vma=False,
    )
```

```python
import math

import jax
import jax.numpy as jnp
import numpy as np
from jax import lax
from jax.experimental import pallas as pl
from jax.experimental.pallas import tpu as pltpu
from jax.sharding import PartitionSpec as P

F32 = jnp.float32
BF16 = jnp.bfloat16
HI = lax.Precision.HIGHEST
STEP = 16
LANES = 128
SLOTS = 3
MESH = pl.DeviceIdType.MESH


def params(mib=48):
    return pltpu.CompilerParams(vmem_limit_bytes=mib * 2**20)


def dot(a, b, precision=None):
    return jnp.dot(a, b, preferred_element_type=F32, precision=precision)


def dot_nt(a, b, precision=None):
    return lax.dot_general(
        a, b, (((1,), (1,)), ((), ())), preferred_element_type=F32, precision=precision
    )


def dot_tn(a, b, precision=None):
    return lax.dot_general(
        a, b, (((0,), (0,)), ((), ())), preferred_element_type=F32, precision=precision
    )


def width_table(side, modes_y):
    phase = np.arange(side)[:, None] * np.arange(modes_y)[None, :] % side
    angle = phase.astype(np.float32) * np.float32(2.0 * math.pi / side)
    return np.concatenate([np.cos(angle), -np.sin(angle)], axis=1).astype(BF16)


def turn_table(side, modes_x):
    kx = np.arange(modes_x)
    freq = np.where(kx < modes_x // 2, kx, side - modes_x + kx)
    phase = freq[:, None] * np.arange(side)[None, :] % side
    angle = phase.astype(np.float32) * np.float32(2.0 * math.pi / side)
    return np.stack([np.cos(angle), np.sin(angle)]).astype(BF16)


def one_hot(rows, cols, offset):
    row = lax.broadcasted_iota(jnp.int32, (rows, cols), 0)
    col = lax.broadcasted_iota(jnp.int32, (rows, cols), 1)
    return col == row + offset


def spread(values, rows, n, offset=0):
    lane = lax.broadcasted_iota(jnp.int32, (values.shape[1], n * STEP), 1)
    row = lax.broadcasted_iota(jnp.int32, (values.shape[1], n * STEP), 0)
    wide = dot(values, (lane // STEP + offset == row).astype(BF16))
    at = lax.broadcasted_iota(jnp.int32, (STEP, n * STEP), 1) % STEP
    unit = (at == lax.broadcasted_iota(jnp.int32, (STEP, n * STEP), 0)).astype(F32)
    return (wide[:, None, :] * unit[None]).reshape(rows * STEP, n * STEP).astype(BF16)


def flip(index, bits):
    bit = 1
    while bit <= bits:
        if bits & bit:
            index = index + bit * (1 - 2 * (index // bit % 2))
        bit *= 2
    return index


class Place:
    def __init__(self):
        self.grid, self.chan = lax.axis_index("grid"), lax.axis_index("chan")
        self.core = self.chan % 2
        self.planes = lax.axis_size("chan")
        self.stacks = lax.axis_size("grid") // 2
        self.plane = self.chan // 2 * 2 + self.grid % 2
        self.stack = self.grid // 2

    def across_core(self):
        return {"grid": self.grid, "chan": flip(self.chan, 1)}

    def across_plane(self, s):
        return {"grid": flip(self.grid, s % 2), "chan": flip(self.chan, s // 2 * 2)}

    def across_stack(self, s):
        return {"grid": flip(self.grid, s * 2), "chan": self.chan}

    def peers(self):
        return (
            [self.across_core()]
            + [self.across_plane(s) for s in range(1, self.planes)]
            + [self.across_stack(s) for s in range(1, self.stacks)]
        )


def remote(src, dst, send, recv, peer):
    return pltpu.make_async_remote_copy(
        src_ref=src, dst_ref=dst, send_sem=send, recv_sem=recv,
        device_id=peer, device_id_type=MESH,
    )


class Reduce:
    def __init__(self, place, source, result, land_plane, land_stack, send, recv):
        self.at, self.source, self.result = place, source, result
        self.land_plane, self.land_stack = land_plane, land_stack
        self.send, self.recv = send, recv
        self.chunk = source.shape[0] // place.planes

    def plane_copy(self, s):
        there = flip(self.at.plane, s)
        return remote(
            self.source.at[pl.ds(there * self.chunk, self.chunk)],
            self.land_plane.at[s - 1],
            self.send.at[0, s - 1], self.recv.at[0, s - 1], self.at.across_plane(s),
        )

    def plane_send(self):
        for s in range(1, self.at.planes):
            self.plane_copy(s).start()

    def plane_wait(self):
        for s in range(1, self.at.planes):
            self.plane_copy(s).wait()
        total = self.source[pl.ds(self.at.plane * self.chunk, self.chunk)].astype(F32)
        for s in range(1, self.at.planes):
            total = total + self.land_plane[s - 1].astype(F32)
        self.keep(total)

    def keep(self, total):
        self.land_stack[self.at.stack] = total.astype(self.land_stack.dtype)

    def stack_copy(self, s):
        mine = self.land_stack.at[self.at.stack]
        return remote(
            mine, mine, self.send.at[1, s - 1], self.recv.at[1, s - 1], self.at.across_stack(s)
        )

    def stack_send(self):
        for s in range(1, self.at.stacks):
            self.stack_copy(s).start()

    def stack_wait(self):
        for s in range(1, self.at.stacks):
            self.stack_copy(s).wait()
        total = self.land_stack[0].astype(F32)
        for s in range(1, self.at.stacks):
            total = total + self.land_stack[s].astype(F32)
        here = pl.ds(self.at.plane * self.chunk, self.chunk)
        self.result[here] = total.astype(self.result.dtype)

    def plane_back_copy(self, s):
        here = pl.ds(self.at.plane * self.chunk, self.chunk)
        return remote(
            self.result.at[here], self.result.at[here],
            self.send.at[2, s - 1], self.recv.at[2, s - 1], self.at.across_plane(s),
        )

    def plane_back_send(self):
        for s in range(1, self.at.planes):
            self.plane_back_copy(s).start()

    def plane_back_wait(self):
        for s in range(1, self.at.planes):
            self.plane_back_copy(s).wait()


class ScatterReduce(Reduce):
    def __init__(self, place, source, result, land_plane, land_stack, send, recv):
        super().__init__(place, source, result, land_plane, land_stack, send, recv)
        self.piece = self.chunk // place.stacks
        self.mid = land_stack.at[0]
        self.land_stack = [
            land_stack.at[1 + s // place.stacks, pl.ds(s % place.stacks * self.piece, self.piece)]
            for s in range(place.stacks - 1)
        ]

    def keep(self, total):
        self.mid[...] = total.astype(self.mid.dtype)

    def stack_copy(self, s):
        there = flip(self.at.stack, s)
        return remote(
            self.mid.at[pl.ds(there * self.piece, self.piece)],
            self.land_stack[s - 1],
            self.send.at[1, s - 1], self.recv.at[1, s - 1], self.at.across_stack(s),
        )

    def stack_send(self):
        for s in range(1, self.at.stacks):
            self.stack_copy(s).start()

    def own(self):
        return pl.ds(self.at.plane * self.chunk + self.at.stack * self.piece, self.piece)

    def stack_wait(self):
        for s in range(1, self.at.stacks):
            self.stack_copy(s).wait()
        total = self.mid[pl.ds(self.at.stack * self.piece, self.piece)].astype(F32)
        for s in range(1, self.at.stacks):
            total = total + self.land_stack[s - 1][...].astype(F32)
        self.result[self.own()] = total.astype(self.result.dtype)

    def stack_back_copy(self, s):
        return remote(
            self.result.at[self.own()], self.result.at[self.own()],
            self.send.at[3, s - 1], self.recv.at[3, s - 1], self.at.across_stack(s),
        )

    def stack_back_send(self):
        for s in range(1, self.at.stacks):
            self.stack_back_copy(s).start()

    def stack_back_wait(self):
        for s in range(1, self.at.stacks):
            self.stack_back_copy(s).wait()


def spectral_kernel(
    field, cot, turns_in, table_in, first_t, second, third, column,
    rows_out, back_out, kron_out, g_first, g_second, g_third, g_fourth,
    block_v, kron_back, table, back_rows, outer_a, outer_b, modes_v, y, held, spec_stage, spec, s_stage, spec_out, cs, csf, csb, kron, mixed,
    by_ab, by_ba, by_t, kern, lead_f, kgrad, outer, held_o, part_second, back_in, total,
    lead_v, lead_core, lead_x, lead_res, lead_lp, lead_ls,
    lg_x, lg_all, lg_lp, lg_ls,
    gp_core, gp_x, gp_all, gp_lp, gp_ls,
    f_core, f_plane, f_stack,
    lead_send, lead_recv, lg_send, lg_recv, gp_send, gp_recv,
    core_send, core_recv, spec_send, spec_recv, out_send, out_recv, f_send, f_recv,
    block_sem, turns_sem, rows_sem, wide_sem,
):
    if outer.shape[0] * outer.shape[1] * 2 < kern.shape[0]:
        outer = block_v
    at = Place()
    core = at.core
    other = 1 - core
    chan, n, side = cot.shape
    wide = table.shape[1]
    my = wide // 2
    mx = cs.shape[1]
    half = mx // 2
    ra, rb, rd = first_t.shape[0], third.shape[0], third.shape[1]
    pairs = ra * rb
    both = 2 * chan
    channels = g_first.shape[1]
    slots, sub = block_v.shape[:2]
    subs = chan // sub
    parts = lead_lp.shape[0]
    row_groups = n // STEP
    lane = lax.broadcasted_iota(jnp.int32, (1, wide), 1)
    weight = jnp.where(lane % my == 0, 1.0, 2.0) * (1.0 / side)
    partner = at.across_core()

    def block_copy(source, j, k):
        slot = lax.rem(k, slots)
        return pltpu.make_async_copy(
            source.at[pl.ds(j * sub, sub)], block_v.at[slot], block_sem.at[slot]
        )

    def fetch(k):
        @pl.when(k < subs)
        def _():
            block_copy(field, k, k).start()

        @pl.when(jnp.logical_and(k >= subs, k < 2 * subs))
        def _():
            block_copy(cot, k - subs, k).start()

    def rows_of_block(source, j, k):
        block_copy(source, j, k).wait()
        block = block_v[lax.rem(k, slots)].reshape(sub * n, side)
        product = dot(block, table[...]).astype(BF16)
        fetch(k + slots)
        return product

    barrier = pltpu.get_barrier_semaphore()
    peers = at.peers()
    for peer in peers:
        pl.semaphore_signal(barrier, inc=1, device_id=peer, device_id_type=MESH)
    table_copy = pltpu.make_async_copy(table_in, table, turns_sem.at[1])
    table_copy.start()
    for k in range(min(slots, 2 * subs)):
        if k < subs:
            block_copy(field, k, k).start()
        else:
            block_copy(cot, k - subs, k).start()
    turns_copy = pltpu.make_async_copy(turns_in.at[at.grid], cs, turns_sem.at[0])
    turns_copy.start()
    kron[...] = spread(first_t[...].astype(BF16), ra, chan, at.chan * chan)
    table_copy.wait()

    mixed[...] = jnp.zeros_like(mixed)

    def field_body(i, carry):
        product = rows_of_block(field, i, i)
        shaped = product.reshape(sub, n, wide)
        modes_v[pl.ds(i * sub, sub)] = shaped
        for g in range(row_groups):
            y[: sub * STEP, g * wide : (g + 1) * wide] = shaped[
                :, g * STEP : (g + 1) * STEP
            ].reshape(sub * STEP, wide)
        part = pl.ds(pl.multiple_of(i * sub * STEP, sub * STEP), sub * STEP)
        mixed[...] += dot(kron[:, part], y[: sub * STEP, : row_groups * wide])
        return carry

    lax.fori_loop(0, subs, field_body, 0)
    turns_copy.wait()
    c, s = cs[0], cs[1]
    csf[:mx, :n], csf[:mx, n:], csf[mx:, :n], csf[mx:, n:] = c, s, -s, c
    ct = jnp.swapaxes(c.astype(F32), 0, 1).astype(BF16)
    st = jnp.swapaxes(s.astype(F32), 0, 1).astype(BF16)
    csb[:n, :mx], csb[:n, mx:], csb[n:, :mx], csb[n:, mx:] = ct, -st, st, ct
    for g in range(row_groups):
        for q in range(2):
            for a in range(ra):
                back_in[q * n + g * STEP : q * n + (g + 1) * STEP, a * my : (a + 1) * my] = mixed[
                    a * STEP : (a + 1) * STEP, g * wide + q * my : g * wide + (q + 1) * my
                ].astype(BF16)
    z = dot(csf[...], back_in[: 2 * n]) * (1.0 / side)
    for a in range(ra):
        held[a] = z[:, a * my : (a + 1) * my]
    turned = jnp.swapaxes(held[...], 0, 1).astype(BF16)
    lead_v[:, 0] = turned[:mx]
    lead_v[:, 1] = turned[mx:]

    def lead_core_copy():
        return remote(
            lead_v.at[pl.ds(other * half, half)], lead_core,
            core_send.at[0], core_recv.at[0], partner,
        )

    pl.semaphore_wait(barrier, len(peers))
    lead_core_copy().start()

    if second.shape[1] > both and both % LANES == 0:
        sec = second[:, pl.ds(pl.multiple_of(at.chan // 2 * both, both), both)]
    else:
        sec = second[...]
    by_ab[...] = sec.astype(BF16)
    by_ba[...] = jnp.swapaxes(sec.reshape(ra, rb, both), 0, 1).reshape(pairs, both).astype(BF16)
    by_t[...] = jnp.swapaxes(sec, 0, 1).astype(BF16)
    col = jnp.concatenate([column[0], column[1]], axis=1)
    for b in range(rb):
        held_o[b, :mx] = dot_tn(third[b], col, HI)
    own_half = pl.ds(pl.multiple_of(core * half, half), half)
    kern[...] = jnp.swapaxes(held_o[:, own_half, :], 0, 1)

    split = parts > 1

    def sums(kind, source, result, land_plane, land_stack, send, recv):
        share = source.shape[0] // parts
        made = []
        for p in range(parts):
            where = pl.ds(p * share, share)
            made.append(kind(
                at, source.at[where], result(where), land_plane.at[p], land_stack.at[p],
                send.at[p], recv.at[p],
            ))
        return made

    lead_sums = sums(
        Reduce, lead_x, lambda w: lead_res.at[w], lead_lp, lead_ls, lead_send, lead_recv
    )
    lg_sums = sums(
        ScatterReduce if split else Reduce, lg_x, lambda w: lg_all.at[core, w], lg_lp, lg_ls, lg_send, lg_recv
    )
    gp_sum = Reduce(at, gp_x, gp_all.at[core], gp_lp, gp_ls, gp_send, gp_recv)

    lead_core_copy().wait()
    mine = lead_v[pl.ds(core * half, half)].astype(F32) + lead_core[...].astype(F32)
    lead_x[...] = mine.reshape(lead_x.shape).astype(BF16)
    lead_sums[0].plane_send()

    def plan(hooks, index):
        for when, todo in hooks:
            @pl.when(index == when)
            def _():
                for step in todo:
                    step()

    def spec_copy(i):
        return remote(
            spec_stage.at[i, pl.ds(other * half, half)],
            spec.at[:, pl.ds(core * chan + i * STEP, STEP), :],
            spec_send.at[i], spec_recv.at[i], partner,
        )

    first_lead, last_lead = lead_sums[0], lead_sums[-1]
    first_lg, last_lg = lg_sums[0], lg_sums[-1]

    def both_of(one, two):
        return [one] + ([two] if split else [])

    cot_hooks = [
        (
            min(1, subs - 1),
            [first_lead.plane_wait, first_lead.stack_send]
            + ([last_lead.plane_send] if split else []),
        ),
        (
            min(3, subs - 1),
            [last_lead.plane_wait, last_lead.stack_send] if split else [],
        ),
    ]

    def cot_body(i, carry):
        product = rows_of_block(cot, i, i + subs)
        for c in range(sub):
            for q in range(2):
                y[q * n : (q + 1) * n, c * my : (c + 1) * my] = product[
                    c * n : (c + 1) * n, q * my : (q + 1) * my
                ]
        z = dot(csf[...], y[: 2 * n, : sub * my])
        for c in range(sub):
            held[c] = z[:, c * my : (c + 1) * my] * weight[:, :my]
        turned = jnp.swapaxes(held[...], 0, 1).astype(BF16)
        spec_stage[i, :, :, :my] = turned[:mx]
        spec_stage[i, :, :, my:] = turned[mx:]
        spec_copy(i).start()
        spec[:, pl.ds(pl.multiple_of(core * chan + i * STEP, STEP), STEP), :] = spec_stage[
            i, pl.ds(core * half, half)
        ]

        plan(cot_hooks, i)
        return carry

    lax.fori_loop(0, subs, cot_body, 0)
    for i in range(subs):
        spec_copy(i).wait()

    unroll = 4

    def back_body(j, carry):
        for u in range(unroll):
            k = j * unroll + u
            g = dot(by_ba[...], spec[k])
            re = jnp.zeros((ra, my), F32)
            im = jnp.zeros((ra, my), F32)
            for b in range(rb):
                gre = g[b * ra : (b + 1) * ra, :my]
                gim = g[b * ra : (b + 1) * ra, my:]
                kre, kim = kern[k, b : b + 1, :my], kern[k, b : b + 1, my:]
                re += gre * kre + gim * kim
                im += gim * kre - gre * kim
            lg_x[2 * k] = re.astype(BF16)
            lg_x[2 * k + 1] = im.astype(BF16)

        plan(back_hooks, j)
        return carry

    rounds = half // unroll
    back_hooks = []
    if split:
        back_hooks = [
            (rounds * 6 // 16, [first_lead.stack_wait, first_lead.plane_back_send]),
            (rounds * 11 // 16, [first_lg.plane_send]),
        ]
    lax.fori_loop(0, rounds, back_body, 0)
    last_lead.stack_wait()
    last_lead.plane_back_send()
    last_lg.plane_send()
    part_second[...] = jnp.zeros_like(part_second)

    per = 2
    folded = outer.shape[1] != half // per

    def outer_put(j, a, lanes, value):
        row = a * rb
        if folded:
            lanes += row // (pairs // 2) * per * wide
            row %= pairs // 2
        outer[j // outer.shape[1], j % outer.shape[1], row : row + rb, lanes : lanes + my] = value

    def outer_get(j, lanes, size):
        slab = outer.at[j // outer.shape[1], j % outer.shape[1]]
        if not folded:
            return slab[:, lanes : lanes + size]
        low = slab[:, lanes : lanes + size]
        high = slab[:, per * wide + lanes : per * wide + lanes + size]
        return jnp.concatenate([low, high], axis=0)

    outer_b[...] = jnp.zeros_like(outer_b)

    def add_second(kept, j):
        rhs = jnp.concatenate([spec[j * per + u] for u in range(per)], axis=1)
        part_second[...] += dot_nt(kept[...], rhs)

    def products(j, kept):
        for u in range(per):
            k = j * per + u
            g = dot(by_ab[...], spec[k])
            kr = kern[k]
            kre, kim = kr[:, :my], kr[:, my:]
            re = jnp.zeros((rb, my), F32)
            im = jnp.zeros((rb, my), F32)
            for a in range(ra):
                rows = slice(a * rb, (a + 1) * rb)
                lre, lim = lead_f[k, a : a + 1, :my], lead_f[k, a : a + 1, my:]
                ore = (kre * lre - kim * lim).astype(BF16)
                oim = (kre * lim + kim * lre).astype(BF16)
                kept[rows, u * wide : u * wide + my] = ore
                kept[rows, u * wide + my : (u + 1) * wide] = oim
                outer_put(j, a, u * wide, ore)
                outer_put(j, a, u * wide + my, oim)
                gre, gim = g[rows, :my], g[rows, my:]
                re += gre * lre + gim * lim
                im += gim * lre - gre * lim
            at_k = pl.ds(pl.multiple_of(k * rb, rb), rb)
            kgrad[at_k, :my] = re
            kgrad[at_k, my:] = im

    def mix_body(i, carry):
        add_second(outer_b, jnp.maximum(2 * i - 1, 0))
        products(2 * i, outer_a)
        add_second(outer_a, 2 * i)
        products(2 * i + 1, outer_b)
        plan(mix_hooks, i)
        return carry

    turns_of_part = half // per // parts // 2
    tp = turns_of_part
    if split:
        mix_hooks = [
            (tp * 6 // 8, [first_lg.plane_wait, first_lg.stack_send]),
            (tp + tp // 8, [last_lg.plane_wait, last_lg.stack_send]),
            (tp + tp * 3 // 8, [first_lg.stack_wait, first_lg.stack_back_send]),
            (tp + tp * 5 // 8, [last_lg.stack_wait, last_lg.stack_back_send]),
            (tp + tp * 7 // 8, [first_lg.stack_back_wait, first_lg.plane_back_send]),
        ]
    else:
        mix_hooks = [
            (tp // 4, [last_lg.plane_wait, last_lg.stack_send]),
            (tp * 7 // 8, [last_lg.stack_wait, last_lg.plane_back_send]),
        ]
    for p in range(parts):
        share = half // parts
        lead_sums[p].plane_back_wait()
        where = pl.ds(p * 2 * share, 2 * share)
        got = lead_res[where].reshape(share, 2, ra, my).astype(F32)
        lead_f[p * share : (p + 1) * share, :, :my] = got[:, 0]
        lead_f[p * share : (p + 1) * share, :, my:] = got[:, 1]
        lax.fori_loop(p * turns_of_part, (p + 1) * turns_of_part, mix_body, 0)
    add_second(outer_b, half // per - 1)

    def second_copy():
        return remote(
            part_second.at[pl.ds(other * (pairs // 2), pairs // 2)], gp_core,
            core_send.at[1], core_recv.at[1], partner,
        )

    def back_copy(p):
        where = pl.ds(p * (lg_all.shape[1] // parts), lg_all.shape[1] // parts)
        return remote(
            lg_all.at[core, where], lg_all.at[core, where],
            core_send.at[5 + p], core_recv.at[5 + p], partner,
        )

    second_copy().start()
    by_mode = jnp.swapaxes(kgrad[...].reshape(half, rb, wide), 0, 1).reshape(rb * half, wide)
    by_mode = by_mode.astype(BF16)
    part_third = dot_nt(col.astype(BF16), by_mode)
    third_flat = jnp.concatenate(
        [jnp.where(core == 0, third[b][:, :half], third[b][:, half:]) for b in range(rb)], axis=1
    )
    part_fourth = dot(third_flat.astype(BF16), by_mode)
    second_copy().wait()
    mine = part_second[pl.ds(core * (pairs // 2), pairs // 2)] + gp_core[...]
    if both % LANES:
        mine = dot(mine, one_hot(both, channels, at.chan // 2 * both).astype(F32), HI)
    else:
        mine = jnp.concatenate(
            [jnp.where(at.chan // 2 == p, mine, 0.0) for p in range(channels // both)], axis=1
        )

    pieces = []
    for value in (mine, part_third, part_fourth):
        for c in range(value.shape[1] // LANES):
            pieces.append((value, c))
    spots, count = [], 0
    for value, c in pieces:
        tiles = value.shape[0] // STEP
        gp_x[count : count + tiles] = value[:, c * LANES : (c + 1) * LANES].astype(BF16).reshape(
            tiles, STEP, LANES
        )
        spots.append((count, tiles))
        count += tiles
    if count < gp_x.shape[0]:
        gp_x[count:] = jnp.zeros((gp_x.shape[0] - count, STEP, LANES), BF16)
    gp_sum.plane_send()
    if split:
        last_lg.stack_back_wait()
        last_lg.plane_back_send()
    pick = one_hot(chan, channels, at.chan * chan).astype(BF16)
    first_bf = dot_nt(pick, first_t[...].astype(BF16)).astype(BF16)
    kron_back[...] = spread(first_bf, chan, ra)
    kron_copy = pltpu.make_async_copy(kron_back, kron_out, turns_sem.at[3])
    kron_copy.start()

    groups = half // STEP

    def out_copy(g):
        return remote(
            s_stage.at[g, :, :, pl.ds(other * chan * my, chan * my)],
            spec_out.at[:, pl.ds(core * half + g * STEP, STEP), :],
            out_send.at[g], out_recv.at[g], partner,
        )

    def out_body(g, carry):
        for j in range(STEP // per):
            for u in range(per):
                held_o[j * per + u, :both] = dot(
                    by_t[...], outer_get(g * (STEP // per) + j, u * wide, wide)
                )
        turned = jnp.swapaxes(held_o[:, :both], 0, 1).astype(BF16)
        for o in range(both):
            for q in range(2):
                s_stage[g, q, :, o * my : (o + 1) * my] = turned[o, :, q * my : (q + 1) * my]
        out_copy(g).start()
        row = pl.ds(pl.multiple_of(core * half + g * STEP, STEP), STEP)
        lanes = pl.ds(pl.multiple_of(core * chan * my, chan * my), chan * my)
        spec_out[:, row, :] = s_stage[g, :, :, lanes]

        @pl.when(g == groups // 2)
        def _():
            gp_sum.plane_wait()
            gp_sum.stack_send()

        if split:
            @pl.when(g == groups - 1)
            def _():
                first_lg.plane_back_wait()
                back_copy(0).start()

        return carry

    lax.fori_loop(0, groups, out_body, 0)
    last_lg.plane_back_wait()
    back_copy(parts - 1).start()
    for p in range(parts):
        back_copy(p).wait()
    for q in range(2):
        for h in range(2):
            got = lg_all[h].reshape(half, 2, ra, my)[:, q].astype(F32)
            turned = jnp.swapaxes(got, 0, 1).astype(BF16)
            for a in range(ra):
                back_in[
                    q * mx + h * half : q * mx + (h + 1) * half, a * my : (a + 1) * my
                ] = turned[a]
    r = dot(csb[...], back_in[...]).astype(BF16)
    for a in range(ra):
        for q in range(2):
            back_rows[a, :, q * my : (q + 1) * my] = r[
                q * n : (q + 1) * n, a * my : (a + 1) * my
            ]
    total[...] = jnp.zeros_like(total)

    def first_body(i, carry):
        row = pl.ds(pl.multiple_of(i * STEP, STEP), STEP)
        block = back_rows[:, row, :].reshape(ra * STEP, wide)
        total[...] += dot_nt(modes_v[:, row, :].reshape(chan * STEP, wide), block)
        return carry

    lax.fori_loop(0, n // STEP, first_body, 0)
    shape = (STEP, ra * STEP)
    unit = lax.broadcasted_iota(jnp.int32, shape, 1) % STEP == lax.broadcasted_iota(
        jnp.int32, shape, 0
    )
    kept = total[...].reshape(chan, STEP, ra * STEP) * unit.astype(F32)[None]
    lane_f = lax.broadcasted_iota(jnp.int32, (ra, ra * STEP), 1)
    row_f = lax.broadcasted_iota(jnp.int32, (ra, ra * STEP), 0)
    pick = (lane_f // STEP == row_f).astype(F32)
    part_first = dot_nt(pick, jnp.sum(kept, axis=1), HI)
    f_core[core] = dot(part_first, one_hot(chan, channels, at.chan * chan).astype(F32), HI)

    def first_core_copy():
        return remote(f_core.at[core], f_core.at[core], core_send.at[3], core_recv.at[3], partner)

    def first_plane_copy(s):
        return remote(
            f_plane.at[at.plane], f_plane.at[at.plane],
            f_send.at[0, s - 1], f_recv.at[0, s - 1], at.across_plane(s),
        )

    def first_stack_copy(s):
        return remote(
            f_stack.at[at.stack], f_stack.at[at.stack],
            f_send.at[1, s - 1], f_recv.at[1, s - 1], at.across_stack(s),
        )

    def first_plane():
        first_core_copy().wait()
        f_plane[at.plane] = f_core[0] + f_core[1]
        for s in range(1, at.planes):
            first_plane_copy(s).start()

    def first_stack():
        for s in range(1, at.planes):
            first_plane_copy(s).wait()
        value = f_plane[0]
        for s in range(1, at.planes):
            value = value + f_plane[s]
        f_stack[at.stack] = value
        for s in range(1, at.stacks):
            first_stack_copy(s).start()

    first_core_copy().start()
    for g in range(groups):
        out_copy(g).wait()

    turns = 8

    def rows_copy(i):
        where = pl.ds(i * turns, turns)
        return pltpu.make_async_copy(modes_v.at[where], rows_out.at[where], rows_sem.at[i])

    def rows_body(i, carry):
        lanes = pl.ds(pl.multiple_of(i * turns * my, turns * my), turns * my)
        r = dot(csb[...], spec_out[:, :, lanes].reshape(2 * mx, turns * my))
        for c in range(turns):
            for q in range(2):
                part = r[q * n : (q + 1) * n, c * my : (c + 1) * my] * weight[:, :my]
                modes_v[i * turns + c, :, q * my : (q + 1) * my] = part.astype(BF16)
        rows_copy(i).start()

        @pl.when(i == steps // 4)
        def _():
            first_plane()

        @pl.when(i == steps * 5 // 8)
        def _():
            gp_sum.stack_wait()
            gp_sum.plane_back_send()

        return carry

    steps = chan // turns
    lax.fori_loop(0, steps, rows_body, 0)
    first_stack()

    def wide_copy(i):
        where = pl.ds(i * 4, 4)
        return pltpu.make_async_copy(block_v.at[0, where], back_out.at[where], wide_sem.at[i])

    def wide_body(i, carry):
        part = back_rows[pl.ds(i * 4, 4)].reshape(4 * n, wide)
        product = dot_nt(part, table[...]) * (1.0 / side)
        block_v[0, pl.ds(i * 4, 4)] = product.astype(BF16).reshape(4, n, side)
        wide_copy(i).start()
        return carry

    lax.fori_loop(0, ra // 4, wide_body, 0)
    for s in range(1, at.stacks):
        first_stack_copy(s).wait()
    value = f_stack[0]
    for s in range(1, at.stacks):
        value = value + f_stack[s]
    g_first[...] = value * (1.0 / (side * mx))
    gp_sum.plane_back_wait()

    def grads_copy():
        return remote(gp_all.at[core], gp_all.at[core], core_send.at[4], core_recv.at[4], partner)

    grads_copy().start()
    grads_copy().wait()

    def tile(h, index):
        start, size = spots[index]
        return gp_all[h, start : start + size].reshape(size * STEP, LANES).astype(F32) * (1.0 / mx)

    cols = channels // LANES
    for h in range(2):
        for c in range(cols):
            g_second[
                h * (pairs // 2) : (h + 1) * (pairs // 2), c * LANES : (c + 1) * LANES
            ] = tile(h, c)
    low = lax.broadcasted_iota(jnp.int32, (rd, LANES), 1) < half
    for j in range(rb // 2):
        t0, t1 = tile(0, cols + j), tile(1, cols + j)
        g_third[2 * j] = jnp.where(low, t0, pltpu.roll(t1, half, 1))
        g_third[2 * j + 1] = jnp.where(low, pltpu.roll(t0, half, 1), t1)
    for q in range(2):
        g_fourth[q] = tile(0, cols + rb // 2 + q) + tile(1, cols + rb // 2 + q)
    for i in range(steps):
        rows_copy(i).wait()
    kron_copy.wait()
    for i in range(ra // 4):
        wide_copy(i).wait()


def output_kernel(
    table_in, rows_in, back_in, kron_in, *refs
):
    grads_in, (out, out_back), grads_out = refs[:4], refs[4:6], refs[6:10]
    table, rows, back, out_v, back_v, kron = refs[10:16]
    grads, (in_sem, rows_sem, grad_sem, out_sem, back_sem) = refs[16:20], refs[20:]
    chan, n, side = out.shape
    rank, wide = back.shape[0], rows.shape[2]
    slots, block = out_v.shape[:2]
    steps, row_steps = chan // block, n // STEP
    back_slots = back_v.shape[0]

    def rows_copy(i):
        where = pl.ds(i * block, block)
        return pltpu.make_async_copy(rows_in.at[where], rows.at[where], rows_sem.at[i])

    table_copy = pltpu.make_async_copy(table_in, table, in_sem.at[0])
    back_copy = pltpu.make_async_copy(back_in, back, in_sem.at[1])
    table_copy.start()
    for i in range(steps):
        rows_copy(i).start()
    kron_copy = pltpu.make_async_copy(kron_in, kron, in_sem.at[2])
    kron_copy.start()
    back_copy.start()
    for i in range(4):
        pltpu.make_async_copy(grads_in[i], grads[i], grad_sem.at[0, i]).start()

    def out_copy(i):
        slot = lax.rem(i, slots)
        return pltpu.make_async_copy(
            out_v.at[slot], out.at[pl.ds(i * block, block)], out_sem.at[slot]
        )

    def out_body(i, carry):
        rows_copy(i).wait()

        @pl.when(i >= slots)
        def _():
            out_copy(i - slots).wait()

        product = dot(rows[pl.ds(i * block, block)].reshape(block * n, wide), table[...])
        out_v[lax.rem(i, slots)] = product.astype(BF16).reshape(block, n, side)
        out_copy(i).start()
        return carry

    def in_copy(i):
        slot = lax.rem(i, back_slots)
        return pltpu.make_async_copy(
            back_v.at[slot],
            out_back.at[:, pl.ds(pl.multiple_of(i * STEP, STEP), STEP), :],
            back_sem.at[slot],
        )

    def in_body(i, carry):
        @pl.when(i >= back_slots)
        def _():
            in_copy(i - back_slots).wait()

        part = back[:, pl.ds(pl.multiple_of(i * STEP, STEP), STEP), :].reshape(rank * STEP, side)
        product = dot(kron[...], part)
        back_v[lax.rem(i, back_slots)] = product.astype(BF16).reshape(chan, STEP, side)
        in_copy(i).start()
        return carry

    table_copy.wait()
    lax.fori_loop(0, steps, out_body, 0)
    kron_copy.wait()
    back_copy.wait()
    for i in range(4):
        pltpu.make_async_copy(grads_in[i], grads[i], grad_sem.at[0, i]).wait()
        pltpu.make_async_copy(grads[i], grads_out[i], grad_sem.at[1, i]).start()
    lax.fori_loop(0, row_steps, in_body, 0)
    for i in range(max(steps - slots, 0), steps):
        out_copy(jnp.int32(i)).wait()
    for i in range(max(row_steps - back_slots, 0), row_steps):
        in_copy(jnp.int32(i)).wait()
    for i in range(4):
        pltpu.make_async_copy(grads[i], grads_out[i], grad_sem.at[1, i]).wait()


def local(input_field, out_cotangent, core_first, core_second, core_third, column_mode_core):
    grid_count, chan_count = lax.axis_size("grid"), lax.axis_size("chan")
    chan_index = lax.axis_index("chan")
    chan, rows, side = input_field.shape
    channels, rank_a = core_first.shape
    rank_b, modes_x, rank_d = core_third.shape
    modes_y = column_mode_core.shape[2]
    wide = 2 * modes_y
    half = modes_x // 2
    both = 2 * chan
    pairs = rank_a * rank_b

    table_np = width_table(side, modes_y)
    table = jnp.asarray(table_np)
    table_t = jnp.asarray(np.ascontiguousarray(table_np.T))
    turns = turn_table(side, modes_x).reshape(2, modes_x, grid_count, rows)
    turns = jnp.asarray(np.ascontiguousarray(turns.transpose(2, 0, 1, 3)))

    first_t = core_first.T
    second = core_second.transpose(0, 2, 1).reshape(pairs, channels)
    if both % LANES:
        second = lax.dynamic_slice_in_dim(second, chan_index // 2 * both, both, 1)
    third = core_third.transpose(0, 2, 1)
    anywhere = pl.BlockSpec(memory_space=pl.ANY)

    row_steps = rows // STEP
    planes, stacks = chan_count, grid_count // 2
    tiles = 2 * half
    owners = planes * stacks
    grad_tiles = (pairs // 2 * channels + rank_d * rank_b * half + rank_d * wide) // (STEP * LANES)
    grad_tiles += -grad_tiles % planes
    sub = STEP
    subs = chan // sub
    slots = min(SLOTS, 2 * subs)
    blocks = subs
    fold = rows == pairs // 2 and side == 4 * wide and slots * sub >= half // 2
    outer_shape = (1, 1, 16, LANES) if fold else (1, half // 2, pairs, 2 * wide)
    parts = 2 if tiles % (2 * owners) == 0 else 1
    row_groups = rows // STEP
    wide_y = max(sub * modes_y, row_groups * wide)
    groups = half // STEP
    peers = max(planes, stacks) - 1
    steps = chan // 8

    def reduce_buffers(count, shape, dtype, lead=()):
        chunk = count // planes
        return [
            pltpu.VMEM((*lead, planes - 1, chunk, *shape), dtype),
            pltpu.VMEM((*lead, stacks, chunk, *shape), dtype),
        ]

    tile = (rank_a, modes_y)
    scratch = [
        pltpu.VMEM((slots, sub, rows, side), BF16),
        pltpu.VMEM((chan * STEP, rank_a * STEP), BF16),
        pltpu.VMEM((side, wide), BF16),
        pltpu.VMEM((rank_a, rows, wide), BF16),
        pltpu.VMEM((pairs, 2 * wide), BF16),
        pltpu.VMEM((pairs, 2 * wide), BF16),
        pltpu.VMEM((chan, rows, wide), BF16),
        pltpu.VMEM((max(2 * rows, sub * STEP), wide_y), BF16),
        pltpu.VMEM((STEP, 2 * modes_x, modes_y), F32),
        pltpu.VMEM((blocks, modes_x, STEP, wide), BF16),
        pltpu.VMEM((half, both, wide), BF16),
        pltpu.VMEM((groups, 2, STEP, both * modes_y), BF16),
        pltpu.VMEM((2, modes_x, chan * modes_y), BF16),
        pltpu.VMEM((2, modes_x, rows), BF16),
        pltpu.VMEM((2 * modes_x, 2 * rows), BF16),
        pltpu.VMEM((2 * rows, 2 * modes_x), BF16),
        pltpu.VMEM((rank_a * STEP, chan * STEP), BF16),
        pltpu.VMEM((rank_a * STEP, row_groups * wide), F32),
        pltpu.VMEM((pairs, both), BF16),
        pltpu.VMEM((pairs, both), BF16),
        pltpu.VMEM((both, pairs), BF16),
        pltpu.VMEM((half, rank_b, wide), F32),
        pltpu.VMEM((half, rank_a, wide), F32),
        pltpu.VMEM((half * rank_b, wide), F32),
        pltpu.VMEM(outer_shape, BF16),
        pltpu.VMEM((STEP, max(both, modes_x), wide), F32),
        pltpu.VMEM((pairs, both), F32),
        pltpu.VMEM((2 * modes_x, rank_a * modes_y), BF16),
        pltpu.VMEM((chan * STEP, rank_a * STEP), F32),
        pltpu.VMEM((modes_x, 2, *tile), BF16),
        pltpu.VMEM((half, 2, *tile), BF16),
        pltpu.VMEM((tiles, *tile), BF16),
        pltpu.VMEM((tiles, *tile), BF16),
        *reduce_buffers(tiles // parts, tile, BF16, (parts,)),
        pltpu.VMEM((tiles, *tile), BF16),
        pltpu.VMEM((2, tiles, *tile), BF16),
        *reduce_buffers(tiles // parts, tile, BF16, (parts,)),
        pltpu.VMEM((pairs // 2, both), F32),
        pltpu.VMEM((grad_tiles, STEP, LANES), BF16),
        pltpu.VMEM((2, grad_tiles, STEP, LANES), BF16),
        *reduce_buffers(grad_tiles, (STEP, LANES), BF16),
        pltpu.VMEM((2, rank_a, channels), F32),
        pltpu.VMEM((planes, rank_a, channels), F32),
        pltpu.VMEM((stacks, rank_a, channels), F32),
        *[pltpu.SemaphoreType.DMA((parts, 4, peers))] * 4,
        *[pltpu.SemaphoreType.DMA((3, peers))] * 2,
        *[pltpu.SemaphoreType.DMA((5 + parts,))] * 2,
        *[pltpu.SemaphoreType.DMA((blocks,))] * 2,
        *[pltpu.SemaphoreType.DMA((groups,))] * 2,
        *[pltpu.SemaphoreType.DMA((2, peers))] * 2,
        pltpu.SemaphoreType.DMA((slots,)),
        pltpu.SemaphoreType.DMA((4,)),
        pltpu.SemaphoreType.DMA((steps,)),
        pltpu.SemaphoreType.DMA((rank_a // 4,)),
    ]
    vmem = pl.BlockSpec(memory_space=pltpu.VMEM)
    out_rows, back_rows, kron, g_first, g_second, g_third, g_fourth = pl.pallas_call(
        spectral_kernel,
        in_specs=[anywhere] * 4 + [vmem] * 4,
        out_specs=[anywhere] * 3 + [vmem] * 4,
        out_shape=[
            jax.ShapeDtypeStruct((chan, rows, wide), BF16),
            jax.ShapeDtypeStruct((rank_a, rows, side), BF16),
            jax.ShapeDtypeStruct((chan * STEP, rank_a * STEP), BF16),
            jax.ShapeDtypeStruct((rank_a, channels), F32),
            jax.ShapeDtypeStruct((pairs, channels), F32),
            jax.ShapeDtypeStruct((rank_b, rank_d, modes_x), F32),
            jax.ShapeDtypeStruct((2, rank_d, modes_y), F32),
        ],
        scratch_shapes=scratch,
        compiler_params=pltpu.CompilerParams(
            collective_id=0, has_side_effects=True, vmem_limit_bytes=63 * 2**20
        ),
        name="spectral",
    )(input_field, out_cotangent, turns, table, first_t, second, third, column_mode_core)

    out_step = min(chan, 8)
    out_steps = chan // out_step
    out_slots, back_slots = min(4, out_steps), min(4, row_steps)
    grads = [
        (rank_a, channels), (pairs, channels), (rank_b, rank_d, modes_x), (2, rank_d, modes_y)
    ]
    output_field, input_grad, g_first, g_second, g_third, g_fourth = pl.pallas_call(
        output_kernel,
        in_specs=[anywhere] * 8,
        out_specs=[anywhere] * 6,
        out_shape=[
            jax.ShapeDtypeStruct((chan, rows, side), BF16),
            jax.ShapeDtypeStruct((chan, rows, side), BF16),
            *[jax.ShapeDtypeStruct(shape, F32) for shape in grads],
        ],
        scratch_shapes=[
            pltpu.VMEM((wide, side), BF16),
            pltpu.VMEM((chan, rows, wide), BF16),
            pltpu.VMEM((rank_a, rows, side), BF16),
            pltpu.VMEM((out_slots, out_step, rows, side), BF16),
            pltpu.VMEM((back_slots, chan, STEP, side), BF16),
            pltpu.VMEM((chan * STEP, rank_a * STEP), BF16),
            *[pltpu.VMEM(shape, F32) for shape in grads],
            pltpu.SemaphoreType.DMA((3,)),
            pltpu.SemaphoreType.DMA((out_steps,)),
            pltpu.SemaphoreType.DMA((2, 4)),
            pltpu.SemaphoreType.DMA((out_slots,)),
            pltpu.SemaphoreType.DMA((back_slots,)),
        ],
        compiler_params=params(60),
        name="output",
    )(table_t, out_rows, back_rows, kron, g_first, g_second, g_third, g_fourth)

    return (
        output_field,
        input_grad,
        g_first.T,
        g_second.reshape(rank_a, rank_b, channels).transpose(0, 2, 1),
        g_third.transpose(0, 2, 1),
        g_fourth,
    )


def solution(mesh):
    placed = (P("chan", "grid", None), P("chan", "grid", None), P(), P(), P(), P())
    return jax.shard_map(
        local,
        mesh=mesh,
        in_specs=placed,
        out_specs=(P("chan", "grid", None), P("chan", "grid", None), P(), P(), P(), P()),
        check_vma=False,
    )
```

```python
import math

import jax
import jax.numpy as jnp
import numpy as np
from jax import lax
from jax.experimental import pallas as pl
from jax.experimental.pallas import tpu as pltpu
from jax.sharding import PartitionSpec as P

F32 = jnp.float32
BF16 = jnp.bfloat16
HI = lax.Precision.HIGHEST
STEP = 16
LANES = 128
SLOTS = 3
MESH = pl.DeviceIdType.MESH


def params(mib=48):
    return pltpu.CompilerParams(vmem_limit_bytes=mib * 2**20)


def dot(a, b, precision=None):
    return jnp.dot(a, b, preferred_element_type=F32, precision=precision)


def dot_nt(a, b, precision=None):
    return lax.dot_general(
        a, b, (((1,), (1,)), ((), ())), preferred_element_type=F32, precision=precision
    )


def dot_tn(a, b, precision=None):
    return lax.dot_general(
        a, b, (((0,), (0,)), ((), ())), preferred_element_type=F32, precision=precision
    )


def width_table(side, modes_y):
    phase = np.arange(side)[:, None] * np.arange(modes_y)[None, :] % side
    angle = phase.astype(np.float32) * np.float32(2.0 * math.pi / side)
    return np.concatenate([np.cos(angle), -np.sin(angle)], axis=1).astype(BF16)


def turn_table(side, modes_x):
    kx = np.arange(modes_x)
    freq = np.where(kx < modes_x // 2, kx, side - modes_x + kx)
    phase = freq[:, None] * np.arange(side)[None, :] % side
    angle = phase.astype(np.float32) * np.float32(2.0 * math.pi / side)
    return np.stack([np.cos(angle), np.sin(angle)]).astype(BF16)


def one_hot(rows, cols, offset):
    row = lax.broadcasted_iota(jnp.int32, (rows, cols), 0)
    col = lax.broadcasted_iota(jnp.int32, (rows, cols), 1)
    return col == row + offset


def spread(values, rows, n, offset=0):
    lane = lax.broadcasted_iota(jnp.int32, (values.shape[1], n * STEP), 1)
    row = lax.broadcasted_iota(jnp.int32, (values.shape[1], n * STEP), 0)
    wide = dot(values, (lane // STEP + offset == row).astype(BF16))
    at = lax.broadcasted_iota(jnp.int32, (STEP, n * STEP), 1) % STEP
    unit = (at == lax.broadcasted_iota(jnp.int32, (STEP, n * STEP), 0)).astype(F32)
    return (wide[:, None, :] * unit[None]).reshape(rows * STEP, n * STEP).astype(BF16)


def flip(index, bits):
    bit = 1
    while bit <= bits:
        if bits & bit:
            index = index + bit * (1 - 2 * (index // bit % 2))
        bit *= 2
    return index


class Place:
    def __init__(self):
        self.grid, self.chan = lax.axis_index("grid"), lax.axis_index("chan")
        self.core = self.chan % 2
        self.planes = lax.axis_size("chan")
        self.stacks = lax.axis_size("grid") // 2
        self.plane = self.chan // 2 * 2 + self.grid % 2
        self.stack = self.grid // 2

    def across_core(self):
        return {"grid": self.grid, "chan": flip(self.chan, 1)}

    def across_plane(self, s):
        return {"grid": flip(self.grid, s % 2), "chan": flip(self.chan, s // 2 * 2)}

    def across_stack(self, s):
        return {"grid": flip(self.grid, s * 2), "chan": self.chan}

    def peers(self):
        return (
            [self.across_core()]
            + [self.across_plane(s) for s in range(1, self.planes)]
            + [self.across_stack(s) for s in range(1, self.stacks)]
        )


def remote(src, dst, send, recv, peer):
    return pltpu.make_async_remote_copy(
        src_ref=src, dst_ref=dst, send_sem=send, recv_sem=recv,
        device_id=peer, device_id_type=MESH,
    )


class Reduce:
    def __init__(self, place, source, result, land_plane, land_stack, send, recv):
        self.at, self.source, self.result = place, source, result
        self.land_plane, self.land_stack = land_plane, land_stack
        self.send, self.recv = send, recv
        self.chunk = source.shape[0] // place.planes

    def plane_copy(self, s):
        there = flip(self.at.plane, s)
        return remote(
            self.source.at[pl.ds(there * self.chunk, self.chunk)],
            self.land_plane.at[s - 1],
            self.send.at[0, s - 1], self.recv.at[0, s - 1], self.at.across_plane(s),
        )

    def plane_send(self):
        for s in range(1, self.at.planes):
            self.plane_copy(s).start()

    def plane_wait(self):
        for s in range(1, self.at.planes):
            self.plane_copy(s).wait()
        total = self.source[pl.ds(self.at.plane * self.chunk, self.chunk)].astype(F32)
        for s in range(1, self.at.planes):
            total = total + self.land_plane[s - 1].astype(F32)
        self.keep(total)

    def keep(self, total):
        self.land_stack[self.at.stack] = total.astype(self.land_stack.dtype)

    def stack_copy(self, s):
        mine = self.land_stack.at[self.at.stack]
        return remote(
            mine, mine, self.send.at[1, s - 1], self.recv.at[1, s - 1], self.at.across_stack(s)
        )

    def stack_send(self):
        for s in range(1, self.at.stacks):
            self.stack_copy(s).start()

    def stack_wait(self):
        for s in range(1, self.at.stacks):
            self.stack_copy(s).wait()
        total = self.land_stack[0].astype(F32)
        for s in range(1, self.at.stacks):
            total = total + self.land_stack[s].astype(F32)
        here = pl.ds(self.at.plane * self.chunk, self.chunk)
        self.result[here] = total.astype(self.result.dtype)

    def plane_back_copy(self, s):
        here = pl.ds(self.at.plane * self.chunk, self.chunk)
        return remote(
            self.result.at[here], self.result.at[here],
            self.send.at[2, s - 1], self.recv.at[2, s - 1], self.at.across_plane(s),
        )

    def plane_back_send(self):
        for s in range(1, self.at.planes):
            self.plane_back_copy(s).start()

    def plane_back_wait(self):
        for s in range(1, self.at.planes):
            self.plane_back_copy(s).wait()


class ScatterReduce(Reduce):
    def __init__(self, place, source, result, land_plane, land_stack, send, recv):
        super().__init__(place, source, result, land_plane, land_stack, send, recv)
        self.piece = self.chunk // place.stacks
        self.mid = land_stack.at[0]
        self.land_stack = [
            land_stack.at[1 + s // place.stacks, pl.ds(s % place.stacks * self.piece, self.piece)]
            for s in range(place.stacks - 1)
        ]

    def keep(self, total):
        self.mid[...] = total.astype(self.mid.dtype)

    def stack_copy(self, s):
        there = flip(self.at.stack, s)
        return remote(
            self.mid.at[pl.ds(there * self.piece, self.piece)],
            self.land_stack[s - 1],
            self.send.at[1, s - 1], self.recv.at[1, s - 1], self.at.across_stack(s),
        )

    def stack_send(self):
        for s in range(1, self.at.stacks):
            self.stack_copy(s).start()

    def own(self):
        return pl.ds(self.at.plane * self.chunk + self.at.stack * self.piece, self.piece)

    def stack_wait(self):
        for s in range(1, self.at.stacks):
            self.stack_copy(s).wait()
        total = self.mid[pl.ds(self.at.stack * self.piece, self.piece)].astype(F32)
        for s in range(1, self.at.stacks):
            total = total + self.land_stack[s - 1][...].astype(F32)
        self.result[self.own()] = total.astype(self.result.dtype)

    def stack_back_copy(self, s):
        return remote(
            self.result.at[self.own()], self.result.at[self.own()],
            self.send.at[3, s - 1], self.recv.at[3, s - 1], self.at.across_stack(s),
        )

    def stack_back_send(self):
        for s in range(1, self.at.stacks):
            self.stack_back_copy(s).start()

    def stack_back_wait(self):
        for s in range(1, self.at.stacks):
            self.stack_back_copy(s).wait()


def spectral_kernel(
    field, cot, turns_in, table_in, first_t, second, third, column,
    rows_out, back_out, kron_out, g_first, g_second, g_third, g_fourth,
    block_v, kron_back, table, back_rows, outer_a, outer_b, modes_v, y, held, spec_stage, spec, s_stage, spec_out, cs, csf, csb, kron, mixed,
    by_ab, by_ba, by_t, kern, lead_f, kgrad, outer, held_o, part_second, back_in, total,
    lead_v, lead_core, lead_x, lead_res, lead_lp, lead_ls,
    lg_x, lg_all, lg_lp, lg_ls,
    gp_core, gp_x, gp_all, gp_lp, gp_ls,
    f_core, f_plane, f_stack,
    lead_send, lead_recv, lg_send, lg_recv, gp_send, gp_recv,
    core_send, core_recv, spec_send, spec_recv, out_send, out_recv, f_send, f_recv,
    block_sem, turns_sem, rows_sem, wide_sem,
):
    if outer.shape[0] * outer.shape[1] * 2 < kern.shape[0]:
        outer = block_v
    at = Place()
    core = at.core
    other = 1 - core
    chan, n, side = cot.shape
    wide = table.shape[1]
    my = wide // 2
    mx = cs.shape[1]
    half = mx // 2
    ra, rb, rd = first_t.shape[0], third.shape[0], third.shape[1]
    pairs = ra * rb
    both = 2 * chan
    channels = g_first.shape[1]
    slots, sub = block_v.shape[:2]
    subs = chan // sub
    parts = lead_lp.shape[0]
    row_groups = n // STEP
    lane = lax.broadcasted_iota(jnp.int32, (1, wide), 1)
    weight = jnp.where(lane % my == 0, 1.0, 2.0) * (1.0 / side)
    partner = at.across_core()

    def block_copy(source, j, k):
        slot = lax.rem(k, slots)
        return pltpu.make_async_copy(
            source.at[pl.ds(j * sub, sub)], block_v.at[slot], block_sem.at[slot]
        )

    def fetch(k):
        @pl.when(k < subs)
        def _():
            block_copy(field, k, k).start()

        @pl.when(jnp.logical_and(k >= subs, k < 2 * subs))
        def _():
            block_copy(cot, k - subs, k).start()

    def rows_of_block(source, j, k):
        block_copy(source, j, k).wait()
        block = block_v[lax.rem(k, slots)].reshape(sub * n, side)
        product = dot(block, table[...]).astype(BF16)
        fetch(k + slots)
        return product

    barrier = pltpu.get_barrier_semaphore()
    peers = at.peers()
    for peer in peers:
        pl.semaphore_signal(barrier, inc=1, device_id=peer, device_id_type=MESH)
    table_copy = pltpu.make_async_copy(table_in, table, turns_sem.at[1])
    table_copy.start()
    for k in range(min(slots, 2 * subs)):
        if k < subs:
            block_copy(field, k, k).start()
        else:
            block_copy(cot, k - subs, k).start()
    turns_copy = pltpu.make_async_copy(turns_in.at[at.grid], cs, turns_sem.at[0])
    turns_copy.start()
    kron[...] = spread(first_t[...].astype(BF16), ra, chan, at.chan * chan)
    table_copy.wait()

    mixed[...] = jnp.zeros_like(mixed)

    def field_body(i, carry):
        product = rows_of_block(field, i, i)
        shaped = product.reshape(sub, n, wide)
        modes_v[pl.ds(i * sub, sub)] = shaped
        for g in range(row_groups):
            y[: sub * STEP, g * wide : (g + 1) * wide] = shaped[
                :, g * STEP : (g + 1) * STEP
            ].reshape(sub * STEP, wide)
        part = pl.ds(pl.multiple_of(i * sub * STEP, sub * STEP), sub * STEP)
        mixed[...] += dot(kron[:, part], y[: sub * STEP, : row_groups * wide])
        return carry

    lax.fori_loop(0, subs, field_body, 0)
    turns_copy.wait()
    c, s = cs[0], cs[1]
    csf[:mx, :n], csf[:mx, n:], csf[mx:, :n], csf[mx:, n:] = c, s, -s, c
    ct = jnp.swapaxes(c.astype(F32), 0, 1).astype(BF16)
    st = jnp.swapaxes(s.astype(F32), 0, 1).astype(BF16)
    csb[:n, :mx], csb[:n, mx:], csb[n:, :mx], csb[n:, mx:] = ct, -st, st, ct
    for g in range(row_groups):
        for q in range(2):
            for a in range(ra):
                back_in[q * n + g * STEP : q * n + (g + 1) * STEP, a * my : (a + 1) * my] = mixed[
                    a * STEP : (a + 1) * STEP, g * wide + q * my : g * wide + (q + 1) * my
                ].astype(BF16)
    z = dot(csf[...], back_in[: 2 * n]) * (1.0 / side)
    for a in range(ra):
        held[a] = z[:, a * my : (a + 1) * my]
    turned = jnp.swapaxes(held[...], 0, 1).astype(BF16)
    lead_v[:, 0] = turned[:mx]
    lead_v[:, 1] = turned[mx:]

    def lead_core_copy():
        return remote(
            lead_v.at[pl.ds(other * half, half)], lead_core,
            core_send.at[0], core_recv.at[0], partner,
        )

    pl.semaphore_wait(barrier, len(peers))
    lead_core_copy().start()

    if second.shape[1] > both and both % LANES == 0:
        sec = second[:, pl.ds(pl.multiple_of(at.chan // 2 * both, both), both)]
    else:
        sec = second[...]
    by_ab[...] = sec.astype(BF16)
    by_ba[...] = jnp.swapaxes(sec.reshape(ra, rb, both), 0, 1).reshape(pairs, both).astype(BF16)
    by_t[...] = jnp.swapaxes(sec, 0, 1).astype(BF16)
    col = jnp.concatenate([column[0], column[1]], axis=1)
    for b in range(rb):
        held_o[b, :mx] = dot_tn(third[b], col, HI)
    own_half = pl.ds(pl.multiple_of(core * half, half), half)
    kern[...] = jnp.swapaxes(held_o[:, own_half, :], 0, 1)

    split = parts > 1

    def sums(kind, source, result, land_plane, land_stack, send, recv):
        share = source.shape[0] // parts
        made = []
        for p in range(parts):
            where = pl.ds(p * share, share)
            made.append(kind(
                at, source.at[where], result(where), land_plane.at[p], land_stack.at[p],
                send.at[p], recv.at[p],
            ))
        return made

    lead_sums = sums(
        Reduce, lead_x, lambda w: lead_res.at[w], lead_lp, lead_ls, lead_send, lead_recv
    )
    lg_sums = sums(
        ScatterReduce if split else Reduce, lg_x, lambda w: lg_all.at[core, w], lg_lp, lg_ls, lg_send, lg_recv
    )
    gp_sum = Reduce(at, gp_x, gp_all.at[core], gp_lp, gp_ls, gp_send, gp_recv)

    lead_core_copy().wait()
    mine = lead_v[pl.ds(core * half, half)].astype(F32) + lead_core[...].astype(F32)
    lead_x[...] = mine.reshape(lead_x.shape).astype(BF16)
    lead_sums[0].plane_send()

    def plan(hooks, index):
        for when, todo in hooks:
            @pl.when(index == when)
            def _():
                for step in todo:
                    step()

    def spec_copy(i):
        return remote(
            spec_stage.at[i, pl.ds(other * half, half)],
            spec.at[:, pl.ds(core * chan + i * STEP, STEP), :],
            spec_send.at[i], spec_recv.at[i], partner,
        )

    first_lead, last_lead = lead_sums[0], lead_sums[-1]
    first_lg, last_lg = lg_sums[0], lg_sums[-1]

    def both_of(one, two):
        return [one] + ([two] if split else [])

    cot_hooks = [
        (
            min(1, subs - 1),
            [first_lead.plane_wait, first_lead.stack_send]
            + ([last_lead.plane_send] if split else []),
        ),
        (
            min(3, subs - 1),
            [last_lead.plane_wait, last_lead.stack_send] if split else [],
        ),
    ]

    def cot_body(i, carry):
        product = rows_of_block(cot, i, i + subs)
        for c in range(sub):
            for q in range(2):
                y[q * n : (q + 1) * n, c * my : (c + 1) * my] = product[
                    c * n : (c + 1) * n, q * my : (q + 1) * my
                ]
        z = dot(csf[...], y[: 2 * n, : sub * my])
        for c in range(sub):
            held[c] = z[:, c * my : (c + 1) * my] * weight[:, :my]
        turned = jnp.swapaxes(held[...], 0, 1).astype(BF16)
        spec_stage[i, :, :, :my] = turned[:mx]
        spec_stage[i, :, :, my:] = turned[mx:]
        spec_copy(i).start()
        spec[:, pl.ds(pl.multiple_of(core * chan + i * STEP, STEP), STEP), :] = spec_stage[
            i, pl.ds(core * half, half)
        ]

        plan(cot_hooks, i)
        return carry

    lax.fori_loop(0, subs, cot_body, 0)
    for i in range(subs):
        spec_copy(i).wait()

    unroll = 4

    def back_body(j, carry):
        for u in range(unroll):
            k = j * unroll + u
            g = dot(by_ba[...], spec[k])
            re = jnp.zeros((ra, my), F32)
            im = jnp.zeros((ra, my), F32)
            for b in range(rb):
                gre = g[b * ra : (b + 1) * ra, :my]
                gim = g[b * ra : (b + 1) * ra, my:]
                kre, kim = kern[k, b : b + 1, :my], kern[k, b : b + 1, my:]
                re += gre * kre + gim * kim
                im += gim * kre - gre * kim
            lg_x[2 * k] = re.astype(BF16)
            lg_x[2 * k + 1] = im.astype(BF16)

        plan(back_hooks, j)
        return carry

    rounds = half // unroll
    back_hooks = []
    if split:
        back_hooks = [
            (rounds * 6 // 16, [first_lead.stack_wait, first_lead.plane_back_send]),
            (rounds * 11 // 16, [first_lg.plane_send]),
        ]
    lax.fori_loop(0, rounds, back_body, 0)
    last_lead.stack_wait()
    last_lead.plane_back_send()
    last_lg.plane_send()
    part_second[...] = jnp.zeros_like(part_second)

    per = 2
    folded = outer.shape[1] != half // per

    def outer_put(j, a, lanes, value):
        row = a * rb
        if folded:
            lanes += row // (pairs // 2) * per * wide
            row %= pairs // 2
        outer[j // outer.shape[1], j % outer.shape[1], row : row + rb, lanes : lanes + my] = value

    def outer_get(j, lanes, size):
        slab = outer.at[j // outer.shape[1], j % outer.shape[1]]
        if not folded:
            return slab[:, lanes : lanes + size]
        low = slab[:, lanes : lanes + size]
        high = slab[:, per * wide + lanes : per * wide + lanes + size]
        return jnp.concatenate([low, high], axis=0)

    outer_b[...] = jnp.zeros_like(outer_b)

    def add_second(kept, j):
        rhs = jnp.concatenate([spec[j * per + u] for u in range(per)], axis=1)
        part_second[...] += dot_nt(kept[...], rhs)

    def products(j, kept):
        for u in range(per):
            k = j * per + u
            g = dot(by_ab[...], spec[k])
            kr = kern[k]
            kre, kim = kr[:, :my], kr[:, my:]
            re = jnp.zeros((rb, my), F32)
            im = jnp.zeros((rb, my), F32)
            for a in range(ra):
                rows = slice(a * rb, (a + 1) * rb)
                lre, lim = lead_f[k, a : a + 1, :my], lead_f[k, a : a + 1, my:]
                ore = (kre * lre - kim * lim).astype(BF16)
                oim = (kre * lim + kim * lre).astype(BF16)
                kept[rows, u * wide : u * wide + my] = ore
                kept[rows, u * wide + my : (u + 1) * wide] = oim
                outer_put(j, a, u * wide, ore)
                outer_put(j, a, u * wide + my, oim)
                gre, gim = g[rows, :my], g[rows, my:]
                re += gre * lre + gim * lim
                im += gim * lre - gre * lim
            at_k = pl.ds(pl.multiple_of(k * rb, rb), rb)
            kgrad[at_k, :my] = re
            kgrad[at_k, my:] = im

    def mix_body(i, carry):
        add_second(outer_b, jnp.maximum(2 * i - 1, 0))
        products(2 * i, outer_a)
        add_second(outer_a, 2 * i)
        products(2 * i + 1, outer_b)
        plan(mix_hooks, i)
        return carry

    turns_of_part = half // per // parts // 2
    tp = turns_of_part
    if split:
        mix_hooks = [
            (tp * 6 // 8, [first_lg.plane_wait, first_lg.stack_send]),
            (tp + tp // 8, [last_lg.plane_wait, last_lg.stack_send]),
            (tp + tp * 3 // 8, [first_lg.stack_wait, first_lg.stack_back_send]),
            (tp + tp * 5 // 8, [last_lg.stack_wait, last_lg.stack_back_send]),
            (tp + tp * 7 // 8, [first_lg.stack_back_wait, first_lg.plane_back_send]),
        ]
    else:
        mix_hooks = [
            (tp // 4, [last_lg.plane_wait, last_lg.stack_send]),
            (tp * 7 // 8, [last_lg.stack_wait, last_lg.plane_back_send]),
        ]
    for p in range(parts):
        share = half // parts
        lead_sums[p].plane_back_wait()
        where = pl.ds(p * 2 * share, 2 * share)
        got = lead_res[where].reshape(share, 2, ra, my).astype(F32)
        lead_f[p * share : (p + 1) * share, :, :my] = got[:, 0]
        lead_f[p * share : (p + 1) * share, :, my:] = got[:, 1]
        lax.fori_loop(p * turns_of_part, (p + 1) * turns_of_part, mix_body, 0)
    add_second(outer_b, half // per - 1)

    def second_copy():
        return remote(
            part_second.at[pl.ds(other * (pairs // 2), pairs // 2)], gp_core,
            core_send.at[1], core_recv.at[1], partner,
        )

    def back_copy(p):
        where = pl.ds(p * (lg_all.shape[1] // parts), lg_all.shape[1] // parts)
        return remote(
            lg_all.at[core, where], lg_all.at[core, where],
            core_send.at[5 + p], core_recv.at[5 + p], partner,
        )

    second_copy().start()
    by_mode = jnp.swapaxes(kgrad[...].reshape(half, rb, wide), 0, 1).reshape(rb * half, wide)
    by_mode = by_mode.astype(BF16)
    part_third = dot_nt(col.astype(BF16), by_mode)
    third_flat = jnp.concatenate(
        [jnp.where(core == 0, third[b][:, :half], third[b][:, half:]) for b in range(rb)], axis=1
    )
    part_fourth = dot(third_flat.astype(BF16), by_mode)
    second_copy().wait()
    mine = part_second[pl.ds(core * (pairs // 2), pairs // 2)] + gp_core[...]
    if both % LANES:
        mine = dot(mine, one_hot(both, channels, at.chan // 2 * both).astype(F32), HI)
    else:
        mine = jnp.concatenate(
            [jnp.where(at.chan // 2 == p, mine, 0.0) for p in range(channels // both)], axis=1
        )

    pieces = []
    for value in (mine, part_third, part_fourth):
        for c in range(value.shape[1] // LANES):
            pieces.append((value, c))
    spots, count = [], 0
    for value, c in pieces:
        tiles = value.shape[0] // STEP
        gp_x[count : count + tiles] = value[:, c * LANES : (c + 1) * LANES].astype(BF16).reshape(
            tiles, STEP, LANES
        )
        spots.append((count, tiles))
        count += tiles
    if count < gp_x.shape[0]:
        gp_x[count:] = jnp.zeros((gp_x.shape[0] - count, STEP, LANES), BF16)
    gp_sum.plane_send()
    if split:
        last_lg.stack_back_wait()
        last_lg.plane_back_send()
    pick = one_hot(chan, channels, at.chan * chan).astype(BF16)
    first_bf = dot_nt(pick, first_t[...].astype(BF16)).astype(BF16)
    kron_back[...] = spread(first_bf, chan, ra)
    kron_copy = pltpu.make_async_copy(kron_back, kron_out, turns_sem.at[3])
    kron_copy.start()

    groups = half // STEP

    def out_copy(g):
        return remote(
            s_stage.at[g, :, :, pl.ds(other * chan * my, chan * my)],
            spec_out.at[:, pl.ds(core * half + g * STEP, STEP), :],
            out_send.at[g], out_recv.at[g], partner,
        )

    def out_body(g, carry):
        for j in range(STEP // per):
            for u in range(per):
                held_o[j * per + u, :both] = dot(
                    by_t[...], outer_get(g * (STEP // per) + j, u * wide, wide)
                )
        turned = jnp.swapaxes(held_o[:, :both], 0, 1).astype(BF16)
        for o in range(both):
            for q in range(2):
                s_stage[g, q, :, o * my : (o + 1) * my] = turned[o, :, q * my : (q + 1) * my]
        out_copy(g).start()
        row = pl.ds(pl.multiple_of(core * half + g * STEP, STEP), STEP)
        lanes = pl.ds(pl.multiple_of(core * chan * my, chan * my), chan * my)
        spec_out[:, row, :] = s_stage[g, :, :, lanes]

        @pl.when(g == groups // 2)
        def _():
            gp_sum.plane_wait()
            gp_sum.stack_send()

        if split:
            @pl.when(g == groups - 1)
            def _():
                first_lg.plane_back_wait()
                back_copy(0).start()

        return carry

    lax.fori_loop(0, groups, out_body, 0)
    last_lg.plane_back_wait()
    back_copy(parts - 1).start()
    share = half // parts
    for p in range(parts):
        back_copy(p).wait()
        for h in range(2):
            got = lg_all[h, p * 2 * share : (p + 1) * 2 * share].reshape(share, 2, ra, my)
            for q in range(2):
                turned = jnp.swapaxes(got[:, q].astype(F32), 0, 1).astype(BF16)
                row = q * mx + h * half + p * share
                for a in range(ra):
                    back_in[row : row + share, a * my : (a + 1) * my] = turned[a]
    r = dot(csb[...], back_in[...]).astype(BF16)
    for a in range(ra):
        for q in range(2):
            back_rows[a, :, q * my : (q + 1) * my] = r[
                q * n : (q + 1) * n, a * my : (a + 1) * my
            ]
    total[...] = jnp.zeros_like(total)

    def first_body(i, carry):
        row = pl.ds(pl.multiple_of(i * STEP, STEP), STEP)
        block = back_rows[:, row, :].reshape(ra * STEP, wide)
        total[...] += dot_nt(modes_v[:, row, :].reshape(chan * STEP, wide), block)
        return carry

    lax.fori_loop(0, n // STEP, first_body, 0)
    shape = (STEP, ra * STEP)
    unit = lax.broadcasted_iota(jnp.int32, shape, 1) % STEP == lax.broadcasted_iota(
        jnp.int32, shape, 0
    )
    kept = total[...].reshape(chan, STEP, ra * STEP) * unit.astype(F32)[None]
    lane_f = lax.broadcasted_iota(jnp.int32, (ra, ra * STEP), 1)
    row_f = lax.broadcasted_iota(jnp.int32, (ra, ra * STEP), 0)
    pick = (lane_f // STEP == row_f).astype(F32)
    part_first = dot_nt(pick, jnp.sum(kept, axis=1), HI)
    f_core[core] = dot(part_first, one_hot(chan, channels, at.chan * chan).astype(F32), HI)

    def first_core_copy():
        return remote(f_core.at[core], f_core.at[core], core_send.at[3], core_recv.at[3], partner)

    def first_plane_copy(s):
        return remote(
            f_plane.at[at.plane], f_plane.at[at.plane],
            f_send.at[0, s - 1], f_recv.at[0, s - 1], at.across_plane(s),
        )

    def first_stack_copy(s):
        return remote(
            f_stack.at[at.stack], f_stack.at[at.stack],
            f_send.at[1, s - 1], f_recv.at[1, s - 1], at.across_stack(s),
        )

    def first_plane():
        first_core_copy().wait()
        f_plane[at.plane] = f_core[0] + f_core[1]
        for s in range(1, at.planes):
            first_plane_copy(s).start()

    def first_stack():
        for s in range(1, at.planes):
            first_plane_copy(s).wait()
        value = f_plane[0]
        for s in range(1, at.planes):
            value = value + f_plane[s]
        f_stack[at.stack] = value
        for s in range(1, at.stacks):
            first_stack_copy(s).start()

    first_core_copy().start()
    for g in range(groups):
        out_copy(g).wait()

    turns = 8

    def rows_copy(i):
        where = pl.ds(i * turns, turns)
        return pltpu.make_async_copy(modes_v.at[where], rows_out.at[where], rows_sem.at[i])

    def rows_body(i, carry):
        lanes = pl.ds(pl.multiple_of(i * turns * my, turns * my), turns * my)
        r = dot(csb[...], spec_out[:, :, lanes].reshape(2 * mx, turns * my))
        for c in range(turns):
            for q in range(2):
                part = r[q * n : (q + 1) * n, c * my : (c + 1) * my] * weight[:, :my]
                modes_v[i * turns + c, :, q * my : (q + 1) * my] = part.astype(BF16)
        rows_copy(i).start()

        @pl.when(i == steps // 4)
        def _():
            first_plane()

        @pl.when(i == steps * 5 // 8)
        def _():
            gp_sum.stack_wait()
            gp_sum.plane_back_send()

        return carry

    steps = chan // turns
    lax.fori_loop(0, steps, rows_body, 0)
    first_stack()

    def wide_copy(i):
        where = pl.ds(i * 4, 4)
        return pltpu.make_async_copy(block_v.at[0, where], back_out.at[where], wide_sem.at[i])

    def wide_body(i, carry):
        part = back_rows[pl.ds(i * 4, 4)].reshape(4 * n, wide)
        product = dot_nt(part, table[...]) * (1.0 / side)
        block_v[0, pl.ds(i * 4, 4)] = product.astype(BF16).reshape(4, n, side)
        wide_copy(i).start()
        return carry

    lax.fori_loop(0, ra // 4, wide_body, 0)
    for s in range(1, at.stacks):
        first_stack_copy(s).wait()
    value = f_stack[0]
    for s in range(1, at.stacks):
        value = value + f_stack[s]
    g_first[...] = value * (1.0 / (side * mx))
    gp_sum.plane_back_wait()

    def grads_copy():
        return remote(gp_all.at[core], gp_all.at[core], core_send.at[4], core_recv.at[4], partner)

    grads_copy().start()
    grads_copy().wait()

    def tile(h, index):
        start, size = spots[index]
        return gp_all[h, start : start + size].reshape(size * STEP, LANES).astype(F32) * (1.0 / mx)

    cols = channels // LANES
    for h in range(2):
        for c in range(cols):
            g_second[
                h * (pairs // 2) : (h + 1) * (pairs // 2), c * LANES : (c + 1) * LANES
            ] = tile(h, c)
    low = lax.broadcasted_iota(jnp.int32, (rd, LANES), 1) < half
    for j in range(rb // 2):
        t0, t1 = tile(0, cols + j), tile(1, cols + j)
        g_third[2 * j] = jnp.where(low, t0, pltpu.roll(t1, half, 1))
        g_third[2 * j + 1] = jnp.where(low, pltpu.roll(t0, half, 1), t1)
    for q in range(2):
        g_fourth[q] = tile(0, cols + rb // 2 + q) + tile(1, cols + rb // 2 + q)
    for i in range(steps):
        rows_copy(i).wait()
    kron_copy.wait()
    for i in range(ra // 4):
        wide_copy(i).wait()


def output_kernel(
    table_in, rows_in, back_in, kron_in, *refs
):
    grads_in, (out, out_back), grads_out = refs[:4], refs[4:6], refs[6:10]
    table, rows, back, out_v, back_v, kron = refs[10:16]
    grads, (in_sem, rows_sem, grad_sem, out_sem, back_sem) = refs[16:20], refs[20:]
    chan, n, side = out.shape
    rank, wide = back.shape[0], rows.shape[2]
    slots, block = out_v.shape[:2]
    steps, row_steps = chan // block, n // STEP
    back_slots = back_v.shape[0]

    def rows_copy(i):
        where = pl.ds(i * block, block)
        return pltpu.make_async_copy(rows_in.at[where], rows.at[where], rows_sem.at[i])

    table_copy = pltpu.make_async_copy(table_in, table, in_sem.at[0])
    back_copy = pltpu.make_async_copy(back_in, back, in_sem.at[1])
    table_copy.start()
    for i in range(steps):
        rows_copy(i).start()
    kron_copy = pltpu.make_async_copy(kron_in, kron, in_sem.at[2])
    kron_copy.start()
    back_copy.start()
    for i in range(4):
        pltpu.make_async_copy(grads_in[i], grads[i], grad_sem.at[0, i]).start()

    def out_copy(i):
        slot = lax.rem(i, slots)
        return pltpu.make_async_copy(
            out_v.at[slot], out.at[pl.ds(i * block, block)], out_sem.at[slot]
        )

    def out_body(i, carry):
        rows_copy(i).wait()

        @pl.when(i >= slots)
        def _():
            out_copy(i - slots).wait()

        product = dot(rows[pl.ds(i * block, block)].reshape(block * n, wide), table[...])
        out_v[lax.rem(i, slots)] = product.astype(BF16).reshape(block, n, side)
        out_copy(i).start()
        return carry

    def in_copy(i):
        slot = lax.rem(i, back_slots)
        return pltpu.make_async_copy(
            back_v.at[slot],
            out_back.at[:, pl.ds(pl.multiple_of(i * STEP, STEP), STEP), :],
            back_sem.at[slot],
        )

    def in_body(i, carry):
        @pl.when(i >= back_slots)
        def _():
            in_copy(i - back_slots).wait()

        part = back[:, pl.ds(pl.multiple_of(i * STEP, STEP), STEP), :].reshape(rank * STEP, side)
        product = dot(kron[...], part)
        back_v[lax.rem(i, back_slots)] = product.astype(BF16).reshape(chan, STEP, side)
        in_copy(i).start()
        return carry

    table_copy.wait()
    lax.fori_loop(0, steps, out_body, 0)
    kron_copy.wait()
    back_copy.wait()
    for i in range(4):
        pltpu.make_async_copy(grads_in[i], grads[i], grad_sem.at[0, i]).wait()
        pltpu.make_async_copy(grads[i], grads_out[i], grad_sem.at[1, i]).start()
    lax.fori_loop(0, row_steps, in_body, 0)
    for i in range(max(steps - slots, 0), steps):
        out_copy(jnp.int32(i)).wait()
    for i in range(max(row_steps - back_slots, 0), row_steps):
        in_copy(jnp.int32(i)).wait()
    for i in range(4):
        pltpu.make_async_copy(grads[i], grads_out[i], grad_sem.at[1, i]).wait()


def local(input_field, out_cotangent, core_first, core_second, core_third, column_mode_core):
    grid_count, chan_count = lax.axis_size("grid"), lax.axis_size("chan")
    chan_index = lax.axis_index("chan")
    chan, rows, side = input_field.shape
    channels, rank_a = core_first.shape
    rank_b, modes_x, rank_d = core_third.shape
    modes_y = column_mode_core.shape[2]
    wide = 2 * modes_y
    half = modes_x // 2
    both = 2 * chan
    pairs = rank_a * rank_b

    table_np = width_table(side, modes_y)
    table = jnp.asarray(table_np)
    table_t = jnp.asarray(np.ascontiguousarray(table_np.T))
    turns = turn_table(side, modes_x).reshape(2, modes_x, grid_count, rows)
    turns = jnp.asarray(np.ascontiguousarray(turns.transpose(2, 0, 1, 3)))

    first_t = core_first.T
    second = core_second.transpose(0, 2, 1).reshape(pairs, channels)
    if both % LANES:
        second = lax.dynamic_slice_in_dim(second, chan_index // 2 * both, both, 1)
    third = core_third.transpose(0, 2, 1)
    anywhere = pl.BlockSpec(memory_space=pl.ANY)

    row_steps = rows // STEP
    planes, stacks = chan_count, grid_count // 2
    tiles = 2 * half
    owners = planes * stacks
    grad_tiles = (pairs // 2 * channels + rank_d * rank_b * half + rank_d * wide) // (STEP * LANES)
    grad_tiles += -grad_tiles % planes
    sub = STEP
    subs = chan // sub
    slots = min(SLOTS, 2 * subs)
    blocks = subs
    fold = rows == pairs // 2 and side == 4 * wide and slots * sub >= half // 2
    outer_shape = (1, 1, 16, LANES) if fold else (1, half // 2, pairs, 2 * wide)
    parts = 2 if tiles % (2 * owners) == 0 else 1
    row_groups = rows // STEP
    wide_y = max(sub * modes_y, row_groups * wide)
    groups = half // STEP
    peers = max(planes, stacks) - 1
    steps = chan // 8

    def reduce_buffers(count, shape, dtype, lead=()):
        chunk = count // planes
        return [
            pltpu.VMEM((*lead, planes - 1, chunk, *shape), dtype),
            pltpu.VMEM((*lead, stacks, chunk, *shape), dtype),
        ]

    tile = (rank_a, modes_y)
    scratch = [
        pltpu.VMEM((slots, sub, rows, side), BF16),
        pltpu.VMEM((chan * STEP, rank_a * STEP), BF16),
        pltpu.VMEM((side, wide), BF16),
        pltpu.VMEM((rank_a, rows, wide), BF16),
        pltpu.VMEM((pairs, 2 * wide), BF16),
        pltpu.VMEM((pairs, 2 * wide), BF16),
        pltpu.VMEM((chan, rows, wide), BF16),
        pltpu.VMEM((max(2 * rows, sub * STEP), wide_y), BF16),
        pltpu.VMEM((STEP, 2 * modes_x, modes_y), F32),
        pltpu.VMEM((blocks, modes_x, STEP, wide), BF16),
        pltpu.VMEM((half, both, wide), BF16),
        pltpu.VMEM((groups, 2, STEP, both * modes_y), BF16),
        pltpu.VMEM((2, modes_x, chan * modes_y), BF16),
        pltpu.VMEM((2, modes_x, rows), BF16),
        pltpu.VMEM((2 * modes_x, 2 * rows), BF16),
        pltpu.VMEM((2 * rows, 2 * modes_x), BF16),
        pltpu.VMEM((rank_a * STEP, chan * STEP), BF16),
        pltpu.VMEM((rank_a * STEP, row_groups * wide), F32),
        pltpu.VMEM((pairs, both), BF16),
        pltpu.VMEM((pairs, both), BF16),
        pltpu.VMEM((both, pairs), BF16),
        pltpu.VMEM((half, rank_b, wide), F32),
        pltpu.VMEM((half, rank_a, wide), F32),
        pltpu.VMEM((half * rank_b, wide), F32),
        pltpu.VMEM(outer_shape, BF16),
        pltpu.VMEM((STEP, max(both, modes_x), wide), F32),
        pltpu.VMEM((pairs, both), F32),
        pltpu.VMEM((2 * modes_x, rank_a * modes_y), BF16),
        pltpu.VMEM((chan * STEP, rank_a * STEP), F32),
        pltpu.VMEM((modes_x, 2, *tile), BF16),
        pltpu.VMEM((half, 2, *tile), BF16),
        pltpu.VMEM((tiles, *tile), BF16),
        pltpu.VMEM((tiles, *tile), BF16),
        *reduce_buffers(tiles // parts, tile, BF16, (parts,)),
        pltpu.VMEM((tiles, *tile), BF16),
        pltpu.VMEM((2, tiles, *tile), BF16),
        *reduce_buffers(tiles // parts, tile, BF16, (parts,)),
        pltpu.VMEM((pairs // 2, both), F32),
        pltpu.VMEM((grad_tiles, STEP, LANES), BF16),
        pltpu.VMEM((2, grad_tiles, STEP, LANES), BF16),
        *reduce_buffers(grad_tiles, (STEP, LANES), BF16),
        pltpu.VMEM((2, rank_a, channels), F32),
        pltpu.VMEM((planes, rank_a, channels), F32),
        pltpu.VMEM((stacks, rank_a, channels), F32),
        *[pltpu.SemaphoreType.DMA((parts, 4, peers))] * 4,
        *[pltpu.SemaphoreType.DMA((3, peers))] * 2,
        *[pltpu.SemaphoreType.DMA((5 + parts,))] * 2,
        *[pltpu.SemaphoreType.DMA((blocks,))] * 2,
        *[pltpu.SemaphoreType.DMA((groups,))] * 2,
        *[pltpu.SemaphoreType.DMA((2, peers))] * 2,
        pltpu.SemaphoreType.DMA((slots,)),
        pltpu.SemaphoreType.DMA((4,)),
        pltpu.SemaphoreType.DMA((steps,)),
        pltpu.SemaphoreType.DMA((rank_a // 4,)),
    ]
    vmem = pl.BlockSpec(memory_space=pltpu.VMEM)
    out_rows, back_rows, kron, g_first, g_second, g_third, g_fourth = pl.pallas_call(
        spectral_kernel,
        in_specs=[anywhere] * 4 + [vmem] * 4,
        out_specs=[anywhere] * 3 + [vmem] * 4,
        out_shape=[
            jax.ShapeDtypeStruct((chan, rows, wide), BF16),
            jax.ShapeDtypeStruct((rank_a, rows, side), BF16),
            jax.ShapeDtypeStruct((chan * STEP, rank_a * STEP), BF16),
            jax.ShapeDtypeStruct((rank_a, channels), F32),
            jax.ShapeDtypeStruct((pairs, channels), F32),
            jax.ShapeDtypeStruct((rank_b, rank_d, modes_x), F32),
            jax.ShapeDtypeStruct((2, rank_d, modes_y), F32),
        ],
        scratch_shapes=scratch,
        compiler_params=pltpu.CompilerParams(
            collective_id=0, has_side_effects=True, vmem_limit_bytes=63 * 2**20
        ),
        name="spectral",
    )(input_field, out_cotangent, turns, table, first_t, second, third, column_mode_core)

    out_step = min(chan, 8)
    out_steps = chan // out_step
    out_slots, back_slots = min(4, out_steps), min(4, row_steps)
    grads = [
        (rank_a, channels), (pairs, channels), (rank_b, rank_d, modes_x), (2, rank_d, modes_y)
    ]
    output_field, input_grad, g_first, g_second, g_third, g_fourth = pl.pallas_call(
        output_kernel,
        in_specs=[anywhere] * 8,
        out_specs=[anywhere] * 6,
        out_shape=[
            jax.ShapeDtypeStruct((chan, rows, side), BF16),
            jax.ShapeDtypeStruct((chan, rows, side), BF16),
            *[jax.ShapeDtypeStruct(shape, F32) for shape in grads],
        ],
        scratch_shapes=[
            pltpu.VMEM((wide, side), BF16),
            pltpu.VMEM((chan, rows, wide), BF16),
            pltpu.VMEM((rank_a, rows, side), BF16),
            pltpu.VMEM((out_slots, out_step, rows, side), BF16),
            pltpu.VMEM((back_slots, chan, STEP, side), BF16),
            pltpu.VMEM((chan * STEP, rank_a * STEP), BF16),
            *[pltpu.VMEM(shape, F32) for shape in grads],
            pltpu.SemaphoreType.DMA((3,)),
            pltpu.SemaphoreType.DMA((out_steps,)),
            pltpu.SemaphoreType.DMA((2, 4)),
            pltpu.SemaphoreType.DMA((out_slots,)),
            pltpu.SemaphoreType.DMA((back_slots,)),
        ],
        compiler_params=params(60),
        name="output",
    )(table_t, out_rows, back_rows, kron, g_first, g_second, g_third, g_fourth)

    return (
        output_field,
        input_grad,
        g_first.T,
        g_second.reshape(rank_a, rank_b, channels).transpose(0, 2, 1),
        g_third.transpose(0, 2, 1),
        g_fourth,
    )


def solution(mesh):
    placed = (P("chan", "grid", None), P("chan", "grid", None), P(), P(), P(), P())
    return jax.shard_map(
        local,
        mesh=mesh,
        in_specs=placed,
        out_specs=(P("chan", "grid", None), P("chan", "grid", None), P(), P(), P(), P()),
        check_vma=False,
    )
```
